32 devices in a mesh: groups: 2 (over x), tensor: 16 (over z, y, core).
Axes of the slice: x: 2, y: 2, z: 4, core: 2. Of those that a mesh axis runs over, the one named last changes fastest.
Arguments:
- queries: bfloat16 [256, 4096], P(('groups', 'tensor')), parts along dimension 0, may hold values from -6 to 6
- corpus: bfloat16 [2048, 4, 4096], P(('groups', 'tensor')), parts along dimension 0, may hold values from -6 to 6
- block_owner: int32 [48, 1], P('groups'), parts along dimension 0, may hold values from 0 to 15; in each aligned block of 24 rows (0 to 23, 24 to 47, ...) at most 3 rows name the same one
- slot_row: int32 [48], P('groups'), parts along dimension 0, may hold values from 0 to 63
- segment: int32 [48], P('groups'), parts along dimension 0, may hold values from 0 to 3, never falling along the last dimension, each value on 1 to 12 neighbouring positions
- query_weight: bfloat16 [1024, 4096], P('tensor'), may hold values from -3 to 3
- key_weight: bfloat16 [1024, 4096], P('tensor'), may hold values from -3 to 3
- value_weight: bfloat16 [1024, 4096], P('tensor'), may hold values from -0.09375 to 0.09375
- out_weight: bfloat16 [1024, 4096], P('tensor'), may hold values from -0.1875 to 0.1875
- gain_attn: float32 [4096], replicated, may hold values from 0.1 to 1.9
- gain_ffn: float32 [4096], replicated, may hold values from 0.1 to 1.9
- gate_weight: bfloat16 [2560, 4096], P('tensor'), may hold values from -0.09375 to 0.09375
- up_weight: bfloat16 [2560, 4096], P('tensor'), may hold values from -0.09375 to 0.09375
- down_weight: bfloat16 [2560, 4096], P('tensor'), may hold values from -0.125 to 0.125
Outputs:
- encoded: bfloat16 [448, 4096], P(('groups', 'tensor')), parts along dimension 0
The draws below stay inside these ranges and needn't reach their ends.
There are 2 independent parts, one for each index of `groups`. The reference program is written for one: setup_inputs(seed, part) draws one part's arguments, and reference() takes and returns one part's arrays. A program takes and returns all parts, laid end to end along the dimension named above; an argument that names none is the same for every part. Nothing has to cross between parts.
Inputs may be any that keep to these rules, and one draw needn't show every extreme that they name: `block_owner`: every owner holds some block of the pack; no owner holds more than 3 of them, and some owner holds exactly 3. `segment`: never falls along the pack; each pair has 1 to 12 blocks, one exactly 12.
All inputs are finite; a program needn't handle non-finite values.
Results may differ from the reference program's by a relative error of at most 0.008.
Values may be sent and summed in bfloat16 or wider, within the bound.
A program may use at most 64 MiB of HBM per device.

```python
import math
import jax
import jax.numpy as jnp
import numpy as np
from jax import lax

D = 4096
HDIM = 64
QLEN = 32
PAIRS = 4
BLK = 4
CAP = 3
CORP_DEV = 64
HEADS = 16
FF = 2560
NBLK = 24
MOSTB = 12
QROWS = 128
TOK = 224
CORPUS = 1024
N_TENSOR = 16


def shared_base(key):
    return jax.random.truncated_normal(jax.random.fold_in(key, 11), -4.0, 4.0, (HEADS * HDIM, D), jnp.float32) * D ** (-0.5)


def draw_query_weight(key, part):
    base_matrix = shared_base(key)
    return base_matrix.astype(jnp.bfloat16)


def draw_key_weight(key, part):
    other_matrix = jax.random.truncated_normal(jax.random.fold_in(key, 23), -4.0, 4.0, (HEADS * HDIM, D), jnp.float32) * D ** (-0.5)
    return other_matrix.astype(jnp.bfloat16)


def touch_ends(result, own_key, low, largest):
    spot = [jax.random.randint(jax.random.fold_in(own_key, axis), (), 0, length) for axis, length in enumerate(result.shape)]
    longest = result.shape.index(max(result.shape))
    next_to = spot[:longest] + [(spot[longest] + 1) % result.shape[longest]] + spot[longest + 1:]
    return result.at[tuple(spot)].set(low).at[tuple(next_to)].set(largest)


def block_scale(rng, extent, cuts, least, top_value):
    def one(position, shards_of):
        draws = jax.random.uniform(jax.random.fold_in(jax.random.fold_in(rng, 6), position), (shards_of,), jnp.float32, least / len(cuts), top_value / len(cuts))
        return jnp.repeat(jnp.exp(draws), extent[position] // shards_of).reshape((-1,) + (1,) * (len(extent) - position - 1))

    level = one(*cuts[0])
    for cut in cuts[1:]:
        level = level * one(*cut)
    return level


def length_profile(amount, total, limit, lean):
    loads = [(1 << 20) // math.isqrt(standing ** lean) + 1 for standing in range(2, amount + 1)]
    surplus, counts = total - limit - (amount - 1), [1] * (amount - 1)
    while surplus > 0:
        movable = [i for i in range(amount - 1) if counts[i] < limit]
        pool, left = sum([loads[i] for i in movable]), surplus
        for i in movable:
            extra = min(limit - counts[i], max(1, left * loads[i] // pool), surplus)
            counts[i] = counts[i] + extra
            surplus = surplus - extra
    return np.array([limit] + counts)


def ragged_sizes(stream_key, count, total, limit, skew):
    if count == 2:
        one = jax.random.randint(stream_key, (), max(1, total - limit), min(limit, total - 1) + 1)
        return jnp.stack([one, total - one])
    sizes = jnp.asarray(length_profile(count, total, limit, skew), jnp.int32)
    couples = (count - 1) // 2
    donor, sink = sizes[1:1 + 2 * couples:2], sizes[2:2 + 2 * couples:2]
    slack = jnp.minimum(donor - 1, limit - sink)
    passed = jax.random.randint(jax.random.fold_in(stream_key, 1), (couples,), 0, 1 << 20) % (slack + 1)
    sizes = sizes.at[1:1 + 2 * couples:2].set(donor - passed).at[2:2 + 2 * couples:2].set(sink + passed)
    return sizes[jax.random.permutation(jax.random.fold_in(stream_key, 2), count)]


def shared_out(rng, own, number, rows, count, top, bound, slope):
    order = jax.random.permutation(rng, count)
    heavy_load, ordinary = portions_of(count, rows * top, bound, slope, True), portions_of(count, rows * top, bound, slope, False)
    places = jnp.arange(count)

    def named(tallies, turn):
        used = int((tallies > 0).sum())
        fixed = max(1, used // 4)
        moved = fixed + (places - fixed + turn * (used - fixed)) % max(1, count - fixed)
        return jnp.zeros((count,), jnp.int32).at[order[jnp.where(places < fixed, places, moved)]].set(jnp.asarray(tallies, jnp.int32))

    tallies = jnp.where(number % 4 == 0, named(heavy_load, number // 4), named(ordinary, number - number // 4 - 1))
    mixed = jax.random.permutation(jax.random.fold_in(own, 3), count)
    giver, taker = mixed[0:count // 2 * 2:2], mixed[1:count // 2 * 2:2]
    margin = jnp.minimum(tallies[giver] - 1, bound - tallies[taker]) // 2
    margin = jnp.where((giver == order[0]) | (taker == order[0]) | (tallies[taker] == 0), 0, jnp.maximum(margin, 0))
    moved = jax.random.randint(jax.random.fold_in(own, 4), (count // 2,), 0, 1 << 20) % (margin + 1)
    tallies = tallies.at[giver].add(-moved).at[taker].add(moved)
    labels = jnp.searchsorted(jnp.cumsum(tallies), jnp.arange(rows * top), side="right").astype(jnp.int32)
    grid = labels.reshape(top, rows).T
    grid = grid[jax.random.permutation(jax.random.fold_in(own, 1), rows)]
    turn = jax.random.randint(jax.random.fold_in(own, 2), (rows, 1), 0, top)
    return jnp.take_along_axis(grid, (jnp.arange(top)[None, :] + turn) % top, axis=1)


def portions_of(amount, total, reach, slope, full):
    loads = [(1 << 20) // math.isqrt(standing ** slope) + 1 for standing in range(1, amount + 1)]
    largest = reach if full else min(reach, max(-(-total // amount), total * loads[0] // sum(loads)))
    least = 1 if total - largest >= amount - 1 else 0
    holding, surplus = [largest] + [least] * (amount - 1), total - largest - least * (amount - 1)
    while surplus > 0:
        candidates = [i for i in range(1, amount) if holding[i] < largest] or [i for i in range(1, amount) if holding[i] < reach]
        whole, left = sum([loads[i] for i in candidates]), surplus
        for i in candidates:
            more = min(reach - holding[i], max(1, left * loads[i] // whole), surplus)
            holding[i] = holding[i] + more
            surplus = surplus - more
    return np.array(holding)


def gaussian(rng, dims, spread, reach, pieces=(), held_as=jnp.bfloat16):
    level = block_scale(rng, dims, pieces, -0.22, 0.18) if pieces else 1.0
    values = jax.random.normal(rng, dims, jnp.float32) * spread * level
    return jnp.minimum(jnp.maximum(values, -reach), reach).astype(held_as)


def setup_inputs(seed: int = 0, part: int = 0) -> dict:
    streams_of = jax.random.split(jax.random.key(seed), 15)
    part_keys = jax.random.split(jax.random.fold_in(streams_of[14], part), 15)
    queries = gaussian(part_keys[0], (QROWS, D), 1.0, 6.0, ((0, 16),))
    corpus = gaussian(part_keys[1], (CORPUS, BLK, D), 1.0, 6.0, ((0, 16),))
    block_owner_keys = jax.random.split(jax.random.fold_in(part_keys[2], 1), NBLK // NBLK)
    block_owner_turns = jax.random.permutation(jax.random.fold_in(part_keys[2], 3), NBLK // NBLK)
    block_owner = jax.vmap(lambda own, number: shared_out(jax.random.fold_in(part_keys[2], 2), own, number, NBLK, N_TENSOR, 1, CAP, 2))(block_owner_keys, block_owner_turns).reshape((NBLK, 1))
    slot_row = touch_ends(jax.random.randint(part_keys[3], (NBLK,), 0, CORP_DEV), jax.random.fold_in(part_keys[3], 1), 0, CORP_DEV - 1).astype(jnp.int32)
    segment = jnp.searchsorted(jnp.cumsum(ragged_sizes(part_keys[4], PAIRS, NBLK, MOSTB, 1)), jnp.arange(NBLK), side="right").astype(jnp.int32)
    query_weight = draw_query_weight(jax.random.fold_in(streams_of[14], 71), part)
    key_weight = draw_key_weight(jax.random.fold_in(streams_of[14], 71), part)
    value_weight = gaussian(streams_of[7], (HEADS * HDIM, D), D ** -0.5, 0.09375, ((0, 16),))
    out_weight = gaussian(streams_of[8], (HEADS * HDIM, D), (HEADS * HDIM) ** -0.5, 0.1875, ((0, 16),))
    gain_attn = jnp.clip(1.0 + 0.18 * jax.random.normal(streams_of[9], (D,), jnp.float32), 0.1, 1.9)
    gain_ffn = jnp.clip(1.0 + 0.18 * jax.random.normal(streams_of[10], (D,), jnp.float32), 0.1, 1.9)
    gate_weight = gaussian(streams_of[11], (FF, D), D ** -0.5, 0.09375, ((0, 16),))
    up_weight = gaussian(streams_of[12], (FF, D), D ** -0.5, 0.09375, ((0, 16),))
    down_weight = gaussian(streams_of[13], (FF, D), FF ** -0.5, 0.125, ((0, 16),))
    return dict(queries=queries, corpus=corpus, block_owner=block_owner, slot_row=slot_row, segment=segment, query_weight=query_weight, key_weight=key_weight, value_weight=value_weight, out_weight=out_weight, gain_attn=gain_attn, gain_ffn=gain_ffn, gate_weight=gate_weight, up_weight=up_weight, down_weight=down_weight)


def normed(stream, gain):
    values = stream.astype(jnp.float32)
    mean_square = lax.optimization_barrier(jnp.mean(values * values, axis=-1, keepdims=True))
    return (values * lax.rsqrt(mean_square + 1e-06) * gain).astype(jnp.bfloat16)

def by_rows(left, weight):
    return lax.dot_general(left, weight, (((1,), (1,)), ((), ())), preferred_element_type=jnp.float32)

def reference(queries, corpus, block_owner, slot_row, segment, query_weight, key_weight, value_weight, out_weight, gain_attn, gain_ffn, gate_weight, up_weight, down_weight):
    block_index = (block_owner[:, 0] * CORP_DEV + slot_row).astype(jnp.int32)
    fetched = jnp.take(corpus, block_index, axis=0).reshape(NBLK * BLK, D)
    stream_in = jnp.concatenate([queries, fetched], axis=0)
    pair_ids = jnp.concatenate([jnp.arange(QROWS, dtype=jnp.int32) // QLEN, jnp.repeat(segment, BLK).astype(jnp.int32)])
    same_pair = pair_ids[:, None] == pair_ids[None, :]
    normal_in = normed(stream_in, gain_attn)

    def heads_of(weight):
        projected = by_rows(normal_in, weight).astype(jnp.bfloat16)
        return projected.reshape(TOK, HEADS, HDIM).transpose(1, 0, 2)
    stacked = (heads_of(query_weight), heads_of(key_weight), heads_of(value_weight))

    def one_head(head_parts):
        scores = jnp.dot(head_parts[0], head_parts[1].T, preferred_element_type=jnp.float32) * HDIM ** (-0.5)
        scores = jnp.where(same_pair, scores, -1e+30)
        row_max = lax.optimization_barrier(jnp.max(scores, axis=-1, keepdims=True))
        weights = jnp.exp(scores - row_max)
        probability = (weights / lax.optimization_barrier(jnp.sum(weights, axis=-1, keepdims=True))).astype(jnp.bfloat16)
        return jnp.dot(probability, head_parts[2], preferred_element_type=jnp.float32).astype(jnp.bfloat16)
    context = lax.map(one_head, stacked).transpose(1, 0, 2).reshape(TOK, HEADS * HDIM)
    attended = jnp.dot(context, out_weight, preferred_element_type=jnp.float32)
    stream_mid = (stream_in.astype(jnp.float32) + attended).astype(jnp.bfloat16)
    normal_mid = normed(stream_mid, gain_ffn)
    gate_value = by_rows(normal_mid, gate_weight)
    up_value = by_rows(normal_mid, up_weight)
    hidden = (jax.nn.gelu(gate_value, approximate=True) * up_value).astype(jnp.bfloat16)
    ffn_result = jnp.dot(hidden, down_weight, preferred_element_type=jnp.float32)
    return (stream_mid.astype(jnp.float32) + ffn_result).astype(jnp.bfloat16)
```

```python
import functools

import jax
import jax.numpy as jnp
from jax import lax
from jax.experimental import pallas as pl
from jax.experimental.pallas import tpu as pltpu
from jax.sharding import PartitionSpec as P

HDIM = 64
QLEN = 32
BLK = 4
CAP = 3


def normed(stream, gain):
    values = stream.astype(jnp.float32)
    mean_square = jnp.mean(values * values, axis=-1, keepdims=True)
    return (values * lax.rsqrt(mean_square + 1e-06) * gain).astype(jnp.bfloat16)


def by_rows(left, weight):
    return lax.dot_general(
        left, weight, (((1,), (1,)), ((), ())), preferred_element_type=jnp.float32
    )


def plain_body(
    queries,
    corpus,
    block_owner,
    slot_row,
    segment,
    query_weight,
    key_weight,
    value_weight,
    out_weight,
    gain_attn,
    gain_ffn,
    gate_weight,
    up_weight,
    down_weight,
):
    devices = lax.axis_size("tensor")
    my_index = lax.axis_index("tensor")
    owners = block_owner[:, 0]
    blocks_total = owners.shape[0]
    features = queries.shape[1]
    positions = jnp.arange(blocks_total, dtype=jnp.int32)
    earlier = (owners[:, None] == owners[None, :]) & (positions[:, None] < positions[None, :])
    slot_rank = jnp.sum(earlier.astype(jnp.int32), axis=0)
    slot_ids = jnp.arange(CAP, dtype=jnp.int32)
    choose_slot = (owners[None, :] == my_index) & (slot_rank[None, :] == slot_ids[:, None])
    local_rows = jnp.sum(jnp.where(choose_slot, slot_row[None, :], 0), axis=1)
    present = jnp.any(choose_slot, axis=1)
    outgoing = jnp.concatenate(
        [lax.dynamic_slice_in_dim(corpus, local_rows[k], 1, 0) for k in range(CAP)], axis=0
    )
    outgoing = jnp.where(present[:, None, None], outgoing, jnp.zeros_like(outgoing)).reshape(
        CAP, -1
    )
    location = owners * CAP + slot_rank
    query_all, arrived = (
        lax.all_gather(queries, "tensor", axis=0, tiled=True),
        lax.all_gather(outgoing, "tensor", axis=0, tiled=True),
    )
    slots = jnp.arange(arrived.shape[0], dtype=jnp.int32)
    chosen = (location[:, None] == slots[None, :]).astype(jnp.bfloat16)
    fetched = jnp.dot(chosen, arrived, preferred_element_type=jnp.float32).astype(jnp.bfloat16)
    stream_in = jnp.concatenate([query_all, fetched.reshape(-1, features)], axis=0)
    normal_rows = normed(stream_in, gain_attn)
    projected = tuple(
        (
            by_rows(normal_rows, weight).astype(jnp.bfloat16)
            for weight in (query_weight, key_weight, value_weight)
        )
    )
    tokens = stream_in.shape[0]
    heads_here = query_weight.shape[0] // HDIM
    query_rows_total = query_all.shape[0]
    pair_ids = jnp.concatenate(
        [jnp.arange(query_rows_total, dtype=jnp.int32) // QLEN, jnp.repeat(segment, BLK)]
    )
    same_pair = pair_ids[:, None] == pair_ids[None, :]
    query_heads = projected[0].reshape(tokens, heads_here, HDIM)
    key_heads = projected[1].reshape(tokens, heads_here, HDIM)
    value_heads = projected[2].reshape(tokens, heads_here, HDIM)
    scores = jnp.einsum(
        "qhd,khd->hqk", query_heads, key_heads, preferred_element_type=jnp.float32
    ) * HDIM ** (-0.5)
    scores = jnp.where(same_pair[None, :, :], scores, -1e30)
    row_max = jnp.max(scores, axis=-1, keepdims=True)
    weights = jnp.exp(scores - row_max)
    probability = (weights / jnp.sum(weights, axis=-1, keepdims=True)).astype(jnp.bfloat16)
    context = (
        jnp.einsum("hqk,khd->qhd", probability, value_heads, preferred_element_type=jnp.float32)
        .astype(jnp.bfloat16)
        .reshape(tokens, heads_here * HDIM)
    )
    rows_here = tokens // devices
    first_mine = my_index * rows_here
    attended = lax.psum(jnp.dot(context, out_weight, preferred_element_type=jnp.float32), "tensor")
    stream_mid = (stream_in.astype(jnp.float32) + attended).astype(jnp.bfloat16)
    normal_mid = normed(stream_mid, gain_ffn)
    mid_mine = lax.dynamic_slice_in_dim(stream_mid, first_mine, rows_here, 0)
    gate_value = by_rows(normal_mid, gate_weight)
    up_value = by_rows(normal_mid, up_weight)
    hidden = (jax.nn.gelu(gate_value, approximate=True) * up_value).astype(jnp.bfloat16)
    ffn_result = lax.psum_scatter(
        jnp.dot(hidden, down_weight, preferred_element_type=jnp.float32),
        "tensor",
        scatter_dimension=0,
        tiled=True,
    )
    return (mid_mine.astype(jnp.float32) + ffn_result).astype(jnp.bfloat16)


Z, Y, C = 4, 2, 2
UNIT = 16
OWN = 14
HALF = 112
P1 = 2
P2 = 2
SLABS = 5
LAYER = Y * SLABS * 8
MESH = pl.DeviceIdType.MESH


def fits(mesh):
    return mesh.shape["tensor"] == Z * Y * C


def step_count(values, step, most):
    total = jnp.zeros_like(values)
    for k in range(1, most):
        total = total + jnp.where(values >= k * step, 1, 0)
    return total


def fused_kernel(
    queries, corpus, owner, slot, segment, wq, wk, wv, wo, wg, wu, wd, gain1, gain2,
    out_ref,
    corpus_v, arrived, xsend, xin, normal, qkv_v, wqkv_v, wo_v, wg_v, wu_v, wd_v,
    pair_col, ctx_out, ctx_in, resid, mid,
    part1, ry1, s1, rfwd1, rzm1, rzf1,
    part2, ry2, s2, rfwd2, rzm2, rzf2,
    lsem, xs, xr, ag1_s, ag1_r, rs1_s, rs1_r, ag2_s, ag2_r, rs2_s, rs2_r,
):
    bf, f32, i32 = jnp.bfloat16, jnp.float32, jnp.int32
    me = lax.axis_index("tensor")
    z, y, c = me // (Y * C), (me // C) % Y, me % C
    features = gain1.shape[1]
    half = features // 2
    blocks = slot.shape[0]

    def flat(zi, yi, ci):
        return zi * (Y * C) + yi * C + ci

    ypart = flat(z, 1 - y, c)
    cpart = flat(z, y, 1 - c)
    end = (z == 0) | (z == Z - 1)
    inner = (z > 0) & (z < Z - 1)
    zmate = z + 1 - 2 * (z % 2)
    zmid = jnp.where(z < 2, 2, 1)
    zend = jnp.where(z < 2, 3, 0)
    far = (zmid, zend)
    mate = flat(zmate, y, c)
    middle = flat(zmid, y, c)

    def local(src, dst, i):
        return pltpu.make_async_copy(src, dst, lsem.at[i])

    def remote(src, dst, ssem, rsem, peer):
        return pltpu.make_async_remote_copy(
            src_ref=src, dst_ref=dst, send_sem=ssem, recv_sem=rsem,
            device_id={"tensor": peer}, device_id_type=MESH,
        )

    def ag1_view(m, zi, yi, ci):
        if m == 0:
            return arrived.at[zi, yi * SLABS + ci]
        cols = pl.ds(pl.multiple_of(ci * half, half), half)
        return arrived.at[zi, pl.ds(yi * SLABS + 2, 3), :, cols]

    get_query = local(queries, arrived.at[z, y * SLABS + c], 0)
    get_corpus = local(corpus, corpus_v, 1)
    get_query.start()
    get_corpus.start()
    qkv_loads = [
        local(w, wqkv_v.at[pl.ds(k * HDIM, HDIM)], 2 + k) for k, w in enumerate((wq, wk, wv))
    ]
    shared = [(wo, wo_v), (wg, wg_v), (wu, wu_v), (wd, wd_v)]
    own_loads = [local(w, v.at[0], 5 + k) for k, (w, v) in enumerate(shared)]
    give = [
        remote(w, v.at[1], xs.at[2 + k], xr.at[2 + k], cpart) for k, (w, v) in enumerate(shared)
    ]

    barrier = pltpu.get_barrier_semaphore()
    peers = (ypart, cpart, flat((z + 1) % Z, y, c), flat((z + 2) % Z, y, c), flat((z + 3) % Z, y, c))
    for peer in peers:
        pl.semaphore_signal(barrier, inc=1, device_id={"tensor": peer}, device_id_type=MESH)

    found = jnp.int32(0)
    spots = [jnp.int32(0)] * CAP
    for b in range(blocks):
        hit = owner[b, 0] == me
        row = slot[b]
        for k in range(CAP):
            spots[k] = jnp.where(hit & (found == k), row, spots[k])
        found = found + jnp.where(hit, 1, 0)
    pl.semaphore_wait(barrier, len(peers))

    def ag1_y(m, zi, yi):
        v, at = ag1_view(m, zi, yi, c), m * 20 + zi
        return remote(v, v, ag1_s.at[at], ag1_r.at[at], ypart)

    def ag1_c(m, zi, yi):
        v, at = ag1_view(m, zi, yi, c), m * 20 + 4 + zi * 2 + yi
        return remote(v, v, ag1_s.at[at], ag1_r.at[at], cpart)

    def ag1_c_in(m, zi, yi):
        v, at = ag1_view(m, zi, yi, 1 - c), m * 20 + 4 + zi * 2 + yi
        return remote(v, v, ag1_s.at[at], ag1_r.at[at], cpart)

    def ag1_z(m, zi, k, peer):
        v = ag1_view(m, zi, y, c)
        return remote(v, v, ag1_s.at[m * 20 + 12 + k], ag1_r.at[m * 20 + 16 + zi], peer)

    def ag1_first(m):
        ag1_z(m, z, 0, mate).start()
        ag1_z(m, z, 1, middle).start()
        ag1_y(m, z, y).start()
        ag1_c(m, z, y).start()

    get_query.wait()
    ag1_first(0)
    get_corpus.wait()
    mine = [corpus_v[spots[k]] for k in range(CAP)]
    for side in range(2):

        @pl.when(c == side)
        def _():
            here = slice(side * half, side * half + half)
            there = slice((1 - side) * half, (1 - side) * half + half)
            for k in range(CAP):
                xsend[k] = mine[k][:, there]
            swap = remote(xsend, xin, xs.at[0], xr.at[0], cpart)
            swap.start()
            for yi in range(Y):

                @pl.when(y == yi)
                def _():
                    for k in range(CAP):
                        arrived[z, yi * SLABS + 2 + k, side * BLK : side * BLK + BLK, here] = mine[k][:, here]

            swap.wait_recv()
            other = (1 - side) * BLK
            for yi in range(Y):

                @pl.when(y == yi)
                def _():
                    for k in range(CAP):
                        arrived[z, yi * SLABS + 2 + k, other : other + BLK, here] = xin[k]

    ag1_first(1)
    for load in qkv_loads + own_loads:
        load.start()
    for copy in give:
        copy.start()

    lane = lax.broadcasted_iota(i32, (8, 128), 1)
    owner_row = jnp.zeros((8, 128), i32)
    seg_row = jnp.zeros((8, 128), i32)
    for b in range(blocks):
        owner_row = jnp.where(lane == b, owner[b, 0], owner_row)
        seg_row = jnp.where(lane == b, segment[b], seg_row)
    rank_row = jnp.zeros((8, 128), i32)
    for b in range(blocks):
        rank_row = rank_row + jnp.where((owner_row == owner[b, 0]) & (lane > b), 1, 0)
    start_row = (
        (owner_row >> 2) * LAYER + ((owner_row >> 1) & 1) * (SLABS * 8) + 16
        + rank_row * 8 + (owner_row & 1) * BLK
    )
    start_row = jnp.where(lane < blocks, start_row, -1000).astype(f32)[:1]
    seg_row = seg_row.astype(f32)[:1]
    sub = lax.broadcasted_iota(i32, (128, 128), 0)
    lanes = lax.broadcasted_iota(i32, (128, 128), 1)
    start_col = jnp.sum(jnp.where(sub == lanes, start_row, 0.0), axis=1, keepdims=True)
    seg_col = jnp.sum(jnp.where(sub == lanes, seg_row, 0.0), axis=1, keepdims=True)

    def slot_parts(j):
        zj = step_count(j, LAYER, Z)
        rem = j - zj * LAYER
        within = rem - jnp.where(rem >= SLABS * 8, SLABS * 8, 0)
        return zj.astype(f32), within < 16, ((j >> 2) << 2).astype(f32)

    rows_all = Z * LAYER
    zj, is_query, begin = slot_parts(lax.broadcasted_iota(i32, (rows_all, 1), 0))
    held = jnp.max(jnp.where(begin == start_row, seg_row, -1.0), axis=1, keepdims=True)
    pair_col[...] = jnp.where(is_query, zj, held)
    zj, is_query, begin = slot_parts(lax.broadcasted_iota(i32, (1, rows_all), 1))
    held = jnp.max(jnp.where(begin == start_col, seg_col, -1.0), axis=0, keepdims=True)
    pair_row = jnp.where(is_query, zj, held)

    def chosen(first, count, side):
        i = lax.broadcasted_iota(i32, (count, 1), 0) + first
        turn = step_count(i, OWN, 8)
        row = OWN * (2 * turn + side) + i - OWN * turn
        from_query = (
            (row >> 5) * LAYER + ((row >> 4) & 1) * (SLABS * 8) + ((row >> 3) & 1) * 8 + (row & 7)
        )
        behind = row - Z * QLEN
        block = lax.broadcasted_iota(i32, (count, 128), 1) == (behind >> 2)
        start = jnp.sum(jnp.where(block, start_row, 0.0), axis=1, keepdims=True)
        src = jnp.where(behind < 0, from_query, start.astype(i32) + (behind & 3))
        at = lax.broadcasted_iota(i32, (count, rows_all), 1)
        return (at == src).astype(f32).astype(bf)

    def project(zi):
        def some(i, carry):
            rows = arrived[zi, pl.ds(2 * i, 2)].reshape(16, features)
            normal[pl.ds(pl.multiple_of(i * 16, 16), 16), :] = normed(rows, gain1[...])
            return carry

        lax.fori_loop(0, LAYER // 16, some, 0)
        qkv_v[zi] = by_rows(normal[...], wqkv_v[...]).astype(bf)

    order = (z, zmate, zmid, zend)

    def finish_layer(i):
        zi = order[i]
        for m in range(2):
            ag1_y(m, zi, 1 - y).wait_recv()
            ag1_c(m, zi, 1 - y).start()
        for m in range(2):
            for yi in range(Y):
                ag1_c_in(m, zi, yi).wait_recv()
        if i == 0:
            for load in qkv_loads:
                load.wait()
        project(zi)

    for i in range(1, Z):
        zi = order[i]
        for m in range(2):
            ag1_z(m, zi, 0, mate).wait_recv()
            if i > 1:
                pl.when(inner)(lambda: ag1_z(m, zi, 1 + i - 1, mate).start())
            ag1_y(m, zi, y).start()
            ag1_c(m, zi, y).start()
        finish_layer(i - 1)
    finish_layer(Z - 1)

    qkv = qkv_v[...].reshape(rows_all, 3 * HDIM)
    q, k, v = qkv[:, :HDIM], qkv[:, HDIM : 2 * HDIM], qkv[:, 2 * HDIM :]
    scores = by_rows(q, k) * HDIM ** (-0.5)
    scores = jnp.where(pair_col[...] == pair_row, scores, -1e30)
    weights = jnp.exp(scores - jnp.max(scores, axis=-1, keepdims=True))
    probability = (weights / jnp.sum(weights, axis=-1, keepdims=True)).astype(bf)
    context = jnp.dot(probability, v, preferred_element_type=f32).astype(bf)
    ctx_out[...] = jnp.dot(chosen(0, HALF, 1 - c), context, preferred_element_type=f32).astype(bf)
    ctx_swap = remote(ctx_out, ctx_in, xs.at[1], xr.at[1], cpart)
    ctx_swap.start()
    ctx_mine = jnp.dot(chosen(0, HALF, c), context, preferred_element_type=f32).astype(bf)
    own_loads[0].wait()
    give[0].wait_recv()
    ctx_swap.wait_recv()
    ctx = jnp.concatenate([ctx_mine, ctx_in[...]], axis=1)

    def always(zi, yi):
        return None

    def present(zi, yi):
        return (zi < Z - 1) | (yi == c)

    def compact(zi, yi):
        late = jnp.where((c == 1) & (zi == Z - 1) & (yi == 1), 1, 0)
        return jnp.minimum(zi * Y + yi - late, HALF // UNIT - 1)

    def when(cond, fn):
        if cond is None:
            fn()
        else:
            pl.when(cond)(fn)

    def both(a, b):
        return a if b is None else a & b

    class Scatter:
        def __init__(self, part, ry, s, rfwd, rzm, rzf, ss, rs, unit, has):
            self.part, self.ry, self.s, self.rfwd, self.rzm, self.rzf = part, ry, s, rfwd, rzm, rzf
            self.ss, self.rs, self.unit, self.has = ss, rs, unit, has

        def to_y(self, p, d):
            at = p * 12 + d
            return remote(
                self.part.at[p, self.unit(d, 1 - y)], self.ry.at[p, d],
                self.ss.at[at], self.rs.at[at], ypart,
            )

        def to_mate(self, p):
            at = p * 12 + 4
            return remote(self.s.at[p, zmate], self.rzm.at[p], self.ss.at[at], self.rs.at[at], mate)

        def pass_on(self, p, j):
            at = p * 12 + 5 + j
            return remote(
                self.s.at[p, far[j]], self.rfwd.at[p, j], self.ss.at[at], self.rs.at[at], mate
            )

        def across(self, p, j):
            return remote(
                self.s.at[p, far[j]], self.rzf.at[p],
                self.ss.at[p * 12 + 7 + j], self.rs.at[p * 12 + 9], flat(far[j], y, c),
            )

        def send_y(self, p, d):
            when(self.has(d, 1 - y), lambda: self.to_y(p, d).start())

        def mine_and_y(self, p, d):
            self.to_y(p, d).wait_recv()
            return self.part[p, self.unit(d, y)].astype(f32) + self.ry[p, d].astype(f32)

        def middle_steps(self, p):
            def outer(j):
                d = far[j]

                def run():
                    total = self.mine_and_y(p, d)

                    @pl.when(end)
                    def _():
                        self.s[p, d] = total.astype(bf)
                        self.pass_on(p, j).start()

                    @pl.when(inner)
                    def _():
                        self.pass_on(p, j).wait_recv()
                        self.s[p, d] = (total + self.rfwd[p, j].astype(f32)).astype(bf)
                        self.across(p, j).start()

                when(self.has(d, y), run)

            def near():
                self.s[p, zmate] = self.mine_and_y(p, zmate).astype(bf)
                self.to_mate(p).start()

            outer(1)
            outer(0)
            when(self.has(zmate, y), near)

        def own_sum(self, p):
            total = self.mine_and_y(p, z)
            self.to_mate(p).wait_recv()
            self.across(p, 0).wait_recv()
            return total + self.rzm[p].astype(f32) + self.rzf[p].astype(f32)

        def drain(self, pieces):
            for p in range(pieces):
                for d in range(Z):
                    when(self.has(d, 1 - y), lambda: self.to_y(p, d).wait_send())
                when(self.has(zmate, y), lambda: self.to_mate(p).wait_send())
                for j in range(2):
                    there = self.has(far[j], y)
                    when(both(end, there), lambda: self.pass_on(p, j).wait_send())
                    when(both(inner, there), lambda: self.across(p, j).wait_send())

    one = Scatter(part1, ry1, s1, rfwd1, rzm1, rzf1, rs1_s, rs1_r, compact, present)
    width = features // P1
    wo_all = wo_v[...].reshape(2 * HDIM, features)
    for p in range(P1):
        cols = slice(p * width, (p + 1) * width)
        product = jnp.dot(ctx, wo_all[:, cols], preferred_element_type=f32)
        part1[p] = product.astype(bf).reshape(HALF // UNIT, UNIT, width)
        for d in (zend, zmid, zmate, z):
            one.send_y(p, d)

    mine_at = compact(z, y)
    has_unit = present(z, y)
    rows_here = chosen(mine_at * UNIT, UNIT, c)
    for p in range(P1):
        for t in range(Z):
            for half_at in range(2):
                n = width // 2
                cols = slice(p * width + half_at * n, p * width + half_at * n + n)
                rows = arrived[t, :, :, cols].reshape(LAYER, n)
                took = jnp.dot(
                    rows_here[:, t * LAYER : (t + 1) * LAYER], rows, preferred_element_type=f32
                )
                spot = (p, slice(None), slice(half_at * n, half_at * n + n))
                resid[spot] = took if t == 0 else resid[spot] + took

    def ag2_y(p, zi, yi):
        v, at = mid.at[p, compact(zi, yi)], p * 12 + zi
        return remote(v, v, ag2_s.at[at], ag2_r.at[at], ypart)

    def ag2_z(p, zi, k, peer):
        v = mid.at[p, compact(zi, y)]
        return remote(v, v, ag2_s.at[p * 12 + 4 + k], ag2_r.at[p * 12 + 8 + zi], peer)

    def own_piece(p):
        @pl.when(has_unit)
        def _():
            mid[p, mine_at] = (resid[p] + one.own_sum(p)).astype(bf)
            ag2_z(p, z, 0, mate).start()
            ag2_z(p, z, 1, middle).start()
            ag2_y(p, z, y).start()

    def forward(p):
        for i in range(1, Z):
            zi = order[i]

            @pl.when(present(zi, y))
            def _():
                ag2_z(p, zi, 0, mate).wait_recv()
                if i > 1:
                    pl.when(inner)(lambda: ag2_z(p, zi, i, mate).start())
                ag2_y(p, zi, y).start()

    for p in range(P1):
        one.middle_steps(p)
        if p:
            forward(p - 1)
        own_piece(p)
    forward(P1 - 1)

    for k in (1, 2):
        own_loads[k].wait()
        give[k].wait_recv()
    hidden_units = wg_v.shape[1]
    squares = gate = up = None
    for p in range(P1):
        for zi in range(Z):
            when(present(zi, 1 - y), lambda: ag2_y(p, zi, 1 - y).wait_recv())
        cols = slice(p * width, (p + 1) * width)
        rows = mid[p].reshape(HALF, width).astype(f32)
        square = jnp.sum(rows * rows, axis=1, keepdims=True)
        scaled = (rows * gain2[:, cols]).astype(bf)
        g = by_rows(scaled, wg_v[:, :, cols].reshape(2 * hidden_units, width))
        u = by_rows(scaled, wu_v[:, :, cols].reshape(2 * hidden_units, width))
        squares, gate, up = (square, g, u) if p == 0 else (squares + square, gate + g, up + u)
    inverse = lax.rsqrt(squares * (1.0 / features) + 1e-06)
    hidden = (jax.nn.gelu(gate * inverse, approximate=True) * (up * inverse)).astype(bf)

    def spread(first, count):
        j = lax.broadcasted_iota(i32, (count, 1), 0) + first
        turn = j >> 4
        src = jnp.where((j & 15) < OWN, turn * OWN + (j & 15), -1)
        return (lax.broadcasted_iota(i32, (count, HALF), 1) == src).astype(f32).astype(bf)

    hidden = jnp.dot(spread(0, Z * Y * UNIT), hidden, preferred_element_type=f32).astype(bf)
    own_loads[3].wait()
    give[3].wait_recv()

    def plain_unit(zi, yi):
        return zi * Y + yi

    two = Scatter(part2, ry2, s2, rfwd2, rzm2, rzf2, rs2_s, rs2_r, plain_unit, always)
    width2 = features // P2
    wd_all = wd_v[...].reshape(2 * hidden_units, features)
    for p in range(P2):
        cols = slice(p * width2, (p + 1) * width2)
        product = jnp.dot(hidden, wd_all[:, cols], preferred_element_type=f32)
        part2[p] = product.astype(bf).reshape(Z * Y, UNIT, width2)
        two.send_y(p, zend)
    for d in (zmid, zmate, z):
        for p in range(P2):
            two.send_y(p, d)
    last_rows = spread((z * Y + y) * UNIT, UNIT)
    lasts = [
        jnp.dot(last_rows, mid[p].reshape(HALF, width), preferred_element_type=f32)
        for p in range(P1)
    ]
    last = jnp.concatenate(lasts, axis=1)
    for p in range(P2):
        two.middle_steps(p)
    for p in range(P2):
        cols = slice(p * width2, (p + 1) * width2)
        out_ref[:, cols] = (last[:, cols] + two.own_sum(p))[:OWN].astype(bf)

    @pl.when(c == 0)
    def _():
        remote(xsend, xin, xs.at[0], xr.at[0], cpart).wait_send()

    @pl.when(c == 1)
    def _():
        remote(xsend, xin, xs.at[0], xr.at[0], cpart).wait_send()

    ctx_swap.wait_send()
    for copy in give:
        copy.wait_send()
    for m in range(2):
        ag1_z(m, z, 0, mate).wait_send()
        ag1_z(m, z, 1, middle).wait_send()
        for zi in range(Z):
            ag1_y(m, zi, y).wait_send()
            for yi in range(Y):
                ag1_c(m, zi, yi).wait_send()
        for i in (2, 3):
            pl.when(inner)(lambda: ag1_z(m, order[i], i, mate).wait_send())
    one.drain(P1)
    two.drain(P2)
    for p in range(P1):

        @pl.when(has_unit)
        def _():
            ag2_z(p, z, 0, mate).wait_send()
            ag2_z(p, z, 1, middle).wait_send()

        for zi in range(Z):
            pl.when(present(zi, y))(lambda: ag2_y(p, zi, y).wait_send())
        for i in (2, 3):
            pl.when(inner & present(order[i], y))(
                lambda: ag2_z(p, order[i], i, mate).wait_send()
            )


def fused_body(
    queries, corpus, block_owner, slot_row, segment, query_weight, key_weight, value_weight,
    out_weight, gain_attn, gain_ffn, gate_weight, up_weight, down_weight,
):
    features = queries.shape[1]
    hidden = gate_weight.shape[0]
    bf = jnp.bfloat16
    half = features // 2
    units = HALF // UNIT

    def scatter_bufs(pieces, count):
        width = features // pieces
        return [
            pltpu.VMEM((pieces, count, UNIT, width), bf),
            pltpu.VMEM((pieces, Z, UNIT, width), bf),
            pltpu.VMEM((pieces, Z, UNIT, width), bf),
            pltpu.VMEM((pieces, 2, UNIT, width), bf),
            pltpu.VMEM((pieces, UNIT, width), bf),
            pltpu.VMEM((pieces, UNIT, width), bf),
        ]

    dma = pltpu.SemaphoreType.DMA
    any_spec = pl.BlockSpec(memory_space=pl.ANY)
    vmem_spec = pl.BlockSpec(memory_space=pltpu.VMEM)
    smem_spec = pl.BlockSpec(memory_space=pltpu.SMEM)
    return pl.pallas_call(
        fused_kernel,
        out_shape=jax.ShapeDtypeStruct((OWN, features), bf),
        in_specs=[any_spec] * 2 + [smem_spec] * 3 + [any_spec] * 7 + [vmem_spec] * 2,
        out_specs=vmem_spec,
        scratch_shapes=[
            pltpu.VMEM(corpus.shape, bf),
            pltpu.VMEM((Z, Y * SLABS, 8, features), bf),
            pltpu.VMEM((CAP, BLK, half), bf),
            pltpu.VMEM((CAP, BLK, half), bf),
            pltpu.VMEM((LAYER, features), bf),
            pltpu.VMEM((Z, LAYER, 3 * HDIM), bf),
            pltpu.VMEM((3 * HDIM, features), bf),
            pltpu.VMEM((2, HDIM, features), bf),
            pltpu.VMEM((2, hidden, features), bf),
            pltpu.VMEM((2, hidden, features), bf),
            pltpu.VMEM((2, hidden, features), bf),
            pltpu.VMEM((Z * LAYER, 1), jnp.float32),
            pltpu.VMEM((HALF, HDIM), bf),
            pltpu.VMEM((HALF, HDIM), bf),
            pltpu.VMEM((P1, UNIT, features // P1), jnp.float32),
            pltpu.VMEM((P1, units, UNIT, features // P1), bf),
        ]
        + scatter_bufs(P1, units)
        + scatter_bufs(P2, Z * Y)
        + [dma((9,)), dma((6,)), dma((6,))]
        + [dma((40,))] * 2
        + [dma((12 * P1,))] * 4
        + [dma((12 * P2,))] * 2,
        compiler_params=pltpu.CompilerParams(
            collective_id=0, has_side_effects=True, vmem_limit_bytes=56 * 2**20
        ),
    )(
        queries, corpus, block_owner, slot_row, segment, query_weight, key_weight, value_weight,
        out_weight, gate_weight, up_weight, down_weight, gain_attn[None, :], gain_ffn[None, :],
    )


def solution(mesh):
    placed = (
        P(("groups", "tensor"), None),
        P(("groups", "tensor"), None, None),
        P("groups", None),
        P("groups"),
        P("groups"),
        P("tensor", None),
        P("tensor", None),
        P("tensor", None),
        P("tensor", None),
        P(),
        P(),
        P("tensor", None),
        P("tensor", None),
        P("tensor", None),
    )
    body = fused_body if fits(mesh) else plain_body
    return jax.shard_map(
        body, mesh=mesh, in_specs=placed, out_specs=P(("groups", "tensor"), None), check_vma=False
    )
```

```python
import functools

import jax
import jax.numpy as jnp
from jax import lax
from jax.experimental import pallas as pl
from jax.experimental.pallas import tpu as pltpu
from jax.sharding import PartitionSpec as P

HDIM = 64
QLEN = 32
BLK = 4
CAP = 3


def normed(stream, gain):
    values = stream.astype(jnp.float32)
    mean_square = jnp.mean(values * values, axis=-1, keepdims=True)
    return (values * lax.rsqrt(mean_square + 1e-06) * gain).astype(jnp.bfloat16)


def by_rows(left, weight):
    return lax.dot_general(
        left, weight, (((1,), (1,)), ((), ())), preferred_element_type=jnp.float32
    )


def plain_body(
    queries,
    corpus,
    block_owner,
    slot_row,
    segment,
    query_weight,
    key_weight,
    value_weight,
    out_weight,
    gain_attn,
    gain_ffn,
    gate_weight,
    up_weight,
    down_weight,
):
    devices = lax.axis_size("tensor")
    my_index = lax.axis_index("tensor")
    owners = block_owner[:, 0]
    blocks_total = owners.shape[0]
    features = queries.shape[1]
    positions = jnp.arange(blocks_total, dtype=jnp.int32)
    earlier = (owners[:, None] == owners[None, :]) & (positions[:, None] < positions[None, :])
    slot_rank = jnp.sum(earlier.astype(jnp.int32), axis=0)
    slot_ids = jnp.arange(CAP, dtype=jnp.int32)
    choose_slot = (owners[None, :] == my_index) & (slot_rank[None, :] == slot_ids[:, None])
    local_rows = jnp.sum(jnp.where(choose_slot, slot_row[None, :], 0), axis=1)
    present = jnp.any(choose_slot, axis=1)
    outgoing = jnp.concatenate(
        [lax.dynamic_slice_in_dim(corpus, local_rows[k], 1, 0) for k in range(CAP)], axis=0
    )
    outgoing = jnp.where(present[:, None, None], outgoing, jnp.zeros_like(outgoing)).reshape(
        CAP, -1
    )
    location = owners * CAP + slot_rank
    query_all, arrived = (
        lax.all_gather(queries, "tensor", axis=0, tiled=True),
        lax.all_gather(outgoing, "tensor", axis=0, tiled=True),
    )
    slots = jnp.arange(arrived.shape[0], dtype=jnp.int32)
    chosen = (location[:, None] == slots[None, :]).astype(jnp.bfloat16)
    fetched = jnp.dot(chosen, arrived, preferred_element_type=jnp.float32).astype(jnp.bfloat16)
    stream_in = jnp.concatenate([query_all, fetched.reshape(-1, features)], axis=0)
    normal_rows = normed(stream_in, gain_attn)
    projected = tuple(
        (
            by_rows(normal_rows, weight).astype(jnp.bfloat16)
            for weight in (query_weight, key_weight, value_weight)
        )
    )
    tokens = stream_in.shape[0]
    heads_here = query_weight.shape[0] // HDIM
    query_rows_total = query_all.shape[0]
    pair_ids = jnp.concatenate(
        [jnp.arange(query_rows_total, dtype=jnp.int32) // QLEN, jnp.repeat(segment, BLK)]
    )
    same_pair = pair_ids[:, None] == pair_ids[None, :]
    query_heads = projected[0].reshape(tokens, heads_here, HDIM)
    key_heads = projected[1].reshape(tokens, heads_here, HDIM)
    value_heads = projected[2].reshape(tokens, heads_here, HDIM)
    scores = jnp.einsum(
        "qhd,khd->hqk", query_heads, key_heads, preferred_element_type=jnp.float32
    ) * HDIM ** (-0.5)
    scores = jnp.where(same_pair[None, :, :], scores, -1e30)
    row_max = jnp.max(scores, axis=-1, keepdims=True)
    weights = jnp.exp(scores - row_max)
    probability = (weights / jnp.sum(weights, axis=-1, keepdims=True)).astype(jnp.bfloat16)
    context = (
        jnp.einsum("hqk,khd->qhd", probability, value_heads, preferred_element_type=jnp.float32)
        .astype(jnp.bfloat16)
        .reshape(tokens, heads_here * HDIM)
    )
    rows_here = tokens // devices
    first_mine = my_index * rows_here
    attended = lax.psum(jnp.dot(context, out_weight, preferred_element_type=jnp.float32), "tensor")
    stream_mid = (stream_in.astype(jnp.float32) + attended).astype(jnp.bfloat16)
    normal_mid = normed(stream_mid, gain_ffn)
    mid_mine = lax.dynamic_slice_in_dim(stream_mid, first_mine, rows_here, 0)
    gate_value = by_rows(normal_mid, gate_weight)
    up_value = by_rows(normal_mid, up_weight)
    hidden = (jax.nn.gelu(gate_value, approximate=True) * up_value).astype(jnp.bfloat16)
    ffn_result = lax.psum_scatter(
        jnp.dot(hidden, down_weight, preferred_element_type=jnp.float32),
        "tensor",
        scatter_dimension=0,
        tiled=True,
    )
    return (mid_mine.astype(jnp.float32) + ffn_result).astype(jnp.bfloat16)


Z, Y, C = 4, 2, 2
UNIT = 16
OWN = 14
HALF = 112
P1 = 4
P2 = 2
SLABS = 5
LAYER = Y * SLABS * 8
MESH = pl.DeviceIdType.MESH


def fits(mesh):
    return mesh.shape["tensor"] == Z * Y * C


def step_count(values, step, most):
    total = jnp.zeros_like(values)
    for k in range(1, most):
        total = total + jnp.where(values >= k * step, 1, 0)
    return total


def fused_kernel(
    queries, corpus, owner, slot, segment, wq, wk, wv, wo, wg, wu, wd, gain1, gain2,
    out_ref,
    corpus_v, arrived, xsend, xin, normal, qkv_v, wqkv_v, wo_v, wg_v, wu_v, wd_v,
    pair_col, ctx_out, ctx_in, resid, mid,
    part1, ry1, s1, rz1,
    part2, ry2, s2, rz2,
    lsem, xs, xr, ag1_s, ag1_r, rs1_s, rs1_r, ag2_s, ag2_r, rs2_s, rs2_r,
):
    bf, f32, i32 = jnp.bfloat16, jnp.float32, jnp.int32
    me = lax.axis_index("tensor")
    z, y, c = me // (Y * C), (me // C) % Y, me % C
    features = gain1.shape[1]
    half = features // 2
    blocks = slot.shape[0]

    def flat(zi, yi, ci):
        return zi * (Y * C) + yi * C + ci

    ypart = flat(z, 1 - y, c)
    cpart = flat(z, y, 1 - c)
    end = (z == 0) | (z == Z - 1)
    inner = (z > 0) & (z < Z - 1)
    zmate = z + 1 - 2 * (z % 2)
    zmid = jnp.where(z < 2, 2, 1)
    zend = jnp.where(z < 2, 3, 0)
    far = (zmid, zend)
    mate = flat(zmate, y, c)
    middle = flat(zmid, y, c)

    def local(src, dst, i):
        return pltpu.make_async_copy(src, dst, lsem.at[i])

    def remote(src, dst, ssem, rsem, peer):
        return pltpu.make_async_remote_copy(
            src_ref=src, dst_ref=dst, send_sem=ssem, recv_sem=rsem,
            device_id={"tensor": peer}, device_id_type=MESH,
        )

    def ag1_view(m, zi, yi, ci):
        if m == 0:
            return arrived.at[zi, yi * SLABS + ci]
        cols = pl.ds(pl.multiple_of(ci * half, half), half)
        return arrived.at[zi, pl.ds(yi * SLABS + 2, 3), :, cols]

    get_query = local(queries, arrived.at[z, y * SLABS + c], 0)
    get_corpus = local(corpus, corpus_v, 1)
    get_query.start()
    get_corpus.start()
    qkv_loads = [
        local(w, wqkv_v.at[pl.ds(k * HDIM, HDIM)], 2 + k) for k, w in enumerate((wq, wk, wv))
    ]
    shared = [(wo, wo_v), (wg, wg_v), (wu, wu_v), (wd, wd_v)]
    own_loads = [local(w, v.at[0], 5 + k) for k, (w, v) in enumerate(shared)]
    give = [
        remote(w, v.at[1], xs.at[2 + k], xr.at[2 + k], cpart) for k, (w, v) in enumerate(shared)
    ]

    drains = []

    barrier = pltpu.get_barrier_semaphore()
    peers = (ypart, cpart, flat((z + 1) % Z, y, c), flat((z + 2) % Z, y, c), flat((z + 3) % Z, y, c))
    for peer in peers:
        pl.semaphore_signal(barrier, inc=1, device_id={"tensor": peer}, device_id_type=MESH)

    found = jnp.int32(0)
    spots = [jnp.int32(0)] * CAP
    for b in range(blocks):
        hit = owner[b, 0] == me
        row = slot[b]
        for k in range(CAP):
            spots[k] = jnp.where(hit & (found == k), row, spots[k])
        found = found + jnp.where(hit, 1, 0)
    pl.semaphore_wait(barrier, len(peers))

    order = (z, zmate, zmid, zend)

    def ag1_y(m, zi, yi):
        v, at = ag1_view(m, zi, yi, c), m * 20 + zi
        return remote(v, v, ag1_s.at[at], ag1_r.at[at], ypart)

    def ag1_c(m, zi, yi):
        v, at = ag1_view(m, zi, yi, c), m * 20 + 4 + zi * 2 + yi
        return remote(v, v, ag1_s.at[at], ag1_r.at[at], cpart)

    def ag1_c_in(m, zi, yi):
        v, at = ag1_view(m, zi, yi, 1 - c), m * 20 + 4 + zi * 2 + yi
        return remote(v, v, ag1_s.at[at], ag1_r.at[at], cpart)

    def ag1_z(m, zi, k, peer):
        v = ag1_view(m, zi, y, c)
        return remote(v, v, ag1_s.at[m * 20 + 12 + k], ag1_r.at[m * 20 + 16 + zi], peer)

    def ag1_first(m):
        ag1_z(m, z, 0, mate).start()
        ag1_z(m, z, 1, middle).start()
        ag1_y(m, z, y).start()
        ag1_c(m, z, y).start()

    def ag1_drain():
        for m in range(2):
            ag1_z(m, z, 0, mate).wait_send()
            ag1_z(m, z, 1, middle).wait_send()
            for zi in range(Z):
                ag1_y(m, zi, y).wait_send()
                for yi in range(Y):
                    ag1_c(m, zi, yi).wait_send()
            for i in (2, 3):
                pl.when(inner)(lambda: ag1_z(m, order[i], i, mate).wait_send())

    get_query.wait()
    ag1_first(0)
    get_corpus.wait()
    mine = [corpus_v[spots[k]] for k in range(CAP)]
    for side in range(2):

        @pl.when(c == side)
        def _():
            here = slice(side * half, side * half + half)
            there = slice((1 - side) * half, (1 - side) * half + half)
            for k in range(CAP):
                xsend[k] = mine[k][:, there]
            swap = remote(xsend, xin, xs.at[0], xr.at[0], cpart)
            swap.start()
            for yi in range(Y):

                @pl.when(y == yi)
                def _():
                    for k in range(CAP):
                        arrived[z, yi * SLABS + 2 + k, side * BLK : side * BLK + BLK, here] = mine[k][:, here]

            swap.wait_recv()
            other = (1 - side) * BLK
            for yi in range(Y):

                @pl.when(y == yi)
                def _():
                    for k in range(CAP):
                        arrived[z, yi * SLABS + 2 + k, other : other + BLK, here] = xin[k]

    ag1_first(1)
    drains.append(lambda: remote(xsend, xin, xs.at[0], xr.at[0], cpart).wait_send())
    for load in qkv_loads + own_loads:
        load.start()
    for copy in give:
        copy.start()

    drains.append(lambda: [copy.wait_send() for copy in give])
    lane = lax.broadcasted_iota(i32, (8, 128), 1)
    owner_row = jnp.zeros((8, 128), i32)
    seg_row = jnp.zeros((8, 128), i32)
    for b in range(blocks):
        owner_row = jnp.where(lane == b, owner[b, 0], owner_row)
        seg_row = jnp.where(lane == b, segment[b], seg_row)
    rank_row = jnp.zeros((8, 128), i32)
    for b in range(blocks):
        rank_row = rank_row + jnp.where((owner_row == owner[b, 0]) & (lane > b), 1, 0)
    start_row = (
        (owner_row >> 2) * LAYER + ((owner_row >> 1) & 1) * (SLABS * 8) + 16
        + rank_row * 8 + (owner_row & 1) * BLK
    )
    start_row = jnp.where(lane < blocks, start_row, -1000).astype(f32)[:1]
    seg_row = seg_row.astype(f32)[:1]
    sub = lax.broadcasted_iota(i32, (128, 128), 0)
    lanes = lax.broadcasted_iota(i32, (128, 128), 1)
    start_col = jnp.sum(jnp.where(sub == lanes, start_row, 0.0), axis=1, keepdims=True)
    seg_col = jnp.sum(jnp.where(sub == lanes, seg_row, 0.0), axis=1, keepdims=True)

    def slot_parts(j):
        zj = step_count(j, LAYER, Z)
        rem = j - zj * LAYER
        within = rem - jnp.where(rem >= SLABS * 8, SLABS * 8, 0)
        return zj.astype(f32), within < 16, ((j >> 2) << 2).astype(f32)

    rows_all = Z * LAYER
    zj, is_query, begin = slot_parts(lax.broadcasted_iota(i32, (rows_all, 1), 0))
    held = jnp.max(jnp.where(begin == start_row, seg_row, -1.0), axis=1, keepdims=True)
    pair_col[...] = jnp.where(is_query, zj, held)
    zj, is_query, begin = slot_parts(lax.broadcasted_iota(i32, (1, rows_all), 1))
    held = jnp.max(jnp.where(begin == start_col, seg_col, -1.0), axis=0, keepdims=True)
    pair_row = jnp.where(is_query, zj, held)

    def chosen(first, count, side):
        i = lax.broadcasted_iota(i32, (count, 1), 0) + first
        turn = step_count(i, OWN, 8)
        row = OWN * (2 * turn + side) + i - OWN * turn
        from_query = (
            (row >> 5) * LAYER + ((row >> 4) & 1) * (SLABS * 8) + ((row >> 3) & 1) * 8 + (row & 7)
        )
        behind = row - Z * QLEN
        block = lax.broadcasted_iota(i32, (count, 128), 1) == (behind >> 2)
        start = jnp.sum(jnp.where(block, start_row, 0.0), axis=1, keepdims=True)
        src = jnp.where(behind < 0, from_query, start.astype(i32) + (behind & 3))
        at = lax.broadcasted_iota(i32, (count, rows_all), 1)
        return (at == src).astype(f32).astype(bf)

    def project(zi):
        def some(i, carry):
            rows = arrived[zi, pl.ds(2 * i, 2)].reshape(16, features)
            normal[pl.ds(pl.multiple_of(i * 16, 16), 16), :] = normed(rows, gain1[...])
            return carry

        lax.fori_loop(0, LAYER // 16, some, 0)
        qkv_v[zi] = by_rows(normal[...], wqkv_v[...]).astype(bf)

    def finish_layer(i):
        zi = order[i]
        for m in range(2):
            ag1_y(m, zi, 1 - y).wait_recv()
            ag1_c(m, zi, 1 - y).start()
        for m in range(2):
            for yi in range(Y):
                ag1_c_in(m, zi, yi).wait_recv()
        if i == 0:
            for load in qkv_loads:
                load.wait()
        project(zi)

    for i in range(1, Z):
        zi = order[i]
        for m in range(2):
            ag1_z(m, zi, 0, mate).wait_recv()
            if i > 1:
                pl.when(inner)(lambda: ag1_z(m, zi, 1 + i - 1, mate).start())
            ag1_y(m, zi, y).start()
            ag1_c(m, zi, y).start()
        finish_layer(i - 1)
    finish_layer(Z - 1)
    drains.append(ag1_drain)
    qkv = qkv_v[...].reshape(rows_all, 3 * HDIM)
    q, k, v = qkv[:, :HDIM], qkv[:, HDIM : 2 * HDIM], qkv[:, 2 * HDIM :]
    scores = by_rows(q, k) * HDIM ** (-0.5)
    scores = jnp.where(pair_col[...] == pair_row, scores, -1e30)
    weights = jnp.exp(scores - jnp.max(scores, axis=-1, keepdims=True))
    probability = (weights / jnp.sum(weights, axis=-1, keepdims=True)).astype(bf)
    context = jnp.dot(probability, v, preferred_element_type=f32).astype(bf)
    ctx_out[...] = jnp.dot(chosen(0, HALF, 1 - c), context, preferred_element_type=f32).astype(bf)
    ctx_swap = remote(ctx_out, ctx_in, xs.at[1], xr.at[1], cpart)
    ctx_swap.start()
    drains.append(ctx_swap.wait_send)
    ctx_mine = jnp.dot(chosen(0, HALF, c), context, preferred_element_type=f32).astype(bf)
    own_loads[0].wait()
    give[0].wait_recv()
    ctx_swap.wait_recv()
    ctx = jnp.concatenate([ctx_mine, ctx_in[...]], axis=1)

    def always(zi, yi):
        return None

    def present(zi, yi):
        return (zi < Z - 1) | (yi == c)

    def compact(zi, yi):
        late = jnp.where((c == 1) & (zi == Z - 1) & (yi == 1), 1, 0)
        return jnp.minimum(zi * Y + yi - late, HALF // UNIT - 1)

    def when(cond, fn):
        if cond is None:
            fn()
        else:
            pl.when(cond)(fn)

    def both(a, b):
        return a if b is None else a & b

    class Scatter:
        def __init__(self, part, ry, s, rz, ss, rs, unit, has):
            self.part, self.ry, self.s, self.rz = part, ry, s, rz
            self.ss, self.rs, self.unit, self.has = ss, rs, unit, has

        def to_y(self, p, d):
            at = p * 12 + d
            return remote(
                self.part.at[p, self.unit(d, 1 - y)], self.ry.at[p, d],
                self.ss.at[at], self.rs.at[at], ypart,
            )

        def to_z(self, p, d, src):
            at = p * 12 + 4
            return remote(
                self.s.at[p, d], self.rz.at[p, src],
                self.ss.at[at + d], self.rs.at[at + src], flat(d, y, c),
            )

        def send_y(self, p, d):
            when(self.has(d, 1 - y), lambda: self.to_y(p, d).start())

        def mine_and_y(self, p, d):
            self.to_y(p, d).wait_recv()
            return self.part[p, self.unit(d, y)].astype(f32) + self.ry[p, d].astype(f32)

        def relay(self, p, d):
            def run():
                self.s[p, d] = self.mine_and_y(p, d).astype(bf)
                self.to_z(p, d, z).start()

            when(self.has(d, y), run)

        def own_sum(self, p):
            total = self.mine_and_y(p, z)
            for src in order[1:]:
                self.to_z(p, zmate, src).wait_recv()
                total = total + self.rz[p, src].astype(f32)
            return total

        def drain(self, pieces):
            for p in range(pieces):
                for d in range(Z):
                    when(self.has(d, 1 - y), lambda: self.to_y(p, d).wait_send())
                for d in order[1:]:
                    when(self.has(d, y), lambda: self.to_z(p, d, z).wait_send())

    one = Scatter(part1, ry1, s1, rz1, rs1_s, rs1_r, compact, present)
    width = features // P1
    wo_all = wo_v[...].reshape(2 * HDIM, features)
    for p in range(P1):
        cols = slice(p * width, (p + 1) * width)
        product = jnp.dot(ctx, wo_all[:, cols], preferred_element_type=f32)
        part1[p] = product.astype(bf).reshape(HALF // UNIT, UNIT, width)
        for d in (zend, zmid, zmate, z):
            one.send_y(p, d)

    drains.append(lambda: one.drain(P1))
    mine_at = compact(z, y)
    has_unit = present(z, y)
    rows_here = chosen(mine_at * UNIT, UNIT, c)
    for p in range(P1):
        for t in range(Z):
            for half_at in range(2):
                n = width // 2
                cols = slice(p * width + half_at * n, p * width + half_at * n + n)
                rows = arrived[t, :, :, cols].reshape(LAYER, n)
                took = jnp.dot(
                    rows_here[:, t * LAYER : (t + 1) * LAYER], rows, preferred_element_type=f32
                )
                spot = (p, slice(None), slice(half_at * n, half_at * n + n))
                resid[spot] = took if t == 0 else resid[spot] + took

    def ag2_y(p, zi, yi):
        v, at = mid.at[p, compact(zi, yi)], p * 12 + zi
        return remote(v, v, ag2_s.at[at], ag2_r.at[at], ypart)

    def ag2_z(p, zi, k, peer):
        v = mid.at[p, compact(zi, y)]
        return remote(v, v, ag2_s.at[p * 12 + 4 + k], ag2_r.at[p * 12 + 8 + zi], peer)

    def ag2_drain():
        for p in range(P1):

            @pl.when(has_unit)
            def _():
                for k in range(1, Z):
                    ag2_z(p, z, k, flat(order[k], y, c)).wait_send()

            for zi in range(Z):
                pl.when(present(zi, y))(lambda: ag2_y(p, zi, y).wait_send())

    def own_piece(p):
        @pl.when(has_unit)
        def _():
            mid[p, mine_at] = (resid[p] + one.own_sum(p)).astype(bf)
            for k in range(1, Z):
                ag2_z(p, z, k, flat(order[k], y, c)).start()
            ag2_y(p, z, y).start()

    def forward(p):
        for i in range(1, Z):
            zi = order[i]

            @pl.when(present(zi, y))
            def _():
                ag2_z(p, zi, 0, mate).wait_recv()
                ag2_y(p, zi, y).start()

    for p in range(P1):
        for d in (zend, zmid, zmate):
            one.relay(p, d)
    for p in range(P1):
        own_piece(p)
    for p in range(P1 - 1):
        forward(p)
    forward(P1 - 1)
    drains.append(ag2_drain)

    for k in (1, 2):
        own_loads[k].wait()
        give[k].wait_recv()
    hidden_units = wg_v.shape[1]
    squares = gate = up = None
    for p in range(P1):
        for zi in range(Z):
            when(present(zi, 1 - y), lambda: ag2_y(p, zi, 1 - y).wait_recv())
        cols = slice(p * width, (p + 1) * width)
        rows = mid[p].reshape(HALF, width).astype(f32)
        square = jnp.sum(rows * rows, axis=1, keepdims=True)
        scaled = (rows * gain2[:, cols]).astype(bf)
        g = by_rows(scaled, wg_v[:, :, cols].reshape(2 * hidden_units, width))
        u = by_rows(scaled, wu_v[:, :, cols].reshape(2 * hidden_units, width))
        squares, gate, up = (square, g, u) if p == 0 else (squares + square, gate + g, up + u)
    inverse = lax.rsqrt(squares * (1.0 / features) + 1e-06)
    hidden = (jax.nn.gelu(gate * inverse, approximate=True) * (up * inverse)).astype(bf)

    def spread(first, count):
        j = lax.broadcasted_iota(i32, (count, 1), 0) + first
        turn = j >> 4
        src = jnp.where((j & 15) < OWN, turn * OWN + (j & 15), -1)
        return (lax.broadcasted_iota(i32, (count, HALF), 1) == src).astype(f32).astype(bf)

    hidden = jnp.dot(spread(0, Z * Y * UNIT), hidden, preferred_element_type=f32).astype(bf)
    own_loads[3].wait()
    give[3].wait_recv()

    def plain_unit(zi, yi):
        return zi * Y + yi

    two = Scatter(part2, ry2, s2, rz2, rs2_s, rs2_r, plain_unit, always)
    drains.append(lambda: two.drain(P2))
    width2 = features // P2
    wd_all = wd_v[...].reshape(2 * hidden_units, features)
    for p in range(P2):
        cols = slice(p * width2, (p + 1) * width2)
        product = jnp.dot(hidden, wd_all[:, cols], preferred_element_type=f32)
        part2[p] = product.astype(bf).reshape(Z * Y, UNIT, width2)
        two.send_y(p, zend)
    for d in (zmid, zmate, z):
        for p in range(P2):
            two.send_y(p, d)
    last_rows = spread((z * Y + y) * UNIT, UNIT)
    lasts = [
        jnp.dot(last_rows, mid[p].reshape(HALF, width), preferred_element_type=f32)
        for p in range(P1)
    ]
    last = jnp.concatenate(lasts, axis=1)
    for d in (zend, zmid, zmate):
        for p in range(P2):
            two.relay(p, d)
    for p in range(P2):
        cols = slice(p * width2, (p + 1) * width2)
        out_ref[:, cols] = (last[:, cols] + two.own_sum(p))[:OWN].astype(bf)

    for drain in drains:
        drain()


def fused_body(
    queries, corpus, block_owner, slot_row, segment, query_weight, key_weight, value_weight,
    out_weight, gain_attn, gain_ffn, gate_weight, up_weight, down_weight,
):
    features = queries.shape[1]
    hidden = gate_weight.shape[0]
    bf = jnp.bfloat16
    half = features // 2
    units = HALF // UNIT

    def scatter_bufs(pieces, count):
        width = features // pieces
        return [
            pltpu.VMEM((pieces, count, UNIT, width), bf),
            pltpu.VMEM((pieces, Z, UNIT, width), bf),
            pltpu.VMEM((pieces, Z, UNIT, width), bf),
            pltpu.VMEM((pieces, Z, UNIT, width), bf),
        ]

    dma = pltpu.SemaphoreType.DMA
    any_spec = pl.BlockSpec(memory_space=pl.ANY)
    vmem_spec = pl.BlockSpec(memory_space=pltpu.VMEM)
    smem_spec = pl.BlockSpec(memory_space=pltpu.SMEM)
    return pl.pallas_call(
        fused_kernel,
        out_shape=jax.ShapeDtypeStruct((OWN, features), bf),
        in_specs=[any_spec] * 2 + [smem_spec] * 3 + [any_spec] * 7 + [vmem_spec] * 2,
        out_specs=vmem_spec,
        scratch_shapes=[
            pltpu.VMEM(corpus.shape, bf),
            pltpu.VMEM((Z, Y * SLABS, 8, features), bf),
            pltpu.VMEM((CAP, BLK, half), bf),
            pltpu.VMEM((CAP, BLK, half), bf),
            pltpu.VMEM((LAYER, features), bf),
            pltpu.VMEM((Z, LAYER, 3 * HDIM), bf),
            pltpu.VMEM((3 * HDIM, features), bf),
            pltpu.VMEM((2, HDIM, features), bf),
            pltpu.VMEM((2, hidden, features), bf),
            pltpu.VMEM((2, hidden, features), bf),
            pltpu.VMEM((2, hidden, features), bf),
            pltpu.VMEM((Z * LAYER, 1), jnp.float32),
            pltpu.VMEM((HALF, HDIM), bf),
            pltpu.VMEM((HALF, HDIM), bf),
            pltpu.VMEM((P1, UNIT, features // P1), jnp.float32),
            pltpu.VMEM((P1, units, UNIT, features // P1), bf),
        ]
        + scatter_bufs(P1, units)
        + scatter_bufs(P2, Z * Y)
        + [dma((9,)), dma((6,)), dma((6,))]
        + [dma((40,))] * 2
        + [dma((12 * P1,))] * 4
        + [dma((12 * P2,))] * 2,
        compiler_params=pltpu.CompilerParams(
            collective_id=0, has_side_effects=True, vmem_limit_bytes=56 * 2**20
        ),
    )(
        queries, corpus, block_owner, slot_row, segment, query_weight, key_weight, value_weight,
        out_weight, gate_weight, up_weight, down_weight, gain_attn[None, :], gain_ffn[None, :],
    )


def solution(mesh):
    placed = (
        P(("groups", "tensor"), None),
        P(("groups", "tensor"), None, None),
        P("groups", None),
        P("groups"),
        P("groups"),
        P("tensor", None),
        P("tensor", None),
        P("tensor", None),
        P("tensor", None),
        P(),
        P(),
        P("tensor", None),
        P("tensor", None),
        P("tensor", None),
    )
    body = fused_body if fits(mesh) else plain_body
    return jax.shard_map(
        body, mesh=mesh, in_specs=placed, out_specs=P(("groups", "tensor"), None), check_vma=False
    )
```

```python
import functools

import jax
import jax.numpy as jnp
from jax import lax
from jax.experimental import pallas as pl
from jax.experimental.pallas import tpu as pltpu
from jax.sharding import PartitionSpec as P

HDIM = 64
QLEN = 32
BLK = 4
CAP = 3


def normed(stream, gain):
    values = stream.astype(jnp.float32)
    mean_square = jnp.mean(values * values, axis=-1, keepdims=True)
    return (values * lax.rsqrt(mean_square + 1e-06) * gain).astype(jnp.bfloat16)


def by_rows(left, weight):
    return lax.dot_general(
        left, weight, (((1,), (1,)), ((), ())), preferred_element_type=jnp.float32
    )


def plain_body(
    queries,
    corpus,
    block_owner,
    slot_row,
    segment,
    query_weight,
    key_weight,
    value_weight,
    out_weight,
    gain_attn,
    gain_ffn,
    gate_weight,
    up_weight,
    down_weight,
):
    devices = lax.axis_size("tensor")
    my_index = lax.axis_index("tensor")
    owners = block_owner[:, 0]
    blocks_total = owners.shape[0]
    features = queries.shape[1]
    positions = jnp.arange(blocks_total, dtype=jnp.int32)
    earlier = (owners[:, None] == owners[None, :]) & (positions[:, None] < positions[None, :])
    slot_rank = jnp.sum(earlier.astype(jnp.int32), axis=0)
    slot_ids = jnp.arange(CAP, dtype=jnp.int32)
    choose_slot = (owners[None, :] == my_index) & (slot_rank[None, :] == slot_ids[:, None])
    local_rows = jnp.sum(jnp.where(choose_slot, slot_row[None, :], 0), axis=1)
    present = jnp.any(choose_slot, axis=1)
    outgoing = jnp.concatenate(
        [lax.dynamic_slice_in_dim(corpus, local_rows[k], 1, 0) for k in range(CAP)], axis=0
    )
    outgoing = jnp.where(present[:, None, None], outgoing, jnp.zeros_like(outgoing)).reshape(
        CAP, -1
    )
    location = owners * CAP + slot_rank
    query_all, arrived = (
        lax.all_gather(queries, "tensor", axis=0, tiled=True),
        lax.all_gather(outgoing, "tensor", axis=0, tiled=True),
    )
    slots = jnp.arange(arrived.shape[0], dtype=jnp.int32)
    chosen = (location[:, None] == slots[None, :]).astype(jnp.bfloat16)
    fetched = jnp.dot(chosen, arrived, preferred_element_type=jnp.float32).astype(jnp.bfloat16)
    stream_in = jnp.concatenate([query_all, fetched.reshape(-1, features)], axis=0)
    normal_rows = normed(stream_in, gain_attn)
    projected = tuple(
        (
            by_rows(normal_rows, weight).astype(jnp.bfloat16)
            for weight in (query_weight, key_weight, value_weight)
        )
    )
    tokens = stream_in.shape[0]
    heads_here = query_weight.shape[0] // HDIM
    query_rows_total = query_all.shape[0]
    pair_ids = jnp.concatenate(
        [jnp.arange(query_rows_total, dtype=jnp.int32) // QLEN, jnp.repeat(segment, BLK)]
    )
    same_pair = pair_ids[:, None] == pair_ids[None, :]
    query_heads = projected[0].reshape(tokens, heads_here, HDIM)
    key_heads = projected[1].reshape(tokens, heads_here, HDIM)
    value_heads = projected[2].reshape(tokens, heads_here, HDIM)
    scores = jnp.einsum(
        "qhd,khd->hqk", query_heads, key_heads, preferred_element_type=jnp.float32
    ) * HDIM ** (-0.5)
    scores = jnp.where(same_pair[None, :, :], scores, -1e30)
    row_max = jnp.max(scores, axis=-1, keepdims=True)
    weights = jnp.exp(scores - row_max)
    probability = (weights / jnp.sum(weights, axis=-1, keepdims=True)).astype(jnp.bfloat16)
    context = (
        jnp.einsum("hqk,khd->qhd", probability, value_heads, preferred_element_type=jnp.float32)
        .astype(jnp.bfloat16)
        .reshape(tokens, heads_here * HDIM)
    )
    rows_here = tokens // devices
    first_mine = my_index * rows_here
    attended = lax.psum(jnp.dot(context, out_weight, preferred_element_type=jnp.float32), "tensor")
    stream_mid = (stream_in.astype(jnp.float32) + attended).astype(jnp.bfloat16)
    normal_mid = normed(stream_mid, gain_ffn)
    mid_mine = lax.dynamic_slice_in_dim(stream_mid, first_mine, rows_here, 0)
    gate_value = by_rows(normal_mid, gate_weight)
    up_value = by_rows(normal_mid, up_weight)
    hidden = (jax.nn.gelu(gate_value, approximate=True) * up_value).astype(jnp.bfloat16)
    ffn_result = lax.psum_scatter(
        jnp.dot(hidden, down_weight, preferred_element_type=jnp.float32),
        "tensor",
        scatter_dimension=0,
        tiled=True,
    )
    return (mid_mine.astype(jnp.float32) + ffn_result).astype(jnp.bfloat16)


Z, Y, C = 4, 2, 2
UNIT = 16
OWN = 14
HALF = 112
P1 = 4
P2 = 2
LAG1 = 2
LAG2 = 5
SLABS = 5
LAYER = Y * SLABS * 8
MESH = pl.DeviceIdType.MESH


def fits(mesh):
    return mesh.shape["tensor"] == Z * Y * C


def step_count(values, step, most):
    total = jnp.zeros_like(values)
    for k in range(1, most):
        total = total + jnp.where(values >= k * step, 1, 0)
    return total


def fused_kernel(
    queries, corpus, owner_h, slot_h, segment_h, wq, wk, wv, wo, wg, wu, wd, gain1_h, gain2_h,
    out_ref,
    owner, slot, segment, gain1, gain2, corpus_v, arrived, xsend, xin, normal, qkv_v, wqkv_v, wo_v, wg_v, wu_v, wd_v,
    pair_col, ctx_out, ctx_in, resid, mid,
    part1, ry1, s1, rz1,
    part2, ry2, s2, rz2,
    lsem, xs, xr, ag1_s, ag1_r, rs1_s, rs1_r, ag2_s, ag2_r, rs2_s, rs2_r,
):
    bf, f32, i32 = jnp.bfloat16, jnp.float32, jnp.int32
    me = lax.axis_index("tensor")
    z, y, c = me // (Y * C), (me // C) % Y, me % C
    features = gain1.shape[1]
    half = features // 2
    blocks = slot.shape[0]

    def flat(zi, yi, ci):
        return zi * (Y * C) + yi * C + ci

    ypart = flat(z, 1 - y, c)
    cpart = flat(z, y, 1 - c)
    end = (z == 0) | (z == Z - 1)
    inner = (z > 0) & (z < Z - 1)
    zmate = z + 1 - 2 * (z % 2)
    zmid = jnp.where(z < 2, 2, 1)
    zend = jnp.where(z < 2, 3, 0)
    far = (zmid, zend)
    mate = flat(zmate, y, c)
    middle = flat(zmid, y, c)

    def local(src, dst, i):
        return pltpu.make_async_copy(src, dst, lsem.at[i])

    def remote(src, dst, ssem, rsem, peer):
        return pltpu.make_async_remote_copy(
            src_ref=src, dst_ref=dst, send_sem=ssem, recv_sem=rsem,
            device_id={"tensor": peer}, device_id_type=MESH,
        )

    def ag1_view(m, zi, yi, ci):
        if m == 0:
            return arrived.at[zi, yi * SLABS + ci]
        cols = pl.ds(pl.multiple_of(ci * half, half), half)
        return arrived.at[zi, pl.ds(yi * SLABS + 2, 3), :, cols]

    barrier = pltpu.get_barrier_semaphore()
    peers = (ypart, cpart, flat((z + 1) % Z, y, c), flat((z + 2) % Z, y, c), flat((z + 3) % Z, y, c))
    for peer in peers:
        pl.semaphore_signal(barrier, inc=1, device_id={"tensor": peer}, device_id_type=MESH)

    tables = [
        local(src, dst, 9 + k)
        for k, (src, dst) in enumerate(((owner_h, owner), (slot_h, slot), (segment_h, segment)))
    ]
    gains = [local(gain1_h, gain1, 12), local(gain2_h, gain2, 13)]
    for copy in tables:
        copy.start()
    get_query = local(queries, arrived.at[z, y * SLABS + c], 0)
    get_corpus = local(corpus, corpus_v, 1)
    get_query.start()
    get_corpus.start()
    for copy in gains:
        copy.start()
    qkv_loads = [
        local(w, wqkv_v.at[pl.ds(k * HDIM, HDIM)], 2 + k) for k, w in enumerate((wq, wk, wv))
    ]
    shared = [(wo, wo_v), (wg, wg_v), (wu, wu_v), (wd, wd_v)]
    own_loads = [local(w, v.at[0], 5 + k) for k, (w, v) in enumerate(shared)]
    give = [
        remote(w, v.at[1], xs.at[2 + k], xr.at[2 + k], cpart) for k, (w, v) in enumerate(shared)
    ]

    drains = []

    for copy in tables:
        copy.wait()
    found = jnp.int32(0)
    spots = [jnp.int32(0)] * CAP
    for b in range(blocks):
        hit = owner[0, b] == me
        row = slot[b]
        for k in range(CAP):
            spots[k] = jnp.where(hit & (found == k), row, spots[k])
        found = found + jnp.where(hit, 1, 0)
    pl.semaphore_wait(barrier, len(peers))

    order = (z, zmate, zmid, zend)

    def ag1_y(m, zi, yi):
        v, at = ag1_view(m, zi, yi, c), m * 20 + zi
        return remote(v, v, ag1_s.at[at], ag1_r.at[at], ypart)

    def ag1_c(m, zi, yi):
        v, at = ag1_view(m, zi, yi, c), m * 20 + 4 + zi * 2 + yi
        return remote(v, v, ag1_s.at[at], ag1_r.at[at], cpart)

    def ag1_c_in(m, zi, yi):
        v, at = ag1_view(m, zi, yi, 1 - c), m * 20 + 4 + zi * 2 + yi
        return remote(v, v, ag1_s.at[at], ag1_r.at[at], cpart)

    def ag1_z(m, zi, k, peer):
        v = ag1_view(m, zi, y, c)
        return remote(v, v, ag1_s.at[m * 20 + 12 + k], ag1_r.at[m * 20 + 16 + zi], peer)

    def ag1_first(m):
        ag1_z(m, z, 0, mate).start()
        ag1_z(m, z, 1, middle).start()
        ag1_y(m, z, y).start()
        ag1_c(m, z, y).start()

    def ag1_drain():
        for m in range(2):
            ag1_z(m, z, 0, mate).wait_send()
            ag1_z(m, z, 1, middle).wait_send()
            for zi in range(Z):
                ag1_y(m, zi, y).wait_send()
                for yi in range(Y):
                    ag1_c(m, zi, yi).wait_send()
            for i in (2, 3):
                pl.when(inner)(lambda: ag1_z(m, order[i], i, mate).wait_send())

    get_query.wait()
    ag1_first(0)
    get_corpus.wait()
    mine = [corpus_v[spots[k]] for k in range(CAP)]
    for side in range(2):

        @pl.when(c == side)
        def _():
            here = slice(side * half, side * half + half)
            there = slice((1 - side) * half, (1 - side) * half + half)
            for k in range(CAP):
                xsend[k] = mine[k][:, there]
            swap = remote(xsend, xin, xs.at[0], xr.at[0], cpart)
            swap.start()
            for yi in range(Y):

                @pl.when(y == yi)
                def _():
                    for k in range(CAP):
                        arrived[z, yi * SLABS + 2 + k, side * BLK : side * BLK + BLK, here] = mine[k][:, here]

            swap.wait_recv()
            other = (1 - side) * BLK
            for yi in range(Y):

                @pl.when(y == yi)
                def _():
                    for k in range(CAP):
                        arrived[z, yi * SLABS + 2 + k, other : other + BLK, here] = xin[k]

    ag1_first(1)
    drains.append(lambda: remote(xsend, xin, xs.at[0], xr.at[0], cpart).wait_send())
    for load in qkv_loads + own_loads:
        load.start()
    for copy in give:
        copy.start()

    drains.append(lambda: [copy.wait_send() for copy in give])
    lane = lax.broadcasted_iota(i32, (8, 128), 1)
    owner_row = jnp.zeros((8, 128), i32)
    seg_row = jnp.zeros((8, 128), i32)
    for b in range(blocks):
        owner_row = jnp.where(lane == b, owner[0, b], owner_row)
        seg_row = jnp.where(lane == b, segment[b], seg_row)
    rank_row = jnp.zeros((8, 128), i32)
    for b in range(blocks):
        rank_row = rank_row + jnp.where((owner_row == owner[0, b]) & (lane > b), 1, 0)
    start_row = (
        (owner_row >> 2) * LAYER + ((owner_row >> 1) & 1) * (SLABS * 8) + 16
        + rank_row * 8 + (owner_row & 1) * BLK
    )
    start_row = jnp.where(lane < blocks, start_row, -1000).astype(f32)[:1]
    seg_row = seg_row.astype(f32)[:1]
    sub = lax.broadcasted_iota(i32, (128, 128), 0)
    lanes = lax.broadcasted_iota(i32, (128, 128), 1)
    start_col = jnp.sum(jnp.where(sub == lanes, start_row, 0.0), axis=1, keepdims=True)
    seg_col = jnp.sum(jnp.where(sub == lanes, seg_row, 0.0), axis=1, keepdims=True)

    def slot_parts(j):
        zj = step_count(j, LAYER, Z)
        rem = j - zj * LAYER
        within = rem - jnp.where(rem >= SLABS * 8, SLABS * 8, 0)
        return zj.astype(f32), within < 16, ((j >> 2) << 2).astype(f32)

    rows_all = Z * LAYER
    zj, is_query, begin = slot_parts(lax.broadcasted_iota(i32, (rows_all, 1), 0))
    held = jnp.max(jnp.where(begin == start_row, seg_row, -1.0), axis=1, keepdims=True)
    pair_col[...] = jnp.where(is_query, zj, held)
    zj, is_query, begin = slot_parts(lax.broadcasted_iota(i32, (1, rows_all), 1))
    held = jnp.max(jnp.where(begin == start_col, seg_col, -1.0), axis=0, keepdims=True)
    pair_row = jnp.where(is_query, zj, held)

    def chosen(first, count, side):
        i = lax.broadcasted_iota(i32, (count, 1), 0) + first
        turn = step_count(i, OWN, 8)
        row = OWN * (2 * turn + side) + i - OWN * turn
        from_query = (
            (row >> 5) * LAYER + ((row >> 4) & 1) * (SLABS * 8) + ((row >> 3) & 1) * 8 + (row & 7)
        )
        behind = row - Z * QLEN
        block = lax.broadcasted_iota(i32, (count, 128), 1) == (behind >> 2)
        start = jnp.sum(jnp.where(block, start_row, 0.0), axis=1, keepdims=True)
        src = jnp.where(behind < 0, from_query, start.astype(i32) + (behind & 3))
        at = lax.broadcasted_iota(i32, (count, rows_all), 1)
        return (at == src).astype(f32).astype(bf)

    def project(zi):
        def some(i, carry):
            rows = arrived[zi, pl.ds(2 * i, 2)].reshape(16, features)
            normal[pl.ds(pl.multiple_of(i * 16, 16), 16), :] = normed(rows, gain1[...])
            return carry

        lax.fori_loop(0, LAYER // 16, some, 0)
        qkv_v[zi] = by_rows(normal[...], wqkv_v[...]).astype(bf)

    def from_z(i):
        zi = order[i]
        for m in range(2):
            ag1_z(m, zi, 0, mate).wait_recv()
            if i > 1:
                pl.when(inner)(lambda: ag1_z(m, zi, i, mate).start())
            ag1_y(m, zi, y).start()
            ag1_c(m, zi, y).start()

    def from_y(i):
        zi = order[i]
        for m in range(2):
            ag1_y(m, zi, 1 - y).wait_recv()
            ag1_c(m, zi, 1 - y).start()

    def finish_layer(i):
        zi = order[i]
        for m in range(2):
            for yi in range(Y):
                ag1_c_in(m, zi, yi).wait_recv()
        if i == 0:
            for load in qkv_loads + gains:
                load.wait()
        project(zi)

    from_z(1)
    from_y(0)
    from_z(2)
    finish_layer(0)
    from_z(3)
    from_y(1)
    finish_layer(1)
    from_y(2)
    finish_layer(2)
    from_y(3)
    finish_layer(3)
    drains.append(ag1_drain)
    qkv = qkv_v[...].reshape(rows_all, 3 * HDIM)
    q, k, v = qkv[:, :HDIM], qkv[:, HDIM : 2 * HDIM], qkv[:, 2 * HDIM :]
    scores = by_rows(q, k) * HDIM ** (-0.5)
    scores = jnp.where(pair_col[...] == pair_row, scores, -1e30)
    weights = jnp.exp(scores - jnp.max(scores, axis=-1, keepdims=True))
    probability = (weights / jnp.sum(weights, axis=-1, keepdims=True)).astype(bf)
    context = jnp.dot(probability, v, preferred_element_type=f32).astype(bf)
    ctx_out[...] = jnp.dot(chosen(0, HALF, 1 - c), context, preferred_element_type=f32).astype(bf)
    ctx_swap = remote(ctx_out, ctx_in, xs.at[1], xr.at[1], cpart)
    ctx_swap.start()
    drains.append(ctx_swap.wait_send)
    ctx_mine = jnp.dot(chosen(0, HALF, c), context, preferred_element_type=f32).astype(bf)
    own_loads[0].wait()
    give[0].wait_recv()
    ctx_swap.wait_recv()
    ctx = jnp.concatenate([ctx_mine, ctx_in[...]], axis=1)

    def always(zi, yi):
        return None

    def present(zi, yi):
        return (zi < Z - 1) | (yi == c)

    def compact(zi, yi):
        late = jnp.where((c == 1) & (zi == Z - 1) & (yi == 1), 1, 0)
        return jnp.minimum(zi * Y + yi - late, HALF // UNIT - 1)

    def when(cond, fn):
        if cond is None:
            fn()
        else:
            pl.when(cond)(fn)

    def both(a, b):
        return a if b is None else a & b

    class Scatter:
        def __init__(self, part, ry, s, rz, ss, rs, unit, has):
            self.part, self.ry, self.s, self.rz = part, ry, s, rz
            self.ss, self.rs, self.unit, self.has = ss, rs, unit, has

        def to_y(self, p, d):
            at = p * 12 + d
            return remote(
                self.part.at[p, self.unit(d, 1 - y)], self.ry.at[p, d],
                self.ss.at[at], self.rs.at[at], ypart,
            )

        def to_z(self, p, d, src):
            at = p * 12 + 4
            return remote(
                self.s.at[p, d], self.rz.at[p, src],
                self.ss.at[at + d], self.rs.at[at + src], flat(d, y, c),
            )

        def send_y(self, p, d):
            when(self.has(d, 1 - y), lambda: self.to_y(p, d).start())

        def mine_and_y(self, p, d):
            self.to_y(p, d).wait_recv()
            return self.part[p, self.unit(d, y)].astype(f32) + self.ry[p, d].astype(f32)

        def relay(self, p, d):
            def run():
                self.s[p, d] = self.mine_and_y(p, d).astype(bf)
                self.to_z(p, d, z).start()

            when(self.has(d, y), run)

        def own_sum(self, p):
            total = self.mine_and_y(p, z)
            for src in order[1:]:
                self.to_z(p, zmate, src).wait_recv()
                total = total + self.rz[p, src].astype(f32)
            return total

        def drain(self, pieces):
            for p in range(pieces):
                for d in range(Z):
                    when(self.has(d, 1 - y), lambda: self.to_y(p, d).wait_send())
                for d in order[1:]:
                    when(self.has(d, y), lambda: self.to_z(p, d, z).wait_send())

    one = Scatter(part1, ry1, s1, rz1, rs1_s, rs1_r, compact, present)
    width = features // P1
    wo_all = wo_v[...].reshape(2 * HDIM, features)
    for p in range(P1):
        cols = slice(p * width, (p + 1) * width)
        product = jnp.dot(ctx, wo_all[:, cols], preferred_element_type=f32)
        part1[p] = product.astype(bf).reshape(HALF // UNIT, UNIT, width)
        for d in (zend, zmid, zmate, z):
            one.send_y(p, d)

    drains.append(lambda: one.drain(P1))
    mine_at = compact(z, y)
    has_unit = present(z, y)
    rows_here = chosen(mine_at * UNIT, UNIT, c)
    for p in range(P1):
        for t in range(Z):
            for half_at in range(2):
                n = width // 2
                cols = slice(p * width + half_at * n, p * width + half_at * n + n)
                rows = arrived[t, :, :, cols].reshape(LAYER, n)
                took = jnp.dot(
                    rows_here[:, t * LAYER : (t + 1) * LAYER], rows, preferred_element_type=f32
                )
                spot = (p, slice(None), slice(half_at * n, half_at * n + n))
                resid[spot] = took if t == 0 else resid[spot] + took

    def ag2_y(p, zi, yi):
        v, at = mid.at[p, compact(zi, yi)], p * 12 + zi
        return remote(v, v, ag2_s.at[at], ag2_r.at[at], ypart)

    def ag2_z(p, zi, k, peer):
        v = mid.at[p, compact(zi, y)]
        return remote(v, v, ag2_s.at[p * 12 + 4 + k], ag2_r.at[p * 12 + 8 + zi], peer)

    def ag2_drain():
        for p in range(P1):

            @pl.when(has_unit)
            def _():
                for k in range(1, Z):
                    ag2_z(p, z, k, flat(order[k], y, c)).wait_send()

            for zi in range(Z):
                pl.when(present(zi, y))(lambda: ag2_y(p, zi, y).wait_send())

    def own_piece(p):
        @pl.when(has_unit)
        def _():
            mid[p, mine_at] = (resid[p] + one.own_sum(p)).astype(bf)
            for k in range(1, Z):
                ag2_z(p, z, k, flat(order[k], y, c)).start()
            ag2_y(p, z, y).start()

    def forward(p):
        for i in range(1, Z):
            zi = order[i]

            @pl.when(present(zi, y))
            def _():
                ag2_z(p, zi, 0, mate).wait_recv()
                ag2_y(p, zi, y).start()

    for step in range(P1 + LAG2):
        if step < P1:
            for d in (zend, zmid, zmate):
                one.relay(step, d)
        if 0 <= step - LAG1 < P1:
            own_piece(step - LAG1)
        if 0 <= step - LAG2 < P1:
            forward(step - LAG2)
    drains.append(ag2_drain)

    for k in (1, 2):
        own_loads[k].wait()
        give[k].wait_recv()
    hidden_units = wg_v.shape[1]
    squares = gate = up = None
    for p in range(P1):
        for zi in range(Z):
            when(present(zi, 1 - y), lambda: ag2_y(p, zi, 1 - y).wait_recv())
        cols = slice(p * width, (p + 1) * width)
        rows = mid[p].reshape(HALF, width).astype(f32)
        square = jnp.sum(rows * rows, axis=1, keepdims=True)
        scaled = (rows * gain2[:, cols]).astype(bf)
        g = by_rows(scaled, wg_v[:, :, cols].reshape(2 * hidden_units, width))
        u = by_rows(scaled, wu_v[:, :, cols].reshape(2 * hidden_units, width))
        squares, gate, up = (square, g, u) if p == 0 else (squares + square, gate + g, up + u)
    inverse = lax.rsqrt(squares * (1.0 / features) + 1e-06)
    hidden = (jax.nn.gelu(gate * inverse, approximate=True) * (up * inverse)).astype(bf)

    def spread(first, count):
        j = lax.broadcasted_iota(i32, (count, 1), 0) + first
        turn = j >> 4
        src = jnp.where((j & 15) < OWN, turn * OWN + (j & 15), -1)
        return (lax.broadcasted_iota(i32, (count, HALF), 1) == src).astype(f32).astype(bf)

    hidden = jnp.dot(spread(0, Z * Y * UNIT), hidden, preferred_element_type=f32).astype(bf)
    own_loads[3].wait()
    give[3].wait_recv()

    def plain_unit(zi, yi):
        return zi * Y + yi

    two = Scatter(part2, ry2, s2, rz2, rs2_s, rs2_r, plain_unit, always)
    drains.append(lambda: two.drain(P2))
    width2 = features // P2
    wd_all = wd_v[...].reshape(2 * hidden_units, features)
    for p in range(P2):
        cols = slice(p * width2, (p + 1) * width2)
        product = jnp.dot(hidden, wd_all[:, cols], preferred_element_type=f32)
        part2[p] = product.astype(bf).reshape(Z * Y, UNIT, width2)
        two.send_y(p, zend)
    for d in (zmid, zmate, z):
        for p in range(P2):
            two.send_y(p, d)
    last_rows = spread((z * Y + y) * UNIT, UNIT)
    lasts = [
        jnp.dot(last_rows, mid[p].reshape(HALF, width), preferred_element_type=f32)
        for p in range(P1)
    ]
    last = jnp.concatenate(lasts, axis=1)
    for d in (zend, zmid, zmate):
        for p in range(P2):
            two.relay(p, d)
    for p in range(P2):
        cols = slice(p * width2, (p + 1) * width2)
        out_ref[:, cols] = (last[:, cols] + two.own_sum(p))[:OWN].astype(bf)

    for drain in drains:
        drain()


def fused_body(
    queries, corpus, block_owner, slot_row, segment, query_weight, key_weight, value_weight,
    out_weight, gain_attn, gain_ffn, gate_weight, up_weight, down_weight,
):
    features = queries.shape[1]
    hidden = gate_weight.shape[0]
    bf = jnp.bfloat16
    half = features // 2
    units = HALF // UNIT

    def scatter_bufs(pieces, count):
        width = features // pieces
        return [
            pltpu.VMEM((pieces, count, UNIT, width), bf),
            pltpu.VMEM((pieces, Z, UNIT, width), bf),
            pltpu.VMEM((pieces, Z, UNIT, width), bf),
            pltpu.VMEM((pieces, Z, UNIT, width), bf),
        ]

    dma = pltpu.SemaphoreType.DMA
    any_spec = pl.BlockSpec(memory_space=pl.ANY)
    vmem_spec = pl.BlockSpec(memory_space=pltpu.VMEM)
    return pl.pallas_call(
        fused_kernel,
        out_shape=jax.ShapeDtypeStruct((OWN, features), bf),
        in_specs=[any_spec] * 14,
        out_specs=vmem_spec,
        scratch_shapes=[
            pltpu.SMEM((1, block_owner.shape[0]), jnp.int32),
            pltpu.SMEM(slot_row.shape, jnp.int32),
            pltpu.SMEM(segment.shape, jnp.int32),
            pltpu.VMEM((1, features), jnp.float32),
            pltpu.VMEM((1, features), jnp.float32),
            pltpu.VMEM(corpus.shape, bf),
            pltpu.VMEM((Z, Y * SLABS, 8, features), bf),
            pltpu.VMEM((CAP, BLK, half), bf),
            pltpu.VMEM((CAP, BLK, half), bf),
            pltpu.VMEM((LAYER, features), bf),
            pltpu.VMEM((Z, LAYER, 3 * HDIM), bf),
            pltpu.VMEM((3 * HDIM, features), bf),
            pltpu.VMEM((2, HDIM, features), bf),
            pltpu.VMEM((2, hidden, features), bf),
            pltpu.VMEM((2, hidden, features), bf),
            pltpu.VMEM((2, hidden, features), bf),
            pltpu.VMEM((Z * LAYER, 1), jnp.float32),
            pltpu.VMEM((HALF, HDIM), bf),
            pltpu.VMEM((HALF, HDIM), bf),
            pltpu.VMEM((P1, UNIT, features // P1), jnp.float32),
            pltpu.VMEM((P1, units, UNIT, features // P1), bf),
        ]
        + scatter_bufs(P1, units)
        + scatter_bufs(P2, Z * Y)
        + [dma((14,)), dma((6,)), dma((6,))]
        + [dma((40,))] * 2
        + [dma((12 * P1,))] * 4
        + [dma((12 * P2,))] * 2,
        compiler_params=pltpu.CompilerParams(
            collective_id=0, has_side_effects=True, vmem_limit_bytes=56 * 2**20
        ),
    )(
        queries, corpus, block_owner.reshape(1, -1), slot_row, segment, query_weight, key_weight,
        value_weight, out_weight, gate_weight, up_weight, down_weight, gain_attn[None, :], gain_ffn[None, :],
    )


def solution(mesh):
    placed = (
        P(("groups", "tensor"), None),
        P(("groups", "tensor"), None, None),
        P("groups", None),
        P("groups"),
        P("groups"),
        P("tensor", None),
        P("tensor", None),
        P("tensor", None),
        P("tensor", None),
        P(),
        P(),
        P("tensor", None),
        P("tensor", None),
        P("tensor", None),
    )
    body = fused_body if fits(mesh) else plain_body
    return jax.shard_map(
        body, mesh=mesh, in_specs=placed, out_specs=P(("groups", "tensor"), None), check_vma=False
    )
```

```python
import functools

import jax
import jax.numpy as jnp
from jax import lax
from jax.experimental import pallas as pl
from jax.experimental.pallas import tpu as pltpu
from jax.sharding import PartitionSpec as P

HDIM = 64
QLEN = 32
BLK = 4
CAP = 3


def normed(stream, gain):
    values = stream.astype(jnp.float32)
    mean_square = jnp.mean(values * values, axis=-1, keepdims=True)
    return (values * lax.rsqrt(mean_square + 1e-06) * gain).astype(jnp.bfloat16)


def by_rows(left, weight):
    return lax.dot_general(
        left, weight, (((1,), (1,)), ((), ())), preferred_element_type=jnp.float32
    )


def plain_body(
    queries,
    corpus,
    block_owner,
    slot_row,
    segment,
    query_weight,
    key_weight,
    value_weight,
    out_weight,
    gain_attn,
    gain_ffn,
    gate_weight,
    up_weight,
    down_weight,
):
    devices = lax.axis_size("tensor")
    my_index = lax.axis_index("tensor")
    owners = block_owner[:, 0]
    blocks_total = owners.shape[0]
    features = queries.shape[1]
    positions = jnp.arange(blocks_total, dtype=jnp.int32)
    earlier = (owners[:, None] == owners[None, :]) & (positions[:, None] < positions[None, :])
    slot_rank = jnp.sum(earlier.astype(jnp.int32), axis=0)
    slot_ids = jnp.arange(CAP, dtype=jnp.int32)
    choose_slot = (owners[None, :] == my_index) & (slot_rank[None, :] == slot_ids[:, None])
    local_rows = jnp.sum(jnp.where(choose_slot, slot_row[None, :], 0), axis=1)
    present = jnp.any(choose_slot, axis=1)
    outgoing = jnp.concatenate(
        [lax.dynamic_slice_in_dim(corpus, local_rows[k], 1, 0) for k in range(CAP)], axis=0
    )
    outgoing = jnp.where(present[:, None, None], outgoing, jnp.zeros_like(outgoing)).reshape(
        CAP, -1
    )
    location = owners * CAP + slot_rank
    query_all, arrived = (
        lax.all_gather(queries, "tensor", axis=0, tiled=True),
        lax.all_gather(outgoing, "tensor", axis=0, tiled=True),
    )
    slots = jnp.arange(arrived.shape[0], dtype=jnp.int32)
    chosen = (location[:, None] == slots[None, :]).astype(jnp.bfloat16)
    fetched = jnp.dot(chosen, arrived, preferred_element_type=jnp.float32).astype(jnp.bfloat16)
    stream_in = jnp.concatenate([query_all, fetched.reshape(-1, features)], axis=0)
    normal_rows = normed(stream_in, gain_attn)
    projected = tuple(
        (
            by_rows(normal_rows, weight).astype(jnp.bfloat16)
            for weight in (query_weight, key_weight, value_weight)
        )
    )
    tokens = stream_in.shape[0]
    heads_here = query_weight.shape[0] // HDIM
    query_rows_total = query_all.shape[0]
    pair_ids = jnp.concatenate(
        [jnp.arange(query_rows_total, dtype=jnp.int32) // QLEN, jnp.repeat(segment, BLK)]
    )
    same_pair = pair_ids[:, None] == pair_ids[None, :]
    query_heads = projected[0].reshape(tokens, heads_here, HDIM)
    key_heads = projected[1].reshape(tokens, heads_here, HDIM)
    value_heads = projected[2].reshape(tokens, heads_here, HDIM)
    scores = jnp.einsum(
        "qhd,khd->hqk", query_heads, key_heads, preferred_element_type=jnp.float32
    ) * HDIM ** (-0.5)
    scores = jnp.where(same_pair[None, :, :], scores, -1e30)
    row_max = jnp.max(scores, axis=-1, keepdims=True)
    weights = jnp.exp(scores - row_max)
    probability = (weights / jnp.sum(weights, axis=-1, keepdims=True)).astype(jnp.bfloat16)
    context = (
        jnp.einsum("hqk,khd->qhd", probability, value_heads, preferred_element_type=jnp.float32)
        .astype(jnp.bfloat16)
        .reshape(tokens, heads_here * HDIM)
    )
    rows_here = tokens // devices
    first_mine = my_index * rows_here
    attended = lax.psum(jnp.dot(context, out_weight, preferred_element_type=jnp.float32), "tensor")
    stream_mid = (stream_in.astype(jnp.float32) + attended).astype(jnp.bfloat16)
    normal_mid = normed(stream_mid, gain_ffn)
    mid_mine = lax.dynamic_slice_in_dim(stream_mid, first_mine, rows_here, 0)
    gate_value = by_rows(normal_mid, gate_weight)
    up_value = by_rows(normal_mid, up_weight)
    hidden = (jax.nn.gelu(gate_value, approximate=True) * up_value).astype(jnp.bfloat16)
    ffn_result = lax.psum_scatter(
        jnp.dot(hidden, down_weight, preferred_element_type=jnp.float32),
        "tensor",
        scatter_dimension=0,
        tiled=True,
    )
    return (mid_mine.astype(jnp.float32) + ffn_result).astype(jnp.bfloat16)


Z, Y, C = 4, 2, 2
UNIT = 16
OWN = 14
HALF = 112
P1 = 4
P2 = 2
LAG1 = 2
LAG2 = 5
SLABS = 5
LAYER = Y * SLABS * 8
MESH = pl.DeviceIdType.MESH


def fits(mesh):
    return mesh.shape["tensor"] == Z * Y * C


def step_count(values, step, most):
    total = jnp.zeros_like(values)
    for k in range(1, most):
        total = total + jnp.where(values >= k * step, 1, 0)
    return total


def fused_kernel(
    queries, corpus, owner_h, slot_h, segment_h, wq, wk, wv, wo, wg, wu, wd, gain1_h, gain2_h,
    out_ref,
    owner, slot, segment, gain1, gain2, corpus_v, arrived, xsend, xin, normal, qkv_v, wqkv_v, wo_v, wg_v, wu_v, wd_v,
    pair_col, ctx_out, ctx_in, resid, mid,
    part1, ry1, s1, rz1,
    part2, ry2, s2, rz2,
    lsem, xs, xr, ag1_s, ag1_r, rs1_s, rs1_r, ag2_s, ag2_r, rs2_s, rs2_r,
):
    bf, f32, i32 = jnp.bfloat16, jnp.float32, jnp.int32
    me = lax.axis_index("tensor")
    z, y, c = me // (Y * C), (me // C) % Y, me % C
    features = gain1.shape[1]
    half = features // 2
    blocks = slot.shape[0]

    def flat(zi, yi, ci):
        return zi * (Y * C) + yi * C + ci

    ypart = flat(z, 1 - y, c)
    cpart = flat(z, y, 1 - c)
    end = (z == 0) | (z == Z - 1)
    inner = (z > 0) & (z < Z - 1)
    zmate = z + 1 - 2 * (z % 2)
    zmid = jnp.where(z < 2, 2, 1)
    zend = jnp.where(z < 2, 3, 0)
    far = (zmid, zend)
    mate = flat(zmate, y, c)
    middle = flat(zmid, y, c)

    def local(src, dst, i):
        return pltpu.make_async_copy(src, dst, lsem.at[i])

    def remote(src, dst, ssem, rsem, peer):
        return pltpu.make_async_remote_copy(
            src_ref=src, dst_ref=dst, send_sem=ssem, recv_sem=rsem,
            device_id={"tensor": peer}, device_id_type=MESH,
        )

    def ag1_view(m, zi, yi, ci):
        if m == 0:
            return arrived.at[zi, yi * SLABS + ci]
        cols = pl.ds(pl.multiple_of(ci * half, half), half)
        return arrived.at[zi, pl.ds(yi * SLABS + 2, 3), :, cols]

    barrier = pltpu.get_barrier_semaphore()
    peers = (ypart, cpart, flat((z + 1) % Z, y, c), flat((z + 2) % Z, y, c), flat((z + 3) % Z, y, c))
    for peer in peers:
        pl.semaphore_signal(barrier, inc=1, device_id={"tensor": peer}, device_id_type=MESH)

    tables = [
        local(src, dst, 9 + k)
        for k, (src, dst) in enumerate(((owner_h, owner), (slot_h, slot), (segment_h, segment)))
    ]
    gains = [local(gain1_h, gain1, 12), local(gain2_h, gain2, 13)]
    for copy in tables:
        copy.start()
    get_query = local(queries, arrived.at[z, y * SLABS + c], 0)
    get_corpus = local(corpus, corpus_v, 1)
    get_query.start()
    get_corpus.start()
    for copy in gains:
        copy.start()
    qkv_loads = [
        local(w, wqkv_v.at[pl.ds(k * HDIM, HDIM)], 2 + k) for k, w in enumerate((wq, wk, wv))
    ]
    shared = [(wo, wo_v), (wg, wg_v), (wu, wu_v), (wd, wd_v)]
    own_loads = [local(w, v.at[0], 5 + k) for k, (w, v) in enumerate(shared)]
    give = [
        remote(w, v.at[1], xs.at[2 + k], xr.at[2 + k], cpart) for k, (w, v) in enumerate(shared)
    ]

    drains = []

    for copy in tables:
        copy.wait()
    found = jnp.int32(0)
    spots = [jnp.int32(0)] * CAP
    for b in range(blocks):
        hit = owner[0, b] == me
        row = slot[b]
        for k in range(CAP):
            spots[k] = jnp.where(hit & (found == k), row, spots[k])
        found = found + jnp.where(hit, 1, 0)
    pl.semaphore_wait(barrier, len(peers))

    order = (z, zmate, zmid, zend)

    def ag1_y(m, zi, yi):
        v, at = ag1_view(m, zi, yi, c), m * 20 + zi
        return remote(v, v, ag1_s.at[at], ag1_r.at[at], ypart)

    def ag1_c(m, zi, yi):
        v, at = ag1_view(m, zi, yi, c), m * 20 + 4 + zi * 2 + yi
        return remote(v, v, ag1_s.at[at], ag1_r.at[at], cpart)

    def ag1_c_in(m, zi, yi):
        v, at = ag1_view(m, zi, yi, 1 - c), m * 20 + 4 + zi * 2 + yi
        return remote(v, v, ag1_s.at[at], ag1_r.at[at], cpart)

    def ag1_z(m, zi, k, peer):
        v = ag1_view(m, zi, y, c)
        return remote(v, v, ag1_s.at[m * 20 + 12 + k], ag1_r.at[m * 20 + 12 + zi], peer)

    def ag1_first(m):
        ag1_z(m, z, 0, mate).start()
        pl.when(inner)(lambda: ag1_z(m, z, 1, middle).start())
        ag1_y(m, z, y).start()
        ag1_c(m, z, y).start()

    def ag1_drain():
        for m in range(2):
            ag1_z(m, z, 0, mate).wait_send()
            pl.when(inner)(lambda: ag1_z(m, z, 1, middle).wait_send())
            for zi in range(Z):
                ag1_y(m, zi, y).wait_send()
                for yi in range(Y):
                    ag1_c(m, zi, yi).wait_send()
            for i in (1, 2, 3):
                pl.when(inner)(lambda: ag1_z(m, order[i], 1 + i, mate).wait_send())

    get_query.wait()
    ag1_first(0)
    get_corpus.wait()
    mine = [corpus_v[spots[k]] for k in range(CAP)]
    for side in range(2):

        @pl.when(c == side)
        def _():
            here = slice(side * half, side * half + half)
            there = slice((1 - side) * half, (1 - side) * half + half)
            for k in range(CAP):
                xsend[k] = mine[k][:, there]
            swap = remote(xsend, xin, xs.at[0], xr.at[0], cpart)
            swap.start()
            for yi in range(Y):

                @pl.when(y == yi)
                def _():
                    for k in range(CAP):
                        arrived[z, yi * SLABS + 2 + k, side * BLK : side * BLK + BLK, here] = mine[k][:, here]

            swap.wait_recv()
            other = (1 - side) * BLK
            for yi in range(Y):

                @pl.when(y == yi)
                def _():
                    for k in range(CAP):
                        arrived[z, yi * SLABS + 2 + k, other : other + BLK, here] = xin[k]

    ag1_first(1)
    drains.append(lambda: remote(xsend, xin, xs.at[0], xr.at[0], cpart).wait_send())
    for load in qkv_loads + own_loads:
        load.start()
    for copy in give:
        copy.start()

    drains.append(lambda: [copy.wait_send() for copy in give])
    lane = lax.broadcasted_iota(i32, (8, 128), 1)
    owner_row = jnp.zeros((8, 128), i32)
    seg_row = jnp.zeros((8, 128), i32)
    for b in range(blocks):
        owner_row = jnp.where(lane == b, owner[0, b], owner_row)
        seg_row = jnp.where(lane == b, segment[b], seg_row)
    rank_row = jnp.zeros((8, 128), i32)
    for b in range(blocks):
        rank_row = rank_row + jnp.where((owner_row == owner[0, b]) & (lane > b), 1, 0)
    start_row = (
        (owner_row >> 2) * LAYER + ((owner_row >> 1) & 1) * (SLABS * 8) + 16
        + rank_row * 8 + (owner_row & 1) * BLK
    )
    start_row = jnp.where(lane < blocks, start_row, -1000).astype(f32)[:1]
    seg_row = seg_row.astype(f32)[:1]
    sub = lax.broadcasted_iota(i32, (128, 128), 0)
    lanes = lax.broadcasted_iota(i32, (128, 128), 1)
    start_col = jnp.sum(jnp.where(sub == lanes, start_row, 0.0), axis=1, keepdims=True)
    seg_col = jnp.sum(jnp.where(sub == lanes, seg_row, 0.0), axis=1, keepdims=True)

    def slot_parts(j):
        zj = step_count(j, LAYER, Z)
        rem = j - zj * LAYER
        within = rem - jnp.where(rem >= SLABS * 8, SLABS * 8, 0)
        return zj.astype(f32), within < 16, ((j >> 2) << 2).astype(f32)

    rows_all = Z * LAYER
    zj, is_query, begin = slot_parts(lax.broadcasted_iota(i32, (rows_all, 1), 0))
    held = jnp.max(jnp.where(begin == start_row, seg_row, -1.0), axis=1, keepdims=True)
    pair_col[...] = jnp.where(is_query, zj, held)
    zj, is_query, begin = slot_parts(lax.broadcasted_iota(i32, (1, rows_all), 1))
    held = jnp.max(jnp.where(begin == start_col, seg_col, -1.0), axis=0, keepdims=True)
    pair_row = jnp.where(is_query, zj, held)

    def chosen(first, count, side):
        i = lax.broadcasted_iota(i32, (count, 1), 0) + first
        turn = step_count(i, OWN, 8)
        row = OWN * (2 * turn + side) + i - OWN * turn
        from_query = (
            (row >> 5) * LAYER + ((row >> 4) & 1) * (SLABS * 8) + ((row >> 3) & 1) * 8 + (row & 7)
        )
        behind = row - Z * QLEN
        block = lax.broadcasted_iota(i32, (count, 128), 1) == (behind >> 2)
        start = jnp.sum(jnp.where(block, start_row, 0.0), axis=1, keepdims=True)
        src = jnp.where(behind < 0, from_query, start.astype(i32) + (behind & 3))
        at = lax.broadcasted_iota(i32, (count, rows_all), 1)
        return (at == src).astype(f32).astype(bf)

    def project(zi):
        def some(i, carry):
            rows = arrived[zi, pl.ds(2 * i, 2)].reshape(16, features)
            normal[pl.ds(pl.multiple_of(i * 16, 16), 16), :] = normed(rows, gain1[...])
            return carry

        lax.fori_loop(0, LAYER // 16, some, 0)
        qkv_v[zi] = by_rows(normal[...], wqkv_v[...]).astype(bf)

    def from_z(i):
        zi = order[i]
        for m in range(2):
            ag1_z(m, zi, 0, mate).wait_recv()
            onward = middle if i == 1 else mate
            pl.when(inner)(lambda: ag1_z(m, zi, 1 + i, onward).start())
            ag1_y(m, zi, y).start()
            ag1_c(m, zi, y).start()

    def from_y(i):
        zi = order[i]
        for m in range(2):
            ag1_y(m, zi, 1 - y).wait_recv()
            ag1_c(m, zi, 1 - y).start()

    def finish_layer(i):
        zi = order[i]
        for m in range(2):
            for yi in range(Y):
                ag1_c_in(m, zi, yi).wait_recv()
        if i == 0:
            for load in qkv_loads + gains:
                load.wait()
        project(zi)

    from_z(1)
    from_y(0)
    from_z(2)
    finish_layer(0)
    from_z(3)
    from_y(1)
    finish_layer(1)
    from_y(2)
    finish_layer(2)
    from_y(3)
    finish_layer(3)
    drains.append(ag1_drain)
    qkv = qkv_v[...].reshape(rows_all, 3 * HDIM)
    q, k, v = qkv[:, :HDIM], qkv[:, HDIM : 2 * HDIM], qkv[:, 2 * HDIM :]
    scores = by_rows(q, k) * HDIM ** (-0.5)
    scores = jnp.where(pair_col[...] == pair_row, scores, -1e30)
    weights = jnp.exp(scores - jnp.max(scores, axis=-1, keepdims=True))
    probability = (weights / jnp.sum(weights, axis=-1, keepdims=True)).astype(bf)
    context = jnp.dot(probability, v, preferred_element_type=f32).astype(bf)
    ctx_out[...] = jnp.dot(chosen(0, HALF, 1 - c), context, preferred_element_type=f32).astype(bf)
    ctx_swap = remote(ctx_out, ctx_in, xs.at[1], xr.at[1], cpart)
    ctx_swap.start()
    drains.append(ctx_swap.wait_send)
    ctx_mine = jnp.dot(chosen(0, HALF, c), context, preferred_element_type=f32).astype(bf)
    own_loads[0].wait()
    give[0].wait_recv()
    ctx_swap.wait_recv()
    ctx = jnp.concatenate([ctx_mine, ctx_in[...]], axis=1)

    def always(zi, yi):
        return None

    def present(zi, yi):
        return (zi < Z - 1) | (yi == c)

    def compact(zi, yi):
        late = jnp.where((c == 1) & (zi == Z - 1) & (yi == 1), 1, 0)
        return jnp.minimum(zi * Y + yi - late, HALF // UNIT - 1)

    def when(cond, fn):
        if cond is None:
            fn()
        else:
            pl.when(cond)(fn)

    def both(a, b):
        return a if b is None else a & b

    class Scatter:
        def __init__(self, part, ry, s, rz, ss, rs, unit, has):
            self.part, self.ry, self.s, self.rz = part, ry, s, rz
            self.ss, self.rs, self.unit, self.has = ss, rs, unit, has

        def to_y(self, p, d):
            at = p * 12 + d
            return remote(
                self.part.at[p, self.unit(d, 1 - y)], self.ry.at[p, d],
                self.ss.at[at], self.rs.at[at], ypart,
            )

        def to_z(self, p, d, src):
            at = p * 12 + 4
            return remote(
                self.s.at[p, d], self.rz.at[p, src],
                self.ss.at[at + d], self.rs.at[at + src], flat(d, y, c),
            )

        def send_y(self, p, d):
            when(self.has(d, 1 - y), lambda: self.to_y(p, d).start())

        def mine_and_y(self, p, d):
            self.to_y(p, d).wait_recv()
            return self.part[p, self.unit(d, y)].astype(f32) + self.ry[p, d].astype(f32)

        def relay(self, p, d):
            def run():
                self.s[p, d] = self.mine_and_y(p, d).astype(bf)
                self.to_z(p, d, z).start()

            when(self.has(d, y), run)

        def own_sum(self, p):
            total = self.mine_and_y(p, z)
            for src in order[1:]:
                self.to_z(p, zmate, src).wait_recv()
                total = total + self.rz[p, src].astype(f32)
            return total

        def drain(self, pieces):
            for p in range(pieces):
                for d in range(Z):
                    when(self.has(d, 1 - y), lambda: self.to_y(p, d).wait_send())
                for d in order[1:]:
                    when(self.has(d, y), lambda: self.to_z(p, d, z).wait_send())

    one = Scatter(part1, ry1, s1, rz1, rs1_s, rs1_r, compact, present)
    width = features // P1
    wo_all = wo_v[...].reshape(2 * HDIM, features)
    for p in range(P1):
        cols = slice(p * width, (p + 1) * width)
        product = jnp.dot(ctx, wo_all[:, cols], preferred_element_type=f32)
        part1[p] = product.astype(bf).reshape(HALF // UNIT, UNIT, width)
        for d in (zend, zmid, zmate, z):
            one.send_y(p, d)

    drains.append(lambda: one.drain(P1))
    mine_at = compact(z, y)
    has_unit = present(z, y)
    rows_here = chosen(mine_at * UNIT, UNIT, c)
    for p in range(P1):
        for t in range(Z):
            for half_at in range(2):
                n = width // 2
                cols = slice(p * width + half_at * n, p * width + half_at * n + n)
                rows = arrived[t, :, :, cols].reshape(LAYER, n)
                took = jnp.dot(
                    rows_here[:, t * LAYER : (t + 1) * LAYER], rows, preferred_element_type=f32
                )
                spot = (p, slice(None), slice(half_at * n, half_at * n + n))
                resid[spot] = took if t == 0 else resid[spot] + took

    def ag2_y(p, zi, yi):
        v, at = mid.at[p, compact(zi, yi)], p * 12 + zi
        return remote(v, v, ag2_s.at[at], ag2_r.at[at], ypart)

    def ag2_z(p, zi, k, peer):
        v = mid.at[p, compact(zi, y)]
        return remote(v, v, ag2_s.at[p * 12 + 4 + k], ag2_r.at[p * 12 + 8 + zi], peer)

    def ag2_drain():
        for p in range(P1):

            @pl.when(has_unit)
            def _():
                ag2_z(p, z, 0, mate).wait_send()
                ag2_z(p, z, 1, middle).wait_send()

            for i in (2, 3):

                @pl.when(inner & present(order[i], y))
                def _():
                    ag2_z(p, order[i], i, mate).wait_send()

            for zi in range(Z):
                pl.when(present(zi, y))(lambda: ag2_y(p, zi, y).wait_send())

    def own_piece(p):
        @pl.when(has_unit)
        def _():
            mid[p, mine_at] = (resid[p] + one.own_sum(p)).astype(bf)
            ag2_z(p, z, 0, mate).start()
            ag2_z(p, z, 1, middle).start()
            ag2_y(p, z, y).start()

    def forward(p):
        for i in range(1, Z):
            zi = order[i]

            @pl.when(present(zi, y))
            def _():
                ag2_z(p, zi, 0, mate).wait_recv()
                if i > 1:
                    pl.when(inner)(lambda: ag2_z(p, zi, i, mate).start())
                ag2_y(p, zi, y).start()

    for step in range(P1 + LAG2):
        if step < P1:
            for d in (zend, zmid, zmate):
                one.relay(step, d)
        if 0 <= step - LAG1 < P1:
            own_piece(step - LAG1)
        if 0 <= step - LAG2 < P1:
            forward(step - LAG2)
    drains.append(ag2_drain)

    for k in (1, 2):
        own_loads[k].wait()
        give[k].wait_recv()
    hidden_units = wg_v.shape[1]
    squares = gate = up = None
    for p in range(P1):
        for zi in range(Z):
            when(present(zi, 1 - y), lambda: ag2_y(p, zi, 1 - y).wait_recv())
        cols = slice(p * width, (p + 1) * width)
        rows = mid[p].reshape(HALF, width).astype(f32)
        square = jnp.sum(rows * rows, axis=1, keepdims=True)
        scaled = (rows * gain2[:, cols]).astype(bf)
        g = by_rows(scaled, wg_v[:, :, cols].reshape(2 * hidden_units, width))
        u = by_rows(scaled, wu_v[:, :, cols].reshape(2 * hidden_units, width))
        squares, gate, up = (square, g, u) if p == 0 else (squares + square, gate + g, up + u)
    inverse = lax.rsqrt(squares * (1.0 / features) + 1e-06)
    hidden = (jax.nn.gelu(gate * inverse, approximate=True) * (up * inverse)).astype(bf)

    def spread(first, count):
        j = lax.broadcasted_iota(i32, (count, 1), 0) + first
        turn = j >> 4
        src = jnp.where((j & 15) < OWN, turn * OWN + (j & 15), -1)
        return (lax.broadcasted_iota(i32, (count, HALF), 1) == src).astype(f32).astype(bf)

    hidden = jnp.dot(spread(0, Z * Y * UNIT), hidden, preferred_element_type=f32).astype(bf)
    own_loads[3].wait()
    give[3].wait_recv()

    def plain_unit(zi, yi):
        return zi * Y + yi

    two = Scatter(part2, ry2, s2, rz2, rs2_s, rs2_r, plain_unit, always)
    drains.append(lambda: two.drain(P2))
    width2 = features // P2
    wd_all = wd_v[...].reshape(2 * hidden_units, features)
    for p in range(P2):
        cols = slice(p * width2, (p + 1) * width2)
        product = jnp.dot(hidden, wd_all[:, cols], preferred_element_type=f32)
        part2[p] = product.astype(bf).reshape(Z * Y, UNIT, width2)
        two.send_y(p, zend)
    for d in (zmid, zmate, z):
        for p in range(P2):
            two.send_y(p, d)
    last_rows = spread((z * Y + y) * UNIT, UNIT)
    lasts = [
        jnp.dot(last_rows, mid[p].reshape(HALF, width), preferred_element_type=f32)
        for p in range(P1)
    ]
    last = jnp.concatenate(lasts, axis=1)
    for d in (zend, zmid, zmate):
        for p in range(P2):
            two.relay(p, d)
    for p in range(P2):
        cols = slice(p * width2, (p + 1) * width2)
        out_ref[:, cols] = (last[:, cols] + two.own_sum(p))[:OWN].astype(bf)

    for drain in drains:
        drain()


def fused_body(
    queries, corpus, block_owner, slot_row, segment, query_weight, key_weight, value_weight,
    out_weight, gain_attn, gain_ffn, gate_weight, up_weight, down_weight,
):
    features = queries.shape[1]
    hidden = gate_weight.shape[0]
    bf = jnp.bfloat16
    half = features // 2
    units = HALF // UNIT

    def scatter_bufs(pieces, count):
        width = features // pieces
        return [
            pltpu.VMEM((pieces, count, UNIT, width), bf),
            pltpu.VMEM((pieces, Z, UNIT, width), bf),
            pltpu.VMEM((pieces, Z, UNIT, width), bf),
            pltpu.VMEM((pieces, Z, UNIT, width), bf),
        ]

    dma = pltpu.SemaphoreType.DMA
    any_spec = pl.BlockSpec(memory_space=pl.ANY)
    vmem_spec = pl.BlockSpec(memory_space=pltpu.VMEM)
    return pl.pallas_call(
        fused_kernel,
        out_shape=jax.ShapeDtypeStruct((OWN, features), bf),
        in_specs=[any_spec] * 14,
        out_specs=vmem_spec,
        scratch_shapes=[
            pltpu.SMEM((1, block_owner.shape[0]), jnp.int32),
            pltpu.SMEM(slot_row.shape, jnp.int32),
            pltpu.SMEM(segment.shape, jnp.int32),
            pltpu.VMEM((1, features), jnp.float32),
            pltpu.VMEM((1, features), jnp.float32),
            pltpu.VMEM(corpus.shape, bf),
            pltpu.VMEM((Z, Y * SLABS, 8, features), bf),
            pltpu.VMEM((CAP, BLK, half), bf),
            pltpu.VMEM((CAP, BLK, half), bf),
            pltpu.VMEM((LAYER, features), bf),
            pltpu.VMEM((Z, LAYER, 3 * HDIM), bf),
            pltpu.VMEM((3 * HDIM, features), bf),
            pltpu.VMEM((2, HDIM, features), bf),
            pltpu.VMEM((2, hidden, features), bf),
            pltpu.VMEM((2, hidden, features), bf),
            pltpu.VMEM((2, hidden, features), bf),
            pltpu.VMEM((Z * LAYER, 1), jnp.float32),
            pltpu.VMEM((HALF, HDIM), bf),
            pltpu.VMEM((HALF, HDIM), bf),
            pltpu.VMEM((P1, UNIT, features // P1), jnp.float32),
            pltpu.VMEM((P1, units, UNIT, features // P1), bf),
        ]
        + scatter_bufs(P1, units)
        + scatter_bufs(P2, Z * Y)
        + [dma((14,)), dma((6,)), dma((6,))]
        + [dma((40,))] * 2
        + [dma((12 * P1,))] * 4
        + [dma((12 * P2,))] * 2,
        compiler_params=pltpu.CompilerParams(
            collective_id=0, has_side_effects=True, vmem_limit_bytes=56 * 2**20
        ),
    )(
        queries, corpus, block_owner.reshape(1, -1), slot_row, segment, query_weight, key_weight,
        value_weight, out_weight, gate_weight, up_weight, down_weight, gain_attn[None, :], gain_ffn[None, :],
    )


def solution(mesh):
    placed = (
        P(("groups", "tensor"), None),
        P(("groups", "tensor"), None, None),
        P("groups", None),
        P("groups"),
        P("groups"),
        P("tensor", None),
        P("tensor", None),
        P("tensor", None),
        P("tensor", None),
        P(),
        P(),
        P("tensor", None),
        P("tensor", None),
        P("tensor", None),
    )
    body = fused_body if fits(mesh) else plain_body
    return jax.shard_map(
        body, mesh=mesh, in_specs=placed, out_specs=P(("groups", "tensor"), None), check_vma=False
    )
```

```python
import functools

import jax
import jax.numpy as jnp
from jax import lax
from jax.experimental import pallas as pl
from jax.experimental.pallas import tpu as pltpu
from jax.sharding import PartitionSpec as P

HDIM = 64
QLEN = 32
BLK = 4
CAP = 3


def normed(stream, gain):
    values = stream.astype(jnp.float32)
    mean_square = jnp.mean(values * values, axis=-1, keepdims=True)
    return (values * lax.rsqrt(mean_square + 1e-06) * gain).astype(jnp.bfloat16)


def by_rows(left, weight):
    return lax.dot_general(
        left, weight, (((1,), (1,)), ((), ())), preferred_element_type=jnp.float32
    )


def plain_body(
    queries,
    corpus,
    block_owner,
    slot_row,
    segment,
    query_weight,
    key_weight,
    value_weight,
    out_weight,
    gain_attn,
    gain_ffn,
    gate_weight,
    up_weight,
    down_weight,
):
    devices = lax.axis_size("tensor")
    my_index = lax.axis_index("tensor")
    owners = block_owner[:, 0]
    blocks_total = owners.shape[0]
    features = queries.shape[1]
    positions = jnp.arange(blocks_total, dtype=jnp.int32)
    earlier = (owners[:, None] == owners[None, :]) & (positions[:, None] < positions[None, :])
    slot_rank = jnp.sum(earlier.astype(jnp.int32), axis=0)
    slot_ids = jnp.arange(CAP, dtype=jnp.int32)
    choose_slot = (owners[None, :] == my_index) & (slot_rank[None, :] == slot_ids[:, None])
    local_rows = jnp.sum(jnp.where(choose_slot, slot_row[None, :], 0), axis=1)
    present = jnp.any(choose_slot, axis=1)
    outgoing = jnp.concatenate(
        [lax.dynamic_slice_in_dim(corpus, local_rows[k], 1, 0) for k in range(CAP)], axis=0
    )
    outgoing = jnp.where(present[:, None, None], outgoing, jnp.zeros_like(outgoing)).reshape(
        CAP, -1
    )
    location = owners * CAP + slot_rank
    query_all, arrived = (
        lax.all_gather(queries, "tensor", axis=0, tiled=True),
        lax.all_gather(outgoing, "tensor", axis=0, tiled=True),
    )
    slots = jnp.arange(arrived.shape[0], dtype=jnp.int32)
    chosen = (location[:, None] == slots[None, :]).astype(jnp.bfloat16)
    fetched = jnp.dot(chosen, arrived, preferred_element_type=jnp.float32).astype(jnp.bfloat16)
    stream_in = jnp.concatenate([query_all, fetched.reshape(-1, features)], axis=0)
    normal_rows = normed(stream_in, gain_attn)
    projected = tuple(
        (
            by_rows(normal_rows, weight).astype(jnp.bfloat16)
            for weight in (query_weight, key_weight, value_weight)
        )
    )
    tokens = stream_in.shape[0]
    heads_here = query_weight.shape[0] // HDIM
    query_rows_total = query_all.shape[0]
    pair_ids = jnp.concatenate(
        [jnp.arange(query_rows_total, dtype=jnp.int32) // QLEN, jnp.repeat(segment, BLK)]
    )
    same_pair = pair_ids[:, None] == pair_ids[None, :]
    query_heads = projected[0].reshape(tokens, heads_here, HDIM)
    key_heads = projected[1].reshape(tokens, heads_here, HDIM)
    value_heads = projected[2].reshape(tokens, heads_here, HDIM)
    scores = jnp.einsum(
        "qhd,khd->hqk", query_heads, key_heads, preferred_element_type=jnp.float32
    ) * HDIM ** (-0.5)
    scores = jnp.where(same_pair[None, :, :], scores, -1e30)
    row_max = jnp.max(scores, axis=-1, keepdims=True)
    weights = jnp.exp(scores - row_max)
    probability = (weights / jnp.sum(weights, axis=-1, keepdims=True)).astype(jnp.bfloat16)
    context = (
        jnp.einsum("hqk,khd->qhd", probability, value_heads, preferred_element_type=jnp.float32)
        .astype(jnp.bfloat16)
        .reshape(tokens, heads_here * HDIM)
    )
    rows_here = tokens // devices
    first_mine = my_index * rows_here
    attended = lax.psum(jnp.dot(context, out_weight, preferred_element_type=jnp.float32), "tensor")
    stream_mid = (stream_in.astype(jnp.float32) + attended).astype(jnp.bfloat16)
    normal_mid = normed(stream_mid, gain_ffn)
    mid_mine = lax.dynamic_slice_in_dim(stream_mid, first_mine, rows_here, 0)
    gate_value = by_rows(normal_mid, gate_weight)
    up_value = by_rows(normal_mid, up_weight)
    hidden = (jax.nn.gelu(gate_value, approximate=True) * up_value).astype(jnp.bfloat16)
    ffn_result = lax.psum_scatter(
        jnp.dot(hidden, down_weight, preferred_element_type=jnp.float32),
        "tensor",
        scatter_dimension=0,
        tiled=True,
    )
    return (mid_mine.astype(jnp.float32) + ffn_result).astype(jnp.bfloat16)


Z, Y, C = 4, 2, 2
UNIT = 16
OWN = 14
HALF = 112
P1 = 4
P2 = 2
LAG1 = 2
LAG2 = 5
SLABS = 5
LAYER = Y * SLABS * 8
MESH = pl.DeviceIdType.MESH


def fits(mesh):
    return mesh.shape["tensor"] == Z * Y * C


def step_count(values, step, most):
    total = jnp.zeros_like(values)
    for k in range(1, most):
        total = total + jnp.where(values >= k * step, 1, 0)
    return total


def fused_kernel(
    queries, corpus, owner_h, slot_h, segment_h, wq, wk, wv, wo, wg, wu, wd, gain1_h, gain2_h,
    out_ref,
    owner, slot, segment, gain1, gain2, corpus_v, arrived, xsend, xin, qkv_v, wqkv_v, wo_v, wg_v, wu_v, wd_v,
    pair_col, ctx_out, ctx_in, resid, mid,
    part1, ry1, s1, rz1,
    part2, ry2, s2, rz2,
    lsem, xs, xr, ag1_s, ag1_r, rs1_s, rs1_r, ag2_s, ag2_r, rs2_s, rs2_r,
):
    bf, f32, i32 = jnp.bfloat16, jnp.float32, jnp.int32
    me = lax.axis_index("tensor")
    z, y, c = me // (Y * C), (me // C) % Y, me % C
    features = gain1.shape[1]
    half = features // 2
    blocks = slot.shape[0]

    def flat(zi, yi, ci):
        return zi * (Y * C) + yi * C + ci

    ypart = flat(z, 1 - y, c)
    cpart = flat(z, y, 1 - c)
    end = (z == 0) | (z == Z - 1)
    inner = (z > 0) & (z < Z - 1)
    zmate = z + 1 - 2 * (z % 2)
    zmid = jnp.where(z < 2, 2, 1)
    zend = jnp.where(z < 2, 3, 0)
    far = (zmid, zend)
    mate = flat(zmate, y, c)
    middle = flat(zmid, y, c)

    def local(src, dst, i):
        return pltpu.make_async_copy(src, dst, lsem.at[i])

    def remote(src, dst, ssem, rsem, peer):
        return pltpu.make_async_remote_copy(
            src_ref=src, dst_ref=dst, send_sem=ssem, recv_sem=rsem,
            device_id={"tensor": peer}, device_id_type=MESH,
        )

    def ag1_view(m, zi, yi, ci):
        if m == 0:
            return arrived.at[zi, yi * SLABS + ci]
        cols = pl.ds(pl.multiple_of(ci * half, half), half)
        return arrived.at[zi, pl.ds(yi * SLABS + 2, 3), :, cols]

    barrier = pltpu.get_barrier_semaphore()
    peers = (ypart, cpart, flat((z + 1) % Z, y, c), flat((z + 2) % Z, y, c), flat((z + 3) % Z, y, c))
    for peer in peers:
        pl.semaphore_signal(barrier, inc=1, device_id={"tensor": peer}, device_id_type=MESH)

    tables = [
        local(src, dst, 9 + k)
        for k, (src, dst) in enumerate(((owner_h, owner), (slot_h, slot), (segment_h, segment)))
    ]
    gains = [local(gain1_h, gain1, 12), local(gain2_h, gain2, 13)]
    for copy in tables:
        copy.start()
    get_query = local(queries, arrived.at[z, y * SLABS + c], 0)
    get_corpus = local(corpus, corpus_v, 1)
    get_query.start()
    get_corpus.start()
    for copy in gains:
        copy.start()
    qkv_loads = [
        local(w, wqkv_v.at[pl.ds(k * HDIM, HDIM)], 2 + k) for k, w in enumerate((wq, wk, wv))
    ]
    shared = [(wo, wo_v), (wg, wg_v), (wu, wu_v), (wd, wd_v)]
    own_loads = [local(w, v.at[0], 5 + k) for k, (w, v) in enumerate(shared)]
    give = [
        remote(w, v.at[1], xs.at[2 + k], xr.at[2 + k], cpart) for k, (w, v) in enumerate(shared)
    ]

    drains = []

    for copy in tables:
        copy.wait()
    found = jnp.int32(0)
    spots = [jnp.int32(0)] * CAP
    for b in range(blocks):
        hit = owner[0, b] == me
        row = slot[b]
        for k in range(CAP):
            spots[k] = jnp.where(hit & (found == k), row, spots[k])
        found = found + jnp.where(hit, 1, 0)
    pl.semaphore_wait(barrier, len(peers))

    order = (z, zmate, zmid, zend)

    def ag1_y(m, zi, yi):
        v, at = ag1_view(m, zi, yi, c), m * 20 + zi
        return remote(v, v, ag1_s.at[at], ag1_r.at[at], ypart)

    def ag1_c(m, zi, yi):
        v, at = ag1_view(m, zi, yi, c), m * 20 + 4 + zi * 2 + yi
        return remote(v, v, ag1_s.at[at], ag1_r.at[at], cpart)

    def ag1_c_in(m, zi, yi):
        v, at = ag1_view(m, zi, yi, 1 - c), m * 20 + 4 + zi * 2 + yi
        return remote(v, v, ag1_s.at[at], ag1_r.at[at], cpart)

    def ag1_z(m, zi, k, peer):
        v = ag1_view(m, zi, y, c)
        return remote(v, v, ag1_s.at[m * 20 + 12 + k], ag1_r.at[m * 20 + 12 + zi], peer)

    def ag1_first(m):
        ag1_z(m, z, 0, mate).start()
        pl.when(inner)(lambda: ag1_z(m, z, 1, middle).start())
        ag1_y(m, z, y).start()
        ag1_c(m, z, y).start()

    def ag1_drain():
        for m in range(2):
            ag1_z(m, z, 0, mate).wait_send()
            pl.when(inner)(lambda: ag1_z(m, z, 1, middle).wait_send())
            for zi in range(Z):
                ag1_y(m, zi, y).wait_send()
                for yi in range(Y):
                    ag1_c(m, zi, yi).wait_send()
            for i in (1, 2, 3):
                pl.when(inner)(lambda: ag1_z(m, order[i], 1 + i, mate).wait_send())

    get_query.wait()
    ag1_first(0)
    get_corpus.wait()
    mine = [corpus_v[spots[k]] for k in range(CAP)]
    for side in range(2):

        @pl.when(c == side)
        def _():
            here = slice(side * half, side * half + half)
            there = slice((1 - side) * half, (1 - side) * half + half)
            for k in range(CAP):
                xsend[k] = mine[k][:, there]
            swap = remote(xsend, xin, xs.at[0], xr.at[0], cpart)
            swap.start()
            for yi in range(Y):

                @pl.when(y == yi)
                def _():
                    for k in range(CAP):
                        arrived[z, yi * SLABS + 2 + k, side * BLK : side * BLK + BLK, here] = mine[k][:, here]

            swap.wait_recv()
            other = (1 - side) * BLK
            for yi in range(Y):

                @pl.when(y == yi)
                def _():
                    for k in range(CAP):
                        arrived[z, yi * SLABS + 2 + k, other : other + BLK, here] = xin[k]

    ag1_first(1)
    drains.append(lambda: remote(xsend, xin, xs.at[0], xr.at[0], cpart).wait_send())
    for load in qkv_loads + own_loads:
        load.start()
    for copy in give:
        copy.start()

    drains.append(lambda: [copy.wait_send() for copy in give])
    lane = lax.broadcasted_iota(i32, (8, 128), 1)
    owner_row = jnp.zeros((8, 128), i32)
    seg_row = jnp.zeros((8, 128), i32)
    for b in range(blocks):
        owner_row = jnp.where(lane == b, owner[0, b], owner_row)
        seg_row = jnp.where(lane == b, segment[b], seg_row)
    rank_row = jnp.zeros((8, 128), i32)
    for b in range(blocks):
        rank_row = rank_row + jnp.where((owner_row == owner[0, b]) & (lane > b), 1, 0)
    start_row = (
        (owner_row >> 2) * LAYER + ((owner_row >> 1) & 1) * (SLABS * 8) + 16
        + rank_row * 8 + (owner_row & 1) * BLK
    )
    start_row = jnp.where(lane < blocks, start_row, -1000).astype(f32)[:1]
    seg_row = seg_row.astype(f32)[:1]
    sub = lax.broadcasted_iota(i32, (128, 128), 0)
    lanes = lax.broadcasted_iota(i32, (128, 128), 1)
    start_col = jnp.sum(jnp.where(sub == lanes, start_row, 0.0), axis=1, keepdims=True)
    seg_col = jnp.sum(jnp.where(sub == lanes, seg_row, 0.0), axis=1, keepdims=True)

    def slot_parts(j):
        zj = step_count(j, LAYER, Z)
        rem = j - zj * LAYER
        within = rem - jnp.where(rem >= SLABS * 8, SLABS * 8, 0)
        return zj.astype(f32), within < 16, ((j >> 2) << 2).astype(f32)

    rows_all = Z * LAYER
    zj, is_query, begin = slot_parts(lax.broadcasted_iota(i32, (rows_all, 1), 0))
    held = jnp.max(jnp.where(begin == start_row, seg_row, -1.0), axis=1, keepdims=True)
    pair_col[...] = jnp.where(is_query, zj, held)
    zj, is_query, begin = slot_parts(lax.broadcasted_iota(i32, (1, rows_all), 1))
    held = jnp.max(jnp.where(begin == start_col, seg_col, -1.0), axis=0, keepdims=True)
    pair_row = jnp.where(is_query, zj, held)

    def chosen(first, count, side):
        i = lax.broadcasted_iota(i32, (count, 1), 0) + first
        turn = step_count(i, OWN, 8)
        row = OWN * (2 * turn + side) + i - OWN * turn
        from_query = (
            (row >> 5) * LAYER + ((row >> 4) & 1) * (SLABS * 8) + ((row >> 3) & 1) * 8 + (row & 7)
        )
        behind = row - Z * QLEN
        block = lax.broadcasted_iota(i32, (count, 128), 1) == (behind >> 2)
        start = jnp.sum(jnp.where(block, start_row, 0.0), axis=1, keepdims=True)
        src = jnp.where(behind < 0, from_query, start.astype(i32) + (behind & 3))
        at = lax.broadcasted_iota(i32, (count, rows_all), 1)
        return (at == src).astype(f32).astype(bf)

    for load in qkv_loads + gains:
        load.wait()

    def fold(i, carry):
        at = pl.ds(pl.multiple_of(i * 16, 16), 16)
        wqkv_v[at, :] = (wqkv_v[at, :].astype(f32) * gain1[...]).astype(bf)
        return carry

    lax.fori_loop(0, 3 * HDIM // 16, fold, 0)

    def project(layers):
        rows = jnp.concatenate([arrived[zi].reshape(LAYER, features) for zi in layers], axis=0)
        wide = rows.astype(f32)
        inverse = lax.rsqrt(jnp.mean(wide * wide, axis=1, keepdims=True) + 1e-06)
        found = (by_rows(rows, wqkv_v[...]) * inverse).astype(bf)
        for k, zi in enumerate(layers):
            qkv_v[zi] = found[k * LAYER : (k + 1) * LAYER]

    def from_z(i):
        zi = order[i]
        for m in range(2):
            ag1_z(m, zi, 0, mate).wait_recv()
            onward = middle if i == 1 else mate
            pl.when(inner)(lambda: ag1_z(m, zi, 1 + i, onward).start())
            ag1_y(m, zi, y).start()
            ag1_c(m, zi, y).start()

    def from_y(i):
        zi = order[i]
        for m in range(2):
            ag1_y(m, zi, 1 - y).wait_recv()
            ag1_c(m, zi, 1 - y).start()

    def finish(*layers):
        for i in layers:
            for m in range(2):
                for yi in range(Y):
                    ag1_c_in(m, order[i], yi).wait_recv()
        project([order[i] for i in layers])

    from_z(1)
    from_y(0)
    from_z(2)
    from_z(3)
    from_y(1)
    finish(0, 1)
    from_y(2)
    finish(2)
    from_y(3)
    finish(3)
    drains.append(ag1_drain)
    qkv = qkv_v[...].reshape(rows_all, 3 * HDIM)
    q, k, v = qkv[:, :HDIM], qkv[:, HDIM : 2 * HDIM], qkv[:, 2 * HDIM :]
    scores = by_rows(q, k) * HDIM ** (-0.5)
    scores = jnp.where(pair_col[...] == pair_row, scores, -1e30)
    weights = jnp.exp(scores - jnp.max(scores, axis=-1, keepdims=True))
    probability = (weights / jnp.sum(weights, axis=-1, keepdims=True)).astype(bf)
    context = jnp.dot(probability, v, preferred_element_type=f32).astype(bf)
    ctx_out[...] = jnp.dot(chosen(0, HALF, 1 - c), context, preferred_element_type=f32).astype(bf)
    ctx_swap = remote(ctx_out, ctx_in, xs.at[1], xr.at[1], cpart)
    ctx_swap.start()
    drains.append(ctx_swap.wait_send)
    ctx_mine = jnp.dot(chosen(0, HALF, c), context, preferred_element_type=f32).astype(bf)
    own_loads[0].wait()
    give[0].wait_recv()
    ctx_swap.wait_recv()
    ctx = jnp.concatenate([ctx_mine, ctx_in[...]], axis=1)

    def always(zi, yi):
        return None

    def present(zi, yi):
        return (zi < Z - 1) | (yi == c)

    def compact(zi, yi):
        late = jnp.where((c == 1) & (zi == Z - 1) & (yi == 1), 1, 0)
        return jnp.minimum(zi * Y + yi - late, HALF // UNIT - 1)

    def when(cond, fn):
        if cond is None:
            fn()
        else:
            pl.when(cond)(fn)

    def both(a, b):
        return a if b is None else a & b

    class Scatter:
        def __init__(self, part, ry, s, rz, ss, rs, unit, has):
            self.part, self.ry, self.s, self.rz = part, ry, s, rz
            self.ss, self.rs, self.unit, self.has = ss, rs, unit, has

        def to_y(self, p, d):
            at = p * 12 + d
            return remote(
                self.part.at[p, self.unit(d, 1 - y)], self.ry.at[p, d],
                self.ss.at[at], self.rs.at[at], ypart,
            )

        def to_z(self, p, d, src):
            at = p * 12 + 4
            return remote(
                self.s.at[p, d], self.rz.at[p, src],
                self.ss.at[at + d], self.rs.at[at + src], flat(d, y, c),
            )

        def send_y(self, p, d):
            when(self.has(d, 1 - y), lambda: self.to_y(p, d).start())

        def mine_and_y(self, p, d):
            self.to_y(p, d).wait_recv()
            return self.part[p, self.unit(d, y)].astype(f32) + self.ry[p, d].astype(f32)

        def relay(self, p, d):
            def run():
                self.s[p, d] = self.mine_and_y(p, d).astype(bf)
                self.to_z(p, d, z).start()

            when(self.has(d, y), run)

        def own_sum(self, p):
            total = self.mine_and_y(p, z)
            for src in order[1:]:
                self.to_z(p, zmate, src).wait_recv()
                total = total + self.rz[p, src].astype(f32)
            return total

        def drain(self, pieces):
            for p in range(pieces):
                for d in range(Z):
                    when(self.has(d, 1 - y), lambda: self.to_y(p, d).wait_send())
                for d in order[1:]:
                    when(self.has(d, y), lambda: self.to_z(p, d, z).wait_send())

    one = Scatter(part1, ry1, s1, rz1, rs1_s, rs1_r, compact, present)
    width = features // P1
    wo_all = wo_v[...].reshape(2 * HDIM, features)
    for p in range(P1):
        cols = slice(p * width, (p + 1) * width)
        product = jnp.dot(ctx, wo_all[:, cols], preferred_element_type=f32)
        part1[p] = product.astype(bf).reshape(HALF // UNIT, UNIT, width)
        for d in (zend, zmid, zmate, z):
            one.send_y(p, d)

    drains.append(lambda: one.drain(P1))
    mine_at = compact(z, y)
    has_unit = present(z, y)
    rows_here = chosen(mine_at * UNIT, UNIT, c)
    for p in range(P1):
        for t in range(Z):
            for half_at in range(2):
                n = width // 2
                cols = slice(p * width + half_at * n, p * width + half_at * n + n)
                rows = arrived[t, :, :, cols].reshape(LAYER, n)
                took = jnp.dot(
                    rows_here[:, t * LAYER : (t + 1) * LAYER], rows, preferred_element_type=f32
                )
                spot = (p, slice(None), slice(half_at * n, half_at * n + n))
                resid[spot] = took if t == 0 else resid[spot] + took

    def ag2_y(p, zi, yi):
        v, at = mid.at[p, compact(zi, yi)], p * 12 + zi
        return remote(v, v, ag2_s.at[at], ag2_r.at[at], ypart)

    def ag2_z(p, zi, k, peer):
        v = mid.at[p, compact(zi, y)]
        return remote(v, v, ag2_s.at[p * 12 + 4 + k], ag2_r.at[p * 12 + 8 + zi], peer)

    def ag2_drain():
        for p in range(P1):

            @pl.when(has_unit)
            def _():
                ag2_z(p, z, 0, mate).wait_send()
                ag2_z(p, z, 1, middle).wait_send()

            for i in (2, 3):

                @pl.when(inner & present(order[i], y))
                def _():
                    ag2_z(p, order[i], i, mate).wait_send()

            for zi in range(Z):
                pl.when(present(zi, y))(lambda: ag2_y(p, zi, y).wait_send())

    def own_piece(p):
        @pl.when(has_unit)
        def _():
            mid[p, mine_at] = (resid[p] + one.own_sum(p)).astype(bf)
            ag2_z(p, z, 0, mate).start()
            ag2_z(p, z, 1, middle).start()
            ag2_y(p, z, y).start()

    def forward(p):
        for i in range(1, Z):
            zi = order[i]

            @pl.when(present(zi, y))
            def _():
                ag2_z(p, zi, 0, mate).wait_recv()
                if i > 1:
                    pl.when(inner)(lambda: ag2_z(p, zi, i, mate).start())
                ag2_y(p, zi, y).start()

    for step in range(P1 + LAG2):
        if step < P1:
            for d in (zend, zmid, zmate):
                one.relay(step, d)
        if 0 <= step - LAG1 < P1:
            own_piece(step - LAG1)
        if 0 <= step - LAG2 < P1:
            forward(step - LAG2)
    drains.append(ag2_drain)

    for k in (1, 2):
        own_loads[k].wait()
        give[k].wait_recv()
    hidden_units = wg_v.shape[1]
    squares = gate = up = None
    for p in range(P1):
        for zi in range(Z):
            when(present(zi, 1 - y), lambda: ag2_y(p, zi, 1 - y).wait_recv())
        cols = slice(p * width, (p + 1) * width)
        rows = mid[p].reshape(HALF, width).astype(f32)
        square = jnp.sum(rows * rows, axis=1, keepdims=True)
        scaled = (rows * gain2[:, cols]).astype(bf)
        g = by_rows(scaled, wg_v[:, :, cols].reshape(2 * hidden_units, width))
        u = by_rows(scaled, wu_v[:, :, cols].reshape(2 * hidden_units, width))
        squares, gate, up = (square, g, u) if p == 0 else (squares + square, gate + g, up + u)
    inverse = lax.rsqrt(squares * (1.0 / features) + 1e-06)
    hidden = (jax.nn.gelu(gate * inverse, approximate=True) * (up * inverse)).astype(bf)

    def spread(first, count):
        j = lax.broadcasted_iota(i32, (count, 1), 0) + first
        turn = j >> 4
        src = jnp.where((j & 15) < OWN, turn * OWN + (j & 15), -1)
        return (lax.broadcasted_iota(i32, (count, HALF), 1) == src).astype(f32).astype(bf)

    hidden = jnp.dot(spread(0, Z * Y * UNIT), hidden, preferred_element_type=f32).astype(bf)
    own_loads[3].wait()
    give[3].wait_recv()

    def plain_unit(zi, yi):
        return zi * Y + yi

    two = Scatter(part2, ry2, s2, rz2, rs2_s, rs2_r, plain_unit, always)
    drains.append(lambda: two.drain(P2))
    width2 = features // P2
    wd_all = wd_v[...].reshape(2 * hidden_units, features)
    for p in range(P2):
        cols = slice(p * width2, (p + 1) * width2)
        product = jnp.dot(hidden, wd_all[:, cols], preferred_element_type=f32)
        part2[p] = product.astype(bf).reshape(Z * Y, UNIT, width2)
        two.send_y(p, zend)
    for d in (zmid, zmate, z):
        for p in range(P2):
            two.send_y(p, d)
    last_rows = spread((z * Y + y) * UNIT, UNIT)
    lasts = [
        jnp.dot(last_rows, mid[p].reshape(HALF, width), preferred_element_type=f32)
        for p in range(P1)
    ]
    last = jnp.concatenate(lasts, axis=1)
    for d in (zend, zmid, zmate):
        for p in range(P2):
            two.relay(p, d)
    for p in range(P2):
        cols = slice(p * width2, (p + 1) * width2)
        out_ref[:, cols] = (last[:, cols] + two.own_sum(p))[:OWN].astype(bf)

    for drain in drains:
        drain()


def fused_body(
    queries, corpus, block_owner, slot_row, segment, query_weight, key_weight, value_weight,
    out_weight, gain_attn, gain_ffn, gate_weight, up_weight, down_weight,
):
    features = queries.shape[1]
    hidden = gate_weight.shape[0]
    bf = jnp.bfloat16
    half = features // 2
    units = HALF // UNIT

    def scatter_bufs(pieces, count):
        width = features // pieces
        return [
            pltpu.VMEM((pieces, count, UNIT, width), bf),
            pltpu.VMEM((pieces, Z, UNIT, width), bf),
            pltpu.VMEM((pieces, Z, UNIT, width), bf),
            pltpu.VMEM((pieces, Z, UNIT, width), bf),
        ]

    dma = pltpu.SemaphoreType.DMA
    any_spec = pl.BlockSpec(memory_space=pl.ANY)
    vmem_spec = pl.BlockSpec(memory_space=pltpu.VMEM)
    return pl.pallas_call(
        fused_kernel,
        out_shape=jax.ShapeDtypeStruct((OWN, features), bf),
        in_specs=[any_spec] * 14,
        out_specs=vmem_spec,
        scratch_shapes=[
            pltpu.SMEM((1, block_owner.shape[0]), jnp.int32),
            pltpu.SMEM(slot_row.shape, jnp.int32),
            pltpu.SMEM(segment.shape, jnp.int32),
            pltpu.VMEM((1, features), jnp.float32),
            pltpu.VMEM((1, features), jnp.float32),
            pltpu.VMEM(corpus.shape, bf),
            pltpu.VMEM((Z, Y * SLABS, 8, features), bf),
            pltpu.VMEM((CAP, BLK, half), bf),
            pltpu.VMEM((CAP, BLK, half), bf),
            pltpu.VMEM((Z, LAYER, 3 * HDIM), bf),
            pltpu.VMEM((3 * HDIM, features), bf),
            pltpu.VMEM((2, HDIM, features), bf),
            pltpu.VMEM((2, hidden, features), bf),
            pltpu.VMEM((2, hidden, features), bf),
            pltpu.VMEM((2, hidden, features), bf),
            pltpu.VMEM((Z * LAYER, 1), jnp.float32),
            pltpu.VMEM((HALF, HDIM), bf),
            pltpu.VMEM((HALF, HDIM), bf),
            pltpu.VMEM((P1, UNIT, features // P1), jnp.float32),
            pltpu.VMEM((P1, units, UNIT, features // P1), bf),
        ]
        + scatter_bufs(P1, units)
        + scatter_bufs(P2, Z * Y)
        + [dma((14,)), dma((6,)), dma((6,))]
        + [dma((40,))] * 2
        + [dma((12 * P1,))] * 4
        + [dma((12 * P2,))] * 2,
        compiler_params=pltpu.CompilerParams(
            collective_id=0, has_side_effects=True, vmem_limit_bytes=56 * 2**20
        ),
    )(
        queries, corpus, block_owner.reshape(1, -1), slot_row, segment, query_weight, key_weight,
        value_weight, out_weight, gate_weight, up_weight, down_weight, gain_attn[None, :], gain_ffn[None, :],
    )


def solution(mesh):
    placed = (
        P(("groups", "tensor"), None),
        P(("groups", "tensor"), None, None),
        P("groups", None),
        P("groups"),
        P("groups"),
        P("tensor", None),
        P("tensor", None),
        P("tensor", None),
        P("tensor", None),
        P(),
        P(),
        P("tensor", None),
        P("tensor", None),
        P("tensor", None),
    )
    body = fused_body if fits(mesh) else plain_body
    return jax.shard_map(
        body, mesh=mesh, in_specs=placed, out_specs=P(("groups", "tensor"), None), check_vma=False
    )
```

```python
import functools

import jax
import jax.numpy as jnp
from jax import lax
from jax.experimental import pallas as pl
from jax.experimental.pallas import tpu as pltpu
from jax.sharding import PartitionSpec as P

HDIM = 64
QLEN = 32
BLK = 4
CAP = 3


def normed(stream, gain):
    values = stream.astype(jnp.float32)
    mean_square = jnp.mean(values * values, axis=-1, keepdims=True)
    return (values * lax.rsqrt(mean_square + 1e-06) * gain).astype(jnp.bfloat16)


def by_rows(left, weight):
    return lax.dot_general(
        left, weight, (((1,), (1,)), ((), ())), preferred_element_type=jnp.float32
    )


def plain_body(
    queries,
    corpus,
    block_owner,
    slot_row,
    segment,
    query_weight,
    key_weight,
    value_weight,
    out_weight,
    gain_attn,
    gain_ffn,
    gate_weight,
    up_weight,
    down_weight,
):
    devices = lax.axis_size("tensor")
    my_index = lax.axis_index("tensor")
    owners = block_owner[:, 0]
    blocks_total = owners.shape[0]
    features = queries.shape[1]
    positions = jnp.arange(blocks_total, dtype=jnp.int32)
    earlier = (owners[:, None] == owners[None, :]) & (positions[:, None] < positions[None, :])
    slot_rank = jnp.sum(earlier.astype(jnp.int32), axis=0)
    slot_ids = jnp.arange(CAP, dtype=jnp.int32)
    choose_slot = (owners[None, :] == my_index) & (slot_rank[None, :] == slot_ids[:, None])
    local_rows = jnp.sum(jnp.where(choose_slot, slot_row[None, :], 0), axis=1)
    present = jnp.any(choose_slot, axis=1)
    outgoing = jnp.concatenate(
        [lax.dynamic_slice_in_dim(corpus, local_rows[k], 1, 0) for k in range(CAP)], axis=0
    )
    outgoing = jnp.where(present[:, None, None], outgoing, jnp.zeros_like(outgoing)).reshape(
        CAP, -1
    )
    location = owners * CAP + slot_rank
    query_all, arrived = (
        lax.all_gather(queries, "tensor", axis=0, tiled=True),
        lax.all_gather(outgoing, "tensor", axis=0, tiled=True),
    )
    slots = jnp.arange(arrived.shape[0], dtype=jnp.int32)
    chosen = (location[:, None] == slots[None, :]).astype(jnp.bfloat16)
    fetched = jnp.dot(chosen, arrived, preferred_element_type=jnp.float32).astype(jnp.bfloat16)
    stream_in = jnp.concatenate([query_all, fetched.reshape(-1, features)], axis=0)
    normal_rows = normed(stream_in, gain_attn)
    projected = tuple(
        (
            by_rows(normal_rows, weight).astype(jnp.bfloat16)
            for weight in (query_weight, key_weight, value_weight)
        )
    )
    tokens = stream_in.shape[0]
    heads_here = query_weight.shape[0] // HDIM
    query_rows_total = query_all.shape[0]
    pair_ids = jnp.concatenate(
        [jnp.arange(query_rows_total, dtype=jnp.int32) // QLEN, jnp.repeat(segment, BLK)]
    )
    same_pair = pair_ids[:, None] == pair_ids[None, :]
    query_heads = projected[0].reshape(tokens, heads_here, HDIM)
    key_heads = projected[1].reshape(tokens, heads_here, HDIM)
    value_heads = projected[2].reshape(tokens, heads_here, HDIM)
    scores = jnp.einsum(
        "qhd,khd->hqk", query_heads, key_heads, preferred_element_type=jnp.float32
    ) * HDIM ** (-0.5)
    scores = jnp.where(same_pair[None, :, :], scores, -1e30)
    row_max = jnp.max(scores, axis=-1, keepdims=True)
    weights = jnp.exp(scores - row_max)
    probability = (weights / jnp.sum(weights, axis=-1, keepdims=True)).astype(jnp.bfloat16)
    context = (
        jnp.einsum("hqk,khd->qhd", probability, value_heads, preferred_element_type=jnp.float32)
        .astype(jnp.bfloat16)
        .reshape(tokens, heads_here * HDIM)
    )
    rows_here = tokens // devices
    first_mine = my_index * rows_here
    attended = lax.psum(jnp.dot(context, out_weight, preferred_element_type=jnp.float32), "tensor")
    stream_mid = (stream_in.astype(jnp.float32) + attended).astype(jnp.bfloat16)
    normal_mid = normed(stream_mid, gain_ffn)
    mid_mine = lax.dynamic_slice_in_dim(stream_mid, first_mine, rows_here, 0)
    gate_value = by_rows(normal_mid, gate_weight)
    up_value = by_rows(normal_mid, up_weight)
    hidden = (jax.nn.gelu(gate_value, approximate=True) * up_value).astype(jnp.bfloat16)
    ffn_result = lax.psum_scatter(
        jnp.dot(hidden, down_weight, preferred_element_type=jnp.float32),
        "tensor",
        scatter_dimension=0,
        tiled=True,
    )
    return (mid_mine.astype(jnp.float32) + ffn_result).astype(jnp.bfloat16)


Z, Y, C = 4, 2, 2
UNIT = 16
OWN = 14
HALF = 112
P1 = 4
P2 = 2
LAG1 = 2
LAG2 = 5
SLABS = 5
LAYER = Y * SLABS * 8
MESH = pl.DeviceIdType.MESH


def fits(mesh):
    return mesh.shape["tensor"] == Z * Y * C


def step_count(values, step, most):
    total = jnp.zeros_like(values)
    for k in range(1, most):
        total = total + jnp.where(values >= k * step, 1, 0)
    return total


def fused_kernel(
    queries, corpus, owner_h, slot_h, segment_h, wq, wk, wv, wo, wg, wu, wd, gain1_h, gain2_h,
    out_ref,
    owner, slot, segment, gain1, gain2, corpus_v, arrived, xsend, xin, qkv_v, wqkv_v, wo_v, wg_v, wu_v, wd_v,
    pair_col, ctx_out, ctx_in, resid, mid,
    part1, ry1, s1, rz1,
    keep2, part2, ry2, s2, rz2,
    lsem, xs, xr, ag1_s, ag1_r, rs1_s, rs1_r, ag2_s, ag2_r, rs2_s, rs2_r,
):
    bf, f32, i32 = jnp.bfloat16, jnp.float32, jnp.int32
    me = lax.axis_index("tensor")
    z, y, c = me // (Y * C), (me // C) % Y, me % C
    features = gain1.shape[1]
    half = features // 2
    blocks = slot.shape[0]

    def flat(zi, yi, ci):
        return zi * (Y * C) + yi * C + ci

    ypart = flat(z, 1 - y, c)
    cpart = flat(z, y, 1 - c)
    end = (z == 0) | (z == Z - 1)
    inner = (z > 0) & (z < Z - 1)
    zmate = z + 1 - 2 * (z % 2)
    zmid = jnp.where(z < 2, 2, 1)
    zend = jnp.where(z < 2, 3, 0)
    far = (zmid, zend)
    mate = flat(zmate, y, c)
    middle = flat(zmid, y, c)

    def local(src, dst, i):
        return pltpu.make_async_copy(src, dst, lsem.at[i])

    def remote(src, dst, ssem, rsem, peer):
        return pltpu.make_async_remote_copy(
            src_ref=src, dst_ref=dst, send_sem=ssem, recv_sem=rsem,
            device_id={"tensor": peer}, device_id_type=MESH,
        )

    def ag1_view(m, zi, yi, ci):
        if m == 0:
            return arrived.at[zi, yi * SLABS + ci]
        cols = pl.ds(pl.multiple_of(ci * half, half), half)
        return arrived.at[zi, pl.ds(yi * SLABS + 2, 3), :, cols]

    barrier = pltpu.get_barrier_semaphore()
    peers = (ypart, cpart, flat((z + 1) % Z, y, c), flat((z + 2) % Z, y, c), flat((z + 3) % Z, y, c))
    for peer in peers:
        pl.semaphore_signal(barrier, inc=1, device_id={"tensor": peer}, device_id_type=MESH)

    tables = [
        local(src, dst, 9 + k)
        for k, (src, dst) in enumerate(((owner_h, owner), (slot_h, slot), (segment_h, segment)))
    ]
    gains = [local(gain1_h, gain1, 12), local(gain2_h, gain2, 13)]
    for copy in tables:
        copy.start()
    get_query = local(queries, arrived.at[z, y * SLABS + c], 0)
    get_corpus = local(corpus, corpus_v, 1)
    get_query.start()
    get_corpus.start()
    for copy in gains:
        copy.start()
    qkv_loads = [
        local(w, wqkv_v.at[pl.ds(k * HDIM, HDIM)], 2 + k) for k, w in enumerate((wq, wk, wv))
    ]
    shared = [(wo, wo_v), (wg, wg_v), (wu, wu_v), (wd, wd_v)]
    own_loads = [local(w, v.at[0], 5 + k) for k, (w, v) in enumerate(shared)]
    give = [
        remote(w, v.at[1], xs.at[2 + k], xr.at[2 + k], cpart) for k, (w, v) in enumerate(shared)
    ]

    drains = []

    for copy in tables:
        copy.wait()
    found = jnp.int32(0)
    spots = [jnp.int32(0)] * CAP
    for b in range(blocks):
        hit = owner[0, b] == me
        row = slot[b]
        for k in range(CAP):
            spots[k] = jnp.where(hit & (found == k), row, spots[k])
        found = found + jnp.where(hit, 1, 0)
    pl.semaphore_wait(barrier, len(peers))

    order = (z, zmate, zmid, zend)

    def ag1_y(m, zi, yi):
        v, at = ag1_view(m, zi, yi, c), m * 20 + zi
        return remote(v, v, ag1_s.at[at], ag1_r.at[at], ypart)

    def ag1_c(m, zi, yi):
        v, at = ag1_view(m, zi, yi, c), m * 20 + 4 + zi * 2 + yi
        return remote(v, v, ag1_s.at[at], ag1_r.at[at], cpart)

    def ag1_c_in(m, zi, yi):
        v, at = ag1_view(m, zi, yi, 1 - c), m * 20 + 4 + zi * 2 + yi
        return remote(v, v, ag1_s.at[at], ag1_r.at[at], cpart)

    def ag1_z(m, zi, k, peer):
        v = ag1_view(m, zi, y, c)
        return remote(v, v, ag1_s.at[m * 20 + 12 + k], ag1_r.at[m * 20 + 12 + zi], peer)

    def ag1_first(m):
        ag1_z(m, z, 0, mate).start()
        pl.when(inner)(lambda: ag1_z(m, z, 1, middle).start())
        ag1_y(m, z, y).start()
        ag1_c(m, z, y).start()

    def ag1_drain():
        for m in range(2):
            ag1_z(m, z, 0, mate).wait_send()
            pl.when(inner)(lambda: ag1_z(m, z, 1, middle).wait_send())
            for zi in range(Z):
                ag1_y(m, zi, y).wait_send()
                for yi in range(Y):
                    ag1_c(m, zi, yi).wait_send()
            for i in (1, 2, 3):
                pl.when(inner)(lambda: ag1_z(m, order[i], 1 + i, mate).wait_send())

    get_query.wait()
    ag1_first(0)
    get_corpus.wait()
    mine = [corpus_v[spots[k]] for k in range(CAP)]
    for side in range(2):

        @pl.when(c == side)
        def _():
            here = slice(side * half, side * half + half)
            there = slice((1 - side) * half, (1 - side) * half + half)
            for k in range(CAP):
                xsend[k] = mine[k][:, there]
            swap = remote(xsend, xin, xs.at[0], xr.at[0], cpart)
            swap.start()
            for yi in range(Y):

                @pl.when(y == yi)
                def _():
                    for k in range(CAP):
                        arrived[z, yi * SLABS + 2 + k, side * BLK : side * BLK + BLK, here] = mine[k][:, here]

            swap.wait_recv()
            other = (1 - side) * BLK
            for yi in range(Y):

                @pl.when(y == yi)
                def _():
                    for k in range(CAP):
                        arrived[z, yi * SLABS + 2 + k, other : other + BLK, here] = xin[k]

    ag1_first(1)
    drains.append(lambda: remote(xsend, xin, xs.at[0], xr.at[0], cpart).wait_send())
    for load in qkv_loads + own_loads:
        load.start()
    for copy in give:
        copy.start()

    drains.append(lambda: [copy.wait_send() for copy in give])
    lane = lax.broadcasted_iota(i32, (8, 128), 1)
    owner_row = jnp.zeros((8, 128), i32)
    seg_row = jnp.zeros((8, 128), i32)
    for b in range(blocks):
        owner_row = jnp.where(lane == b, owner[0, b], owner_row)
        seg_row = jnp.where(lane == b, segment[b], seg_row)
    rank_row = jnp.zeros((8, 128), i32)
    for b in range(blocks):
        rank_row = rank_row + jnp.where((owner_row == owner[0, b]) & (lane > b), 1, 0)
    start_row = (
        (owner_row >> 2) * LAYER + ((owner_row >> 1) & 1) * (SLABS * 8) + 16
        + rank_row * 8 + (owner_row & 1) * BLK
    )
    start_row = jnp.where(lane < blocks, start_row, -1000).astype(f32)[:1]
    seg_row = seg_row.astype(f32)[:1]
    sub = lax.broadcasted_iota(i32, (128, 128), 0)
    lanes = lax.broadcasted_iota(i32, (128, 128), 1)
    start_col = jnp.sum(jnp.where(sub == lanes, start_row, 0.0), axis=1, keepdims=True)
    seg_col = jnp.sum(jnp.where(sub == lanes, seg_row, 0.0), axis=1, keepdims=True)

    def slot_parts(j):
        zj = step_count(j, LAYER, Z)
        rem = j - zj * LAYER
        within = rem - jnp.where(rem >= SLABS * 8, SLABS * 8, 0)
        return zj.astype(f32), within < 16, ((j >> 2) << 2).astype(f32)

    rows_all = Z * LAYER
    zj, is_query, begin = slot_parts(lax.broadcasted_iota(i32, (rows_all, 1), 0))
    held = jnp.max(jnp.where(begin == start_row, seg_row, -1.0), axis=1, keepdims=True)
    pair_col[...] = jnp.where(is_query, zj, held)
    zj, is_query, begin = slot_parts(lax.broadcasted_iota(i32, (1, rows_all), 1))
    held = jnp.max(jnp.where(begin == start_col, seg_col, -1.0), axis=0, keepdims=True)
    pair_row = jnp.where(is_query, zj, held)

    def chosen(first, count, side):
        i = lax.broadcasted_iota(i32, (count, 1), 0) + first
        turn = step_count(i, OWN, 8)
        row = OWN * (2 * turn + side) + i - OWN * turn
        from_query = (
            (row >> 5) * LAYER + ((row >> 4) & 1) * (SLABS * 8) + ((row >> 3) & 1) * 8 + (row & 7)
        )
        behind = row - Z * QLEN
        block = lax.broadcasted_iota(i32, (count, 128), 1) == (behind >> 2)
        start = jnp.sum(jnp.where(block, start_row, 0.0), axis=1, keepdims=True)
        src = jnp.where(behind < 0, from_query, start.astype(i32) + (behind & 3))
        at = lax.broadcasted_iota(i32, (count, rows_all), 1)
        return (at == src).astype(f32).astype(bf)

    for load in qkv_loads + gains:
        load.wait()

    def fold(i, carry):
        at = pl.ds(pl.multiple_of(i * 16, 16), 16)
        wqkv_v[at, :] = (wqkv_v[at, :].astype(f32) * gain1[...]).astype(bf)
        return carry

    lax.fori_loop(0, 3 * HDIM // 16, fold, 0)

    def project(layers):
        rows = jnp.concatenate([arrived[zi].reshape(LAYER, features) for zi in layers], axis=0)
        wide = rows.astype(f32)
        inverse = lax.rsqrt(jnp.mean(wide * wide, axis=1, keepdims=True) + 1e-06)
        found = (by_rows(rows, wqkv_v[...]) * inverse).astype(bf)
        for k, zi in enumerate(layers):
            qkv_v[zi] = found[k * LAYER : (k + 1) * LAYER]

    def from_z(i):
        zi = order[i]
        for m in range(2):
            ag1_z(m, zi, 0, mate).wait_recv()
            onward = middle if i == 1 else mate
            pl.when(inner)(lambda: ag1_z(m, zi, 1 + i, onward).start())
            ag1_y(m, zi, y).start()
            ag1_c(m, zi, y).start()

    def from_y(i):
        zi = order[i]
        for m in range(2):
            ag1_y(m, zi, 1 - y).wait_recv()
            ag1_c(m, zi, 1 - y).start()

    def finish(*layers):
        for i in layers:
            for m in range(2):
                for yi in range(Y):
                    ag1_c_in(m, order[i], yi).wait_recv()
        project([order[i] for i in layers])

    from_z(1)
    from_y(0)
    from_z(2)
    from_z(3)
    from_y(1)
    finish(0, 1)
    from_y(2)
    from_y(3)
    finish(2, 3)
    drains.append(ag1_drain)
    qkv = qkv_v[...].reshape(rows_all, 3 * HDIM)
    q, k, v = qkv[:, :HDIM], qkv[:, HDIM : 2 * HDIM], qkv[:, 2 * HDIM :]
    scores = by_rows(q, k) * HDIM ** (-0.5)
    scores = jnp.where(pair_col[...] == pair_row, scores, -1e30)
    weights = jnp.exp(scores - jnp.max(scores, axis=-1, keepdims=True))
    probability = (weights / jnp.sum(weights, axis=-1, keepdims=True)).astype(bf)
    context = jnp.dot(probability, v, preferred_element_type=f32).astype(bf)
    ctx_out[...] = jnp.dot(chosen(0, HALF, 1 - c), context, preferred_element_type=f32).astype(bf)
    ctx_swap = remote(ctx_out, ctx_in, xs.at[1], xr.at[1], cpart)
    ctx_swap.start()
    drains.append(ctx_swap.wait_send)
    ctx_mine = jnp.dot(chosen(0, HALF, c), context, preferred_element_type=f32).astype(bf)
    own_loads[0].wait()
    give[0].wait_recv()
    ctx_swap.wait_recv()
    ctx = jnp.concatenate([ctx_mine, ctx_in[...]], axis=1)

    def present(zi, yi):
        return (zi < Z - 1) | (yi == c)

    def compact(zi, yi):
        late = jnp.where((c == 1) & (zi == Z - 1) & (yi == 1), 1, 0)
        return jnp.minimum(zi * Y + yi - late, HALF // UNIT - 1)

    def when(cond, fn):
        if cond is None:
            fn()
        else:
            pl.when(cond)(fn)

    def both(a, b):
        return a if b is None else a & b

    class Scatter:
        def __init__(self, part, ry, s, rz, ss, rs, unit, has):
            self.part, self.ry, self.s, self.rz = part, ry, s, rz
            self.ss, self.rs, self.unit, self.has = ss, rs, unit, has

        def to_y(self, p, d):
            at = p * 12 + d
            return remote(
                self.part.at[p, self.unit(d, 1 - y)], self.ry.at[p, d],
                self.ss.at[at], self.rs.at[at], ypart,
            )

        def to_z(self, p, d, src):
            at = p * 12 + 4
            return remote(
                self.s.at[p, d], self.rz.at[p, src],
                self.ss.at[at + d], self.rs.at[at + src], flat(d, y, c),
            )

        def send_y(self, p, d):
            when(self.has(d, 1 - y), lambda: self.to_y(p, d).start())

        def mine_and_y(self, p, d):
            self.to_y(p, d).wait_recv()
            return self.part[p, self.unit(d, y)].astype(f32) + self.ry[p, d].astype(f32)

        def relay(self, p, d):
            def run():
                self.s[p, d] = self.mine_and_y(p, d).astype(bf)
                self.to_z(p, d, z).start()

            when(self.has(d, y), run)

        def own_sum(self, p):
            total = self.mine_and_y(p, z)
            for src in order[1:]:
                self.to_z(p, zmate, src).wait_recv()
                total = total + self.rz[p, src].astype(f32)
            return total

        def drain(self, pieces):
            for p in range(pieces):
                for d in range(Z):
                    when(self.has(d, 1 - y), lambda: self.to_y(p, d).wait_send())
                for d in order[1:]:
                    when(self.has(d, y), lambda: self.to_z(p, d, z).wait_send())

    turns = (zend, zmid, zmate, z)

    class Slabs(Scatter):
        def to_y(self, p, j):
            at, slabs = p * 12 + j, pl.ds(2 * j, 2 if j < Z - 1 else 1)
            return remote(
                self.part.at[p, slabs], self.ry.at[p, slabs], self.ss.at[at], self.rs.at[at], ypart
            )

        def mine_and_y(self, p, j):
            self.to_y(p, j).wait_recv()
            first, past = OWN * j // 8, -(-OWN * (j + 1) // 8)
            count = 8 * (past - first)
            i = lax.broadcasted_iota(i32, (UNIT, count), 0)
            k = lax.broadcasted_iota(i32, (UNIT, count), 1)
            pick = (i < OWN) & (k == i + OWN * j - 8 * first)
            rows = self.ry[p, first:past].reshape(count, self.ry.shape[-1])
            moved = jnp.dot(pick.astype(f32).astype(bf), rows, preferred_element_type=f32)
            return self.unit[p, j].astype(f32) + moved

        def relay(self, p, j):
            self.s[p, j] = self.mine_and_y(p, j).astype(bf)
            self.to_z(p, j, z).start()

        def to_z(self, p, j, src):
            at = p * 12 + 4
            return remote(
                self.s.at[p, j], self.rz.at[p, src],
                self.ss.at[at + j], self.rs.at[at + src], flat(turns[j], y, c),
            )

        def own_sum(self, p):
            total = self.mine_and_y(p, Z - 1)
            for src in order[1:]:
                self.to_z(p, 0, src).wait_recv()
                total = total + self.rz[p, src].astype(f32)
            return total

        def drain(self, pieces):
            for p in range(pieces):
                for j in range(Z):
                    self.to_y(p, j).wait_send()
                for j in range(Z - 1):
                    self.to_z(p, j, z).wait_send()

    one = Scatter(part1, ry1, s1, rz1, rs1_s, rs1_r, compact, present)
    width = features // P1
    wo_all = wo_v[...].reshape(2 * HDIM, features)
    for p in range(P1):
        cols = slice(p * width, (p + 1) * width)
        product = jnp.dot(ctx, wo_all[:, cols], preferred_element_type=f32)
        part1[p] = product.astype(bf).reshape(HALF // UNIT, UNIT, width)
        for d in (zend, zmid, zmate, z):
            one.send_y(p, d)

    drains.append(lambda: one.drain(P1))
    mine_at = compact(z, y)
    has_unit = present(z, y)
    rows_here = chosen(mine_at * UNIT, UNIT, c)
    for p in range(P1):
        for t in range(Z):
            for half_at in range(2):
                n = width // 2
                cols = slice(p * width + half_at * n, p * width + half_at * n + n)
                rows = arrived[t, :, :, cols].reshape(LAYER, n)
                took = jnp.dot(
                    rows_here[:, t * LAYER : (t + 1) * LAYER], rows, preferred_element_type=f32
                )
                spot = (p, slice(None), slice(half_at * n, half_at * n + n))
                resid[spot] = took if t == 0 else resid[spot] + took

    def ag2_y(p, zi, yi):
        v, at = mid.at[p, compact(zi, yi)], p * 12 + zi
        return remote(v, v, ag2_s.at[at], ag2_r.at[at], ypart)

    def ag2_z(p, zi, k, peer):
        v = mid.at[p, compact(zi, y)]
        return remote(v, v, ag2_s.at[p * 12 + 4 + k], ag2_r.at[p * 12 + 8 + zi], peer)

    def ag2_drain():
        for p in range(P1):

            @pl.when(has_unit)
            def _():
                ag2_z(p, z, 0, mate).wait_send()
                ag2_z(p, z, 1, middle).wait_send()

            for i in (2, 3):

                @pl.when(inner & present(order[i], y))
                def _():
                    ag2_z(p, order[i], i, mate).wait_send()

            for zi in range(Z):
                pl.when(present(zi, y))(lambda: ag2_y(p, zi, y).wait_send())

    def own_piece(p):
        @pl.when(has_unit)
        def _():
            mid[p, mine_at] = (resid[p] + one.own_sum(p)).astype(bf)
            ag2_z(p, z, 0, mate).start()
            ag2_z(p, z, 1, middle).start()
            ag2_y(p, z, y).start()

    def forward(p):
        for i in range(1, Z):
            zi = order[i]

            @pl.when(present(zi, y))
            def _():
                ag2_z(p, zi, 0, mate).wait_recv()
                if i > 1:
                    pl.when(inner)(lambda: ag2_z(p, zi, i, mate).start())
                ag2_y(p, zi, y).start()

    for step in range(P1 + LAG2):
        if step < P1:
            for d in (zend, zmid, zmate):
                one.relay(step, d)
        if 0 <= step - LAG1 < P1:
            own_piece(step - LAG1)
        if 0 <= step - LAG2 < P1:
            forward(step - LAG2)
    drains.append(ag2_drain)

    for k in (1, 2):
        own_loads[k].wait()
        give[k].wait_recv()
    hidden_units = wg_v.shape[1]
    squares = gate = up = None
    for p in range(P1):
        for zi in range(Z):
            when(present(zi, 1 - y), lambda: ag2_y(p, zi, 1 - y).wait_recv())
        cols = slice(p * width, (p + 1) * width)
        rows = mid[p].reshape(HALF, width).astype(f32)
        square = jnp.sum(rows * rows, axis=1, keepdims=True)
        scaled = (rows * gain2[:, cols]).astype(bf)
        g = by_rows(scaled, wg_v[:, :, cols].reshape(2 * hidden_units, width))
        u = by_rows(scaled, wu_v[:, :, cols].reshape(2 * hidden_units, width))
        squares, gate, up = (square, g, u) if p == 0 else (squares + square, gate + g, up + u)
    inverse = lax.rsqrt(squares * (1.0 / features) + 1e-06)
    hidden = (jax.nn.gelu(gate * inverse, approximate=True) * (up * inverse)).astype(bf)

    def spread(first, count):
        j = lax.broadcasted_iota(i32, (count, 1), 0) + first
        turn = j >> 4
        src = jnp.where((j & 15) < OWN, turn * OWN + (j & 15), -1)
        return (lax.broadcasted_iota(i32, (count, HALF), 1) == src).astype(f32).astype(bf)

    def turned(count, step, side):
        j = lax.broadcasted_iota(i32, (count, 1), 0)
        turn = step_count(j, step, Z)
        within = j - turn * step
        dest = jnp.where(
            turn == 0, zend, jnp.where(turn == 1, zmid, jnp.where(turn == 2, zmate, z))
        )
        src = jnp.where(within < OWN, (dest * Y + side) * OWN + within, -1)
        return (lax.broadcasted_iota(i32, (count, HALF), 1) == src).astype(f32).astype(bf)

    hidden = jnp.concatenate(
        [
            jnp.dot(turned(rows, step, side), hidden, preferred_element_type=f32).astype(bf)
            for rows, step, side in ((Z * UNIT, UNIT, y), (Z * OWN, OWN, 1 - y))
        ],
        axis=0,
    )
    own_loads[3].wait()
    give[3].wait_recv()

    two = Slabs(part2, ry2, s2, rz2, rs2_s, rs2_r, keep2, None)
    drains.append(lambda: two.drain(P2))
    width2 = features // P2
    wd_all = wd_v[...].reshape(2 * hidden_units, features)
    for p in range(P2):
        cols = slice(p * width2, (p + 1) * width2)
        product = jnp.dot(hidden, wd_all[:, cols], preferred_element_type=f32)
        product = product.astype(bf)
        keep2[p] = product[: Z * UNIT].reshape(Z, UNIT, width2)
        part2[p] = product[Z * UNIT :].reshape(Z * OWN // 8, 8, width2)
        two.to_y(p, 0).start()
    for j in range(1, Z):
        for p in range(P2):
            two.to_y(p, j).start()
    last_rows = spread((z * Y + y) * UNIT, UNIT)
    lasts = [
        jnp.dot(last_rows, mid[p].reshape(HALF, width), preferred_element_type=f32)
        for p in range(P1)
    ]
    last = jnp.concatenate(lasts, axis=1)
    for j in range(Z - 1):
        for p in range(P2):
            two.relay(p, j)
    for p in range(P2):
        cols = slice(p * width2, (p + 1) * width2)
        out_ref[:, cols] = (last[:, cols] + two.own_sum(p))[:OWN].astype(bf)

    for drain in drains:
        drain()


def fused_body(
    queries, corpus, block_owner, slot_row, segment, query_weight, key_weight, value_weight,
    out_weight, gain_attn, gain_ffn, gate_weight, up_weight, down_weight,
):
    features = queries.shape[1]
    hidden = gate_weight.shape[0]
    bf = jnp.bfloat16
    half = features // 2
    units = HALF // UNIT

    def scatter_bufs(pieces, count):
        width = features // pieces
        return [
            pltpu.VMEM((pieces, count, UNIT, width), bf),
            pltpu.VMEM((pieces, Z, UNIT, width), bf),
            pltpu.VMEM((pieces, Z, UNIT, width), bf),
            pltpu.VMEM((pieces, Z, UNIT, width), bf),
        ]

    dma = pltpu.SemaphoreType.DMA
    any_spec = pl.BlockSpec(memory_space=pl.ANY)
    vmem_spec = pl.BlockSpec(memory_space=pltpu.VMEM)
    return pl.pallas_call(
        fused_kernel,
        out_shape=jax.ShapeDtypeStruct((OWN, features), bf),
        in_specs=[any_spec] * 14,
        out_specs=vmem_spec,
        scratch_shapes=[
            pltpu.SMEM((1, block_owner.shape[0]), jnp.int32),
            pltpu.SMEM(slot_row.shape, jnp.int32),
            pltpu.SMEM(segment.shape, jnp.int32),
            pltpu.VMEM((1, features), jnp.float32),
            pltpu.VMEM((1, features), jnp.float32),
            pltpu.VMEM(corpus.shape, bf),
            pltpu.VMEM((Z, Y * SLABS, 8, features), bf),
            pltpu.VMEM((CAP, BLK, half), bf),
            pltpu.VMEM((CAP, BLK, half), bf),
            pltpu.VMEM((Z, LAYER, 3 * HDIM), bf),
            pltpu.VMEM((3 * HDIM, features), bf),
            pltpu.VMEM((2, HDIM, features), bf),
            pltpu.VMEM((2, hidden, features), bf),
            pltpu.VMEM((2, hidden, features), bf),
            pltpu.VMEM((2, hidden, features), bf),
            pltpu.VMEM((Z * LAYER, 1), jnp.float32),
            pltpu.VMEM((HALF, HDIM), bf),
            pltpu.VMEM((HALF, HDIM), bf),
            pltpu.VMEM((P1, UNIT, features // P1), jnp.float32),
            pltpu.VMEM((P1, units, UNIT, features // P1), bf),
        ]
        + scatter_bufs(P1, units)
        + [
            pltpu.VMEM((P2, Z, UNIT, features // P2), bf),
            pltpu.VMEM((P2, Z * OWN // 8, 8, features // P2), bf),
            pltpu.VMEM((P2, Z * OWN // 8, 8, features // P2), bf),
            pltpu.VMEM((P2, Z, UNIT, features // P2), bf),
            pltpu.VMEM((P2, Z, UNIT, features // P2), bf),
        ]
        + [dma((14,)), dma((6,)), dma((6,))]
        + [dma((40,))] * 2
        + [dma((12 * P1,))] * 4
        + [dma((12 * P2,))] * 2,
        compiler_params=pltpu.CompilerParams(
            collective_id=0, has_side_effects=True, vmem_limit_bytes=56 * 2**20
        ),
    )(
        queries, corpus, block_owner.reshape(1, -1), slot_row, segment, query_weight, key_weight,
        value_weight, out_weight, gate_weight, up_weight, down_weight, gain_attn[None, :], gain_ffn[None, :],
    )


def solution(mesh):
    placed = (
        P(("groups", "tensor"), None),
        P(("groups", "tensor"), None, None),
        P("groups", None),
        P("groups"),
        P("groups"),
        P("tensor", None),
        P("tensor", None),
        P("tensor", None),
        P("tensor", None),
        P(),
        P(),
        P("tensor", None),
        P("tensor", None),
        P("tensor", None),
    )
    body = fused_body if fits(mesh) else plain_body
    return jax.shard_map(
        body, mesh=mesh, in_specs=placed, out_specs=P(("groups", "tensor"), None), check_vma=False
    )
```

```python
import functools

import jax
import jax.numpy as jnp
from jax import lax
from jax.experimental import pallas as pl
from jax.experimental.pallas import tpu as pltpu
from jax.sharding import PartitionSpec as P

HDIM = 64
QLEN = 32
BLK = 4
CAP = 3


def normed(stream, gain):
    values = stream.astype(jnp.float32)
    mean_square = jnp.mean(values * values, axis=-1, keepdims=True)
    return (values * lax.rsqrt(mean_square + 1e-06) * gain).astype(jnp.bfloat16)


def by_rows(left, weight):
    return lax.dot_general(
        left, weight, (((1,), (1,)), ((), ())), preferred_element_type=jnp.float32
    )


def plain_body(
    queries,
    corpus,
    block_owner,
    slot_row,
    segment,
    query_weight,
    key_weight,
    value_weight,
    out_weight,
    gain_attn,
    gain_ffn,
    gate_weight,
    up_weight,
    down_weight,
):
    devices = lax.axis_size("tensor")
    my_index = lax.axis_index("tensor")
    owners = block_owner[:, 0]
    blocks_total = owners.shape[0]
    features = queries.shape[1]
    positions = jnp.arange(blocks_total, dtype=jnp.int32)
    earlier = (owners[:, None] == owners[None, :]) & (positions[:, None] < positions[None, :])
    slot_rank = jnp.sum(earlier.astype(jnp.int32), axis=0)
    slot_ids = jnp.arange(CAP, dtype=jnp.int32)
    choose_slot = (owners[None, :] == my_index) & (slot_rank[None, :] == slot_ids[:, None])
    local_rows = jnp.sum(jnp.where(choose_slot, slot_row[None, :], 0), axis=1)
    present = jnp.any(choose_slot, axis=1)
    outgoing = jnp.concatenate(
        [lax.dynamic_slice_in_dim(corpus, local_rows[k], 1, 0) for k in range(CAP)], axis=0
    )
    outgoing = jnp.where(present[:, None, None], outgoing, jnp.zeros_like(outgoing)).reshape(
        CAP, -1
    )
    location = owners * CAP + slot_rank
    query_all, arrived = (
        lax.all_gather(queries, "tensor", axis=0, tiled=True),
        lax.all_gather(outgoing, "tensor", axis=0, tiled=True),
    )
    slots = jnp.arange(arrived.shape[0], dtype=jnp.int32)
    chosen = (location[:, None] == slots[None, :]).astype(jnp.bfloat16)
    fetched = jnp.dot(chosen, arrived, preferred_element_type=jnp.float32).astype(jnp.bfloat16)
    stream_in = jnp.concatenate([query_all, fetched.reshape(-1, features)], axis=0)
    normal_rows = normed(stream_in, gain_attn)
    projected = tuple(
        (
            by_rows(normal_rows, weight).astype(jnp.bfloat16)
            for weight in (query_weight, key_weight, value_weight)
        )
    )
    tokens = stream_in.shape[0]
    heads_here = query_weight.shape[0] // HDIM
    query_rows_total = query_all.shape[0]
    pair_ids = jnp.concatenate(
        [jnp.arange(query_rows_total, dtype=jnp.int32) // QLEN, jnp.repeat(segment, BLK)]
    )
    same_pair = pair_ids[:, None] == pair_ids[None, :]
    query_heads = projected[0].reshape(tokens, heads_here, HDIM)
    key_heads = projected[1].reshape(tokens, heads_here, HDIM)
    value_heads = projected[2].reshape(tokens, heads_here, HDIM)
    scores = jnp.einsum(
        "qhd,khd->hqk", query_heads, key_heads, preferred_element_type=jnp.float32
    ) * HDIM ** (-0.5)
    scores = jnp.where(same_pair[None, :, :], scores, -1e30)
    row_max = jnp.max(scores, axis=-1, keepdims=True)
    weights = jnp.exp(scores - row_max)
    probability = (weights / jnp.sum(weights, axis=-1, keepdims=True)).astype(jnp.bfloat16)
    context = (
        jnp.einsum("hqk,khd->qhd", probability, value_heads, preferred_element_type=jnp.float32)
        .astype(jnp.bfloat16)
        .reshape(tokens, heads_here * HDIM)
    )
    rows_here = tokens // devices
    first_mine = my_index * rows_here
    attended = lax.psum(jnp.dot(context, out_weight, preferred_element_type=jnp.float32), "tensor")
    stream_mid = (stream_in.astype(jnp.float32) + attended).astype(jnp.bfloat16)
    normal_mid = normed(stream_mid, gain_ffn)
    mid_mine = lax.dynamic_slice_in_dim(stream_mid, first_mine, rows_here, 0)
    gate_value = by_rows(normal_mid, gate_weight)
    up_value = by_rows(normal_mid, up_weight)
    hidden = (jax.nn.gelu(gate_value, approximate=True) * up_value).astype(jnp.bfloat16)
    ffn_result = lax.psum_scatter(
        jnp.dot(hidden, down_weight, preferred_element_type=jnp.float32),
        "tensor",
        scatter_dimension=0,
        tiled=True,
    )
    return (mid_mine.astype(jnp.float32) + ffn_result).astype(jnp.bfloat16)


Z, Y, C = 4, 2, 2
UNIT = 16
OWN = 14
HALF = 112
P1 = 4
P2 = 4
LAG1 = 2
LAG2 = 4
SLABS = 5
LAYER = Y * SLABS * 8
MESH = pl.DeviceIdType.MESH


def fits(mesh):
    return mesh.shape["tensor"] == Z * Y * C


def step_count(values, step, most):
    total = jnp.zeros_like(values)
    for k in range(1, most):
        total = total + jnp.where(values >= k * step, 1, 0)
    return total


def fused_kernel(
    queries, corpus, owner_h, slot_h, segment_h, wq, wk, wv, wo, wg, wu, wd, gain1_h, gain2_h,
    out_ref,
    owner, slot, segment, gain1, gain2, corpus_v, arrived, xsend, xin, qkv_v, wqkv_v, wo_v, wg_v, wu_v, wd_v,
    pair_col, ctx_out, ctx_in, resid, mid,
    part1, ry1, s1, rz1,
    keep2, part2, ry2, s2, rz2,
    lsem, xs, xr, ag1_s, ag1_r, rs1_s, rs1_r, ag2_s, ag2_r, rs2_s, rs2_r,
):
    bf, f32, i32 = jnp.bfloat16, jnp.float32, jnp.int32
    me = lax.axis_index("tensor")
    z, y, c = me // (Y * C), (me // C) % Y, me % C
    features = gain1.shape[1]
    half = features // 2
    blocks = slot.shape[0]

    def flat(zi, yi, ci):
        return zi * (Y * C) + yi * C + ci

    ypart = flat(z, 1 - y, c)
    cpart = flat(z, y, 1 - c)
    end = (z == 0) | (z == Z - 1)
    inner = (z > 0) & (z < Z - 1)
    zmate = z + 1 - 2 * (z % 2)
    zmid = jnp.where(z < 2, 2, 1)
    zend = jnp.where(z < 2, 3, 0)
    far = (zmid, zend)
    mate = flat(zmate, y, c)
    middle = flat(zmid, y, c)

    def local(src, dst, i):
        return pltpu.make_async_copy(src, dst, lsem.at[i])

    def remote(src, dst, ssem, rsem, peer):
        return pltpu.make_async_remote_copy(
            src_ref=src, dst_ref=dst, send_sem=ssem, recv_sem=rsem,
            device_id={"tensor": peer}, device_id_type=MESH,
        )

    def ag1_view(m, zi, yi, ci):
        if m == 0:
            return arrived.at[zi, yi * SLABS + ci]
        cols = pl.ds(pl.multiple_of(ci * half, half), half)
        return arrived.at[zi, pl.ds(yi * SLABS + 2, 3), :, cols]

    barrier = pltpu.get_barrier_semaphore()
    peers = (ypart, cpart, flat((z + 1) % Z, y, c), flat((z + 2) % Z, y, c), flat((z + 3) % Z, y, c))
    for peer in peers:
        pl.semaphore_signal(barrier, inc=1, device_id={"tensor": peer}, device_id_type=MESH)

    tables = [
        local(src, dst, 9 + k)
        for k, (src, dst) in enumerate(((owner_h, owner), (slot_h, slot), (segment_h, segment)))
    ]
    gains = [local(gain1_h, gain1, 12), local(gain2_h, gain2, 13)]
    for copy in tables:
        copy.start()
    get_query = local(queries, arrived.at[z, y * SLABS + c], 0)
    get_corpus = local(corpus, corpus_v, 1)
    get_query.start()
    get_corpus.start()
    for copy in gains:
        copy.start()
    qkv_loads = [
        local(w, wqkv_v.at[pl.ds(k * HDIM, HDIM)], 2 + k) for k, w in enumerate((wq, wk, wv))
    ]
    shared = [(wo, wo_v), (wg, wg_v), (wu, wu_v), (wd, wd_v)]
    own_loads = [local(w, v.at[0], 5 + k) for k, (w, v) in enumerate(shared)]
    give = [
        remote(w, v.at[1], xs.at[2 + k], xr.at[2 + k], cpart) for k, (w, v) in enumerate(shared)
    ]

    drains = []

    for copy in tables:
        copy.wait()
    found = jnp.int32(0)
    spots = [jnp.int32(0)] * CAP
    for b in range(blocks):
        hit = owner[0, b] == me
        row = slot[b]
        for k in range(CAP):
            spots[k] = jnp.where(hit & (found == k), row, spots[k])
        found = found + jnp.where(hit, 1, 0)
    pl.semaphore_wait(barrier, len(peers))

    order = (z, zmate, zmid, zend)

    def ag1_y(m, zi, yi):
        v, at = ag1_view(m, zi, yi, c), m * 20 + zi
        return remote(v, v, ag1_s.at[at], ag1_r.at[at], ypart)

    def ag1_c(m, zi, yi):
        v, at = ag1_view(m, zi, yi, c), m * 20 + 4 + zi * 2 + yi
        return remote(v, v, ag1_s.at[at], ag1_r.at[at], cpart)

    def ag1_c_in(m, zi, yi):
        v, at = ag1_view(m, zi, yi, 1 - c), m * 20 + 4 + zi * 2 + yi
        return remote(v, v, ag1_s.at[at], ag1_r.at[at], cpart)

    def ag1_z(m, zi, k, peer):
        v = ag1_view(m, zi, y, c)
        return remote(v, v, ag1_s.at[m * 20 + 12 + k], ag1_r.at[m * 20 + 12 + zi], peer)

    def ag1_first(m):
        ag1_z(m, z, 0, mate).start()
        pl.when(inner)(lambda: ag1_z(m, z, 1, middle).start())
        ag1_y(m, z, y).start()
        ag1_c(m, z, y).start()

    def ag1_drain():
        for m in range(2):
            ag1_z(m, z, 0, mate).wait_send()
            pl.when(inner)(lambda: ag1_z(m, z, 1, middle).wait_send())
            for zi in range(Z):
                ag1_y(m, zi, y).wait_send()
                for yi in range(Y):
                    ag1_c(m, zi, yi).wait_send()
            for i in (1, 2, 3):
                pl.when(inner)(lambda: ag1_z(m, order[i], 1 + i, mate).wait_send())

    get_query.wait()
    ag1_first(0)
    get_corpus.wait()
    mine = [corpus_v[spots[k]] for k in range(CAP)]
    for side in range(2):

        @pl.when(c == side)
        def _():
            here = slice(side * half, side * half + half)
            there = slice((1 - side) * half, (1 - side) * half + half)
            for k in range(CAP):
                xsend[k] = mine[k][:, there]
            swap = remote(xsend, xin, xs.at[0], xr.at[0], cpart)
            swap.start()
            for yi in range(Y):

                @pl.when(y == yi)
                def _():
                    for k in range(CAP):
                        arrived[z, yi * SLABS + 2 + k, side * BLK : side * BLK + BLK, here] = mine[k][:, here]

            swap.wait_recv()
            other = (1 - side) * BLK
            for yi in range(Y):

                @pl.when(y == yi)
                def _():
                    for k in range(CAP):
                        arrived[z, yi * SLABS + 2 + k, other : other + BLK, here] = xin[k]

    ag1_first(1)
    drains.append(lambda: remote(xsend, xin, xs.at[0], xr.at[0], cpart).wait_send())
    for load in qkv_loads + own_loads:
        load.start()
    for copy in give:
        copy.start()

    drains.append(lambda: [copy.wait_send() for copy in give])
    lane = lax.broadcasted_iota(i32, (8, 128), 1)
    owner_row = jnp.zeros((8, 128), i32)
    seg_row = jnp.zeros((8, 128), i32)
    for b in range(blocks):
        owner_row = jnp.where(lane == b, owner[0, b], owner_row)
        seg_row = jnp.where(lane == b, segment[b], seg_row)
    rank_row = jnp.zeros((8, 128), i32)
    for b in range(blocks):
        rank_row = rank_row + jnp.where((owner_row == owner[0, b]) & (lane > b), 1, 0)
    start_row = (
        (owner_row >> 2) * LAYER + ((owner_row >> 1) & 1) * (SLABS * 8) + 16
        + rank_row * 8 + (owner_row & 1) * BLK
    )
    start_row = jnp.where(lane < blocks, start_row, -1000).astype(f32)[:1]
    seg_row = seg_row.astype(f32)[:1]
    sub = lax.broadcasted_iota(i32, (128, 128), 0)
    lanes = lax.broadcasted_iota(i32, (128, 128), 1)
    start_col = jnp.sum(jnp.where(sub == lanes, start_row, 0.0), axis=1, keepdims=True)
    seg_col = jnp.sum(jnp.where(sub == lanes, seg_row, 0.0), axis=1, keepdims=True)

    def slot_parts(j):
        zj = step_count(j, LAYER, Z)
        rem = j - zj * LAYER
        within = rem - jnp.where(rem >= SLABS * 8, SLABS * 8, 0)
        return zj.astype(f32), within < 16, ((j >> 2) << 2).astype(f32)

    rows_all = Z * LAYER
    zj, is_query, begin = slot_parts(lax.broadcasted_iota(i32, (rows_all, 1), 0))
    held = jnp.max(jnp.where(begin == start_row, seg_row, -1.0), axis=1, keepdims=True)
    pair_col[...] = jnp.where(is_query, zj, held)
    zj, is_query, begin = slot_parts(lax.broadcasted_iota(i32, (1, rows_all), 1))
    held = jnp.max(jnp.where(begin == start_col, seg_col, -1.0), axis=0, keepdims=True)
    pair_row = jnp.where(is_query, zj, held)

    def chosen(first, count, side):
        i = lax.broadcasted_iota(i32, (count, 1), 0) + first
        turn = step_count(i, OWN, 8)
        row = OWN * (2 * turn + side) + i - OWN * turn
        from_query = (
            (row >> 5) * LAYER + ((row >> 4) & 1) * (SLABS * 8) + ((row >> 3) & 1) * 8 + (row & 7)
        )
        behind = row - Z * QLEN
        block = lax.broadcasted_iota(i32, (count, 128), 1) == (behind >> 2)
        start = jnp.sum(jnp.where(block, start_row, 0.0), axis=1, keepdims=True)
        src = jnp.where(behind < 0, from_query, start.astype(i32) + (behind & 3))
        at = lax.broadcasted_iota(i32, (count, rows_all), 1)
        return (at == src).astype(f32).astype(bf)

    for load in qkv_loads + gains:
        load.wait()

    def fold(i, carry):
        at = pl.ds(pl.multiple_of(i * 16, 16), 16)
        wqkv_v[at, :] = (wqkv_v[at, :].astype(f32) * gain1[...]).astype(bf)
        return carry

    lax.fori_loop(0, 3 * HDIM // 16, fold, 0)

    def project(layers):
        rows = jnp.concatenate([arrived[zi].reshape(LAYER, features) for zi in layers], axis=0)
        wide = rows.astype(f32)
        inverse = lax.rsqrt(jnp.mean(wide * wide, axis=1, keepdims=True) + 1e-06)
        found = (by_rows(rows, wqkv_v[...]) * inverse).astype(bf)
        for k, zi in enumerate(layers):
            qkv_v[zi] = found[k * LAYER : (k + 1) * LAYER]

    def from_z(i):
        zi = order[i]
        for m in range(2):
            ag1_z(m, zi, 0, mate).wait_recv()
            onward = middle if i == 1 else mate
            pl.when(inner)(lambda: ag1_z(m, zi, 1 + i, onward).start())
            ag1_y(m, zi, y).start()
            ag1_c(m, zi, y).start()

    def from_y(i):
        zi = order[i]
        for m in range(2):
            ag1_y(m, zi, 1 - y).wait_recv()
            ag1_c(m, zi, 1 - y).start()

    def finish(*layers):
        for i in layers:
            for m in range(2):
                for yi in range(Y):
                    ag1_c_in(m, order[i], yi).wait_recv()
        project([order[i] for i in layers])

    from_z(1)
    from_y(0)
    from_z(2)
    from_z(3)
    from_y(1)
    finish(0, 1)
    from_y(2)
    from_y(3)
    finish(2, 3)
    drains.append(ag1_drain)
    qkv = qkv_v[...].reshape(rows_all, 3 * HDIM)
    q, k, v = qkv[:, :HDIM], qkv[:, HDIM : 2 * HDIM], qkv[:, 2 * HDIM :]
    scores = by_rows(q, k) * HDIM ** (-0.5)
    scores = jnp.where(pair_col[...] == pair_row, scores, -1e30)
    weights = jnp.exp(scores - jnp.max(scores, axis=-1, keepdims=True))
    probability = (weights / jnp.sum(weights, axis=-1, keepdims=True)).astype(bf)
    context = jnp.dot(probability, v, preferred_element_type=f32).astype(bf)
    ctx_out[...] = jnp.dot(chosen(0, HALF, 1 - c), context, preferred_element_type=f32).astype(bf)
    ctx_swap = remote(ctx_out, ctx_in, xs.at[1], xr.at[1], cpart)
    ctx_swap.start()
    drains.append(ctx_swap.wait_send)
    ctx_mine = jnp.dot(chosen(0, HALF, c), context, preferred_element_type=f32).astype(bf)
    own_loads[0].wait()
    give[0].wait_recv()
    ctx_swap.wait_recv()
    ctx = jnp.concatenate([ctx_mine, ctx_in[...]], axis=1)

    def present(zi, yi):
        return (zi < Z - 1) | (yi == c)

    def compact(zi, yi):
        late = jnp.where((c == 1) & (zi == Z - 1) & (yi == 1), 1, 0)
        return jnp.minimum(zi * Y + yi - late, HALF // UNIT - 1)

    def when(cond, fn):
        if cond is None:
            fn()
        else:
            pl.when(cond)(fn)

    def both(a, b):
        return a if b is None else a & b

    class Scatter:
        def __init__(self, part, ry, s, rz, ss, rs, unit, has):
            self.part, self.ry, self.s, self.rz = part, ry, s, rz
            self.ss, self.rs, self.unit, self.has = ss, rs, unit, has

        def to_y(self, p, d):
            at = p * 12 + d
            return remote(
                self.part.at[p, self.unit(d, 1 - y)], self.ry.at[p, d],
                self.ss.at[at], self.rs.at[at], ypart,
            )

        def to_z(self, p, d, src):
            at = p * 12 + 4
            return remote(
                self.s.at[p, d], self.rz.at[p, src],
                self.ss.at[at + d], self.rs.at[at + src], flat(d, y, c),
            )

        def send_y(self, p, d):
            when(self.has(d, 1 - y), lambda: self.to_y(p, d).start())

        def mine_and_y(self, p, d):
            self.to_y(p, d).wait_recv()
            return self.part[p, self.unit(d, y)].astype(f32) + self.ry[p, d].astype(f32)

        def relay(self, p, d):
            def run():
                self.s[p, d] = self.mine_and_y(p, d).astype(bf)
                self.to_z(p, d, z).start()

            when(self.has(d, y), run)

        def own_sum(self, p):
            total = self.mine_and_y(p, z)
            for src in order[1:]:
                self.to_z(p, zmate, src).wait_recv()
                total = total + self.rz[p, src].astype(f32)
            return total

        def drain(self, pieces):
            for p in range(pieces):
                for d in range(Z):
                    when(self.has(d, 1 - y), lambda: self.to_y(p, d).wait_send())
                for d in order[1:]:
                    when(self.has(d, y), lambda: self.to_z(p, d, z).wait_send())

    turns = (zend, zmid, zmate, z)

    class Slabs(Scatter):
        def to_y(self, p, j):
            at, slabs = p * 12 + j, pl.ds(2 * j, 2 if j < Z - 1 else 1)
            return remote(
                self.part.at[p, slabs], self.ry.at[p, slabs], self.ss.at[at], self.rs.at[at], ypart
            )

        def mine_and_y(self, p, j):
            self.to_y(p, j).wait_recv()
            first, past = OWN * j // 8, -(-OWN * (j + 1) // 8)
            count = 8 * (past - first)
            i = lax.broadcasted_iota(i32, (UNIT, count), 0)
            k = lax.broadcasted_iota(i32, (UNIT, count), 1)
            pick = (i < OWN) & (k == i + OWN * j - 8 * first)
            rows = self.ry[p, first:past].reshape(count, self.ry.shape[-1])
            moved = jnp.dot(pick.astype(f32).astype(bf), rows, preferred_element_type=f32)
            return self.unit[p, j].astype(f32) + moved

        def relay(self, p, j):
            self.s[p, j] = self.mine_and_y(p, j).astype(bf)
            self.to_z(p, j, z).start()

        def to_z(self, p, j, src):
            at = p * 12 + 4
            return remote(
                self.s.at[p, j], self.rz.at[p, src],
                self.ss.at[at + j], self.rs.at[at + src], flat(turns[j], y, c),
            )

        def own_sum(self, p):
            total = self.mine_and_y(p, Z - 1)
            for src in order[1:]:
                self.to_z(p, 0, src).wait_recv()
                total = total + self.rz[p, src].astype(f32)
            return total

        def drain(self, pieces):
            for p in range(pieces):
                for j in range(Z):
                    self.to_y(p, j).wait_send()
                for j in range(Z - 1):
                    self.to_z(p, j, z).wait_send()

    one = Scatter(part1, ry1, s1, rz1, rs1_s, rs1_r, compact, present)
    width = features // P1
    wo_all = wo_v[...].reshape(2 * HDIM, features)
    for p in range(P1):
        cols = slice(p * width, (p + 1) * width)
        product = jnp.dot(ctx, wo_all[:, cols], preferred_element_type=f32)
        part1[p] = product.astype(bf).reshape(HALF // UNIT, UNIT, width)
        for d in (zend, zmid, zmate, z):
            one.send_y(p, d)

    drains.append(lambda: one.drain(P1))
    mine_at = compact(z, y)
    has_unit = present(z, y)
    rows_here = chosen(mine_at * UNIT, UNIT, c)
    for p in range(P1):
        for t in range(Z):
            for half_at in range(2):
                n = width // 2
                cols = slice(p * width + half_at * n, p * width + half_at * n + n)
                rows = arrived[t, :, :, cols].reshape(LAYER, n)
                took = jnp.dot(
                    rows_here[:, t * LAYER : (t + 1) * LAYER], rows, preferred_element_type=f32
                )
                spot = (p, slice(None), slice(half_at * n, half_at * n + n))
                resid[spot] = took if t == 0 else resid[spot] + took

    def ag2_y(p, zi, yi):
        v, at = mid.at[p, compact(zi, yi)], p * 12 + zi
        return remote(v, v, ag2_s.at[at], ag2_r.at[at], ypart)

    def ag2_z(p, zi, k, peer):
        v = mid.at[p, compact(zi, y)]
        return remote(v, v, ag2_s.at[p * 12 + 4 + k], ag2_r.at[p * 12 + 8 + zi], peer)

    def ag2_drain():
        for p in range(P1):

            @pl.when(has_unit)
            def _():
                ag2_z(p, z, 0, mate).wait_send()
                ag2_z(p, z, 1, middle).wait_send()

            for i in (2, 3):

                @pl.when(inner & present(order[i], y))
                def _():
                    ag2_z(p, order[i], i, mate).wait_send()

            for zi in range(Z):
                pl.when(present(zi, y))(lambda: ag2_y(p, zi, y).wait_send())

    def own_piece(p):
        @pl.when(has_unit)
        def _():
            mid[p, mine_at] = (resid[p] + one.own_sum(p)).astype(bf)
            ag2_z(p, z, 0, mate).start()
            ag2_z(p, z, 1, middle).start()
            ag2_y(p, z, y).start()

    def forward(p):
        for i in range(1, Z):
            zi = order[i]

            @pl.when(present(zi, y))
            def _():
                ag2_z(p, zi, 0, mate).wait_recv()
                if i > 1:
                    pl.when(inner)(lambda: ag2_z(p, zi, i, mate).start())
                ag2_y(p, zi, y).start()

    for step in range(P1 + LAG2):
        if step < P1:
            for d in (zend, zmid, zmate):
                one.relay(step, d)
        if 0 <= step - LAG1 < P1:
            own_piece(step - LAG1)
        if 0 <= step - LAG2 < P1:
            forward(step - LAG2)
    drains.append(ag2_drain)

    for k in (1, 2):
        own_loads[k].wait()
        give[k].wait_recv()
    hidden_units = wg_v.shape[1]
    squares = gate = up = None
    for p in range(P1):
        for zi in range(Z):
            when(present(zi, 1 - y), lambda: ag2_y(p, zi, 1 - y).wait_recv())
        cols = slice(p * width, (p + 1) * width)
        rows = mid[p].reshape(HALF, width).astype(f32)
        square = jnp.sum(rows * rows, axis=1, keepdims=True)
        scaled = (rows * gain2[:, cols]).astype(bf)
        g = by_rows(scaled, wg_v[:, :, cols].reshape(2 * hidden_units, width))
        u = by_rows(scaled, wu_v[:, :, cols].reshape(2 * hidden_units, width))
        squares, gate, up = (square, g, u) if p == 0 else (squares + square, gate + g, up + u)
    inverse = lax.rsqrt(squares * (1.0 / features) + 1e-06)
    hidden = (jax.nn.gelu(gate * inverse, approximate=True) * (up * inverse)).astype(bf)

    def spread(first, count):
        j = lax.broadcasted_iota(i32, (count, 1), 0) + first
        turn = j >> 4
        src = jnp.where((j & 15) < OWN, turn * OWN + (j & 15), -1)
        return (lax.broadcasted_iota(i32, (count, HALF), 1) == src).astype(f32).astype(bf)

    def turned(count, step, side):
        j = lax.broadcasted_iota(i32, (count, 1), 0)
        turn = step_count(j, step, Z)
        within = j - turn * step
        dest = jnp.where(
            turn == 0, zend, jnp.where(turn == 1, zmid, jnp.where(turn == 2, zmate, z))
        )
        src = jnp.where(within < OWN, (dest * Y + side) * OWN + within, -1)
        return (lax.broadcasted_iota(i32, (count, HALF), 1) == src).astype(f32).astype(bf)

    hidden = jnp.concatenate(
        [
            jnp.dot(turned(rows, step, side), hidden, preferred_element_type=f32).astype(bf)
            for rows, step, side in ((Z * UNIT, UNIT, y), (Z * OWN, OWN, 1 - y))
        ],
        axis=0,
    )
    own_loads[3].wait()
    give[3].wait_recv()

    two = Slabs(part2, ry2, s2, rz2, rs2_s, rs2_r, keep2, None)
    drains.append(lambda: two.drain(P2))
    width2 = features // P2
    wd_all = wd_v[...].reshape(2 * hidden_units, features)
    for p in range(P2):
        cols = slice(p * width2, (p + 1) * width2)
        product = jnp.dot(hidden, wd_all[:, cols], preferred_element_type=f32)
        product = product.astype(bf)
        keep2[p] = product[: Z * UNIT].reshape(Z, UNIT, width2)
        part2[p] = product[Z * UNIT :].reshape(Z * OWN // 8, 8, width2)
        two.to_y(p, 0).start()
    for j in range(1, Z):
        for p in range(P2):
            two.to_y(p, j).start()
    last_rows = spread((z * Y + y) * UNIT, UNIT)
    lasts = [
        jnp.dot(last_rows, mid[p].reshape(HALF, width), preferred_element_type=f32)
        for p in range(P1)
    ]
    last = jnp.concatenate(lasts, axis=1)
    for j in range(Z - 1):
        for p in range(P2):
            two.relay(p, j)
    for p in range(P2):
        cols = slice(p * width2, (p + 1) * width2)
        out_ref[:, cols] = (last[:, cols] + two.own_sum(p))[:OWN].astype(bf)

    for drain in drains:
        drain()


def fused_body(
    queries, corpus, block_owner, slot_row, segment, query_weight, key_weight, value_weight,
    out_weight, gain_attn, gain_ffn, gate_weight, up_weight, down_weight,
):
    features = queries.shape[1]
    hidden = gate_weight.shape[0]
    bf = jnp.bfloat16
    half = features // 2
    units = HALF // UNIT

    def scatter_bufs(pieces, count):
        width = features // pieces
        return [
            pltpu.VMEM((pieces, count, UNIT, width), bf),
            pltpu.VMEM((pieces, Z, UNIT, width), bf),
            pltpu.VMEM((pieces, Z, UNIT, width), bf),
            pltpu.VMEM((pieces, Z, UNIT, width), bf),
        ]

    dma = pltpu.SemaphoreType.DMA
    any_spec = pl.BlockSpec(memory_space=pl.ANY)
    vmem_spec = pl.BlockSpec(memory_space=pltpu.VMEM)
    return pl.pallas_call(
        fused_kernel,
        out_shape=jax.ShapeDtypeStruct((OWN, features), bf),
        in_specs=[any_spec] * 14,
        out_specs=vmem_spec,
        scratch_shapes=[
            pltpu.SMEM((1, block_owner.shape[0]), jnp.int32),
            pltpu.SMEM(slot_row.shape, jnp.int32),
            pltpu.SMEM(segment.shape, jnp.int32),
            pltpu.VMEM((1, features), jnp.float32),
            pltpu.VMEM((1, features), jnp.float32),
            pltpu.VMEM(corpus.shape, bf),
            pltpu.VMEM((Z, Y * SLABS, 8, features), bf),
            pltpu.VMEM((CAP, BLK, half), bf),
            pltpu.VMEM((CAP, BLK, half), bf),
            pltpu.VMEM((Z, LAYER, 3 * HDIM), bf),
            pltpu.VMEM((3 * HDIM, features), bf),
            pltpu.VMEM((2, HDIM, features), bf),
            pltpu.VMEM((2, hidden, features), bf),
            pltpu.VMEM((2, hidden, features), bf),
            pltpu.VMEM((2, hidden, features), bf),
            pltpu.VMEM((Z * LAYER, 1), jnp.float32),
            pltpu.VMEM((HALF, HDIM), bf),
            pltpu.VMEM((HALF, HDIM), bf),
            pltpu.VMEM((P1, UNIT, features // P1), jnp.float32),
            pltpu.VMEM((P1, units, UNIT, features // P1), bf),
        ]
        + scatter_bufs(P1, units)
        + [
            pltpu.VMEM((P2, Z, UNIT, features // P2), bf),
            pltpu.VMEM((P2, Z * OWN // 8, 8, features // P2), bf),
            pltpu.VMEM((P2, Z * OWN // 8, 8, features // P2), bf),
            pltpu.VMEM((P2, Z, UNIT, features // P2), bf),
            pltpu.VMEM((P2, Z, UNIT, features // P2), bf),
        ]
        + [dma((14,)), dma((6,)), dma((6,))]
        + [dma((40,))] * 2
        + [dma((12 * P1,))] * 4
        + [dma((12 * P2,))] * 2,
        compiler_params=pltpu.CompilerParams(
            collective_id=0, has_side_effects=True, vmem_limit_bytes=56 * 2**20
        ),
    )(
        queries, corpus, block_owner.reshape(1, -1), slot_row, segment, query_weight, key_weight,
        value_weight, out_weight, gate_weight, up_weight, down_weight, gain_attn[None, :], gain_ffn[None, :],
    )


def solution(mesh):
    placed = (
        P(("groups", "tensor"), None),
        P(("groups", "tensor"), None, None),
        P("groups", None),
        P("groups"),
        P("groups"),
        P("tensor", None),
        P("tensor", None),
        P("tensor", None),
        P("tensor", None),
        P(),
        P(),
        P("tensor", None),
        P("tensor", None),
        P("tensor", None),
    )
    body = fused_body if fits(mesh) else plain_body
    return jax.shard_map(
        body, mesh=mesh, in_specs=placed, out_specs=P(("groups", "tensor"), None), check_vma=False
    )
```

```python
import functools

import jax
import jax.numpy as jnp
from jax import lax
from jax.experimental import pallas as pl
from jax.experimental.pallas import tpu as pltpu
from jax.sharding import PartitionSpec as P

HDIM = 64
QLEN = 32
BLK = 4
CAP = 3


def normed(stream, gain):
    values = stream.astype(jnp.float32)
    mean_square = jnp.mean(values * values, axis=-1, keepdims=True)
    return (values * lax.rsqrt(mean_square + 1e-06) * gain).astype(jnp.bfloat16)


def by_rows(left, weight):
    return lax.dot_general(
        left, weight, (((1,), (1,)), ((), ())), preferred_element_type=jnp.float32
    )


def plain_body(
    queries,
    corpus,
    block_owner,
    slot_row,
    segment,
    query_weight,
    key_weight,
    value_weight,
    out_weight,
    gain_attn,
    gain_ffn,
    gate_weight,
    up_weight,
    down_weight,
):
    devices = lax.axis_size("tensor")
    my_index = lax.axis_index("tensor")
    owners = block_owner[:, 0]
    blocks_total = owners.shape[0]
    features = queries.shape[1]
    positions = jnp.arange(blocks_total, dtype=jnp.int32)
    earlier = (owners[:, None] == owners[None, :]) & (positions[:, None] < positions[None, :])
    slot_rank = jnp.sum(earlier.astype(jnp.int32), axis=0)
    slot_ids = jnp.arange(CAP, dtype=jnp.int32)
    choose_slot = (owners[None, :] == my_index) & (slot_rank[None, :] == slot_ids[:, None])
    local_rows = jnp.sum(jnp.where(choose_slot, slot_row[None, :], 0), axis=1)
    present = jnp.any(choose_slot, axis=1)
    outgoing = jnp.concatenate(
        [lax.dynamic_slice_in_dim(corpus, local_rows[k], 1, 0) for k in range(CAP)], axis=0
    )
    outgoing = jnp.where(present[:, None, None], outgoing, jnp.zeros_like(outgoing)).reshape(
        CAP, -1
    )
    location = owners * CAP + slot_rank
    query_all, arrived = (
        lax.all_gather(queries, "tensor", axis=0, tiled=True),
        lax.all_gather(outgoing, "tensor", axis=0, tiled=True),
    )
    slots = jnp.arange(arrived.shape[0], dtype=jnp.int32)
    chosen = (location[:, None] == slots[None, :]).astype(jnp.bfloat16)
    fetched = jnp.dot(chosen, arrived, preferred_element_type=jnp.float32).astype(jnp.bfloat16)
    stream_in = jnp.concatenate([query_all, fetched.reshape(-1, features)], axis=0)
    normal_rows = normed(stream_in, gain_attn)
    projected = tuple(
        (
            by_rows(normal_rows, weight).astype(jnp.bfloat16)
            for weight in (query_weight, key_weight, value_weight)
        )
    )
    tokens = stream_in.shape[0]
    heads_here = query_weight.shape[0] // HDIM
    query_rows_total = query_all.shape[0]
    pair_ids = jnp.concatenate(
        [jnp.arange(query_rows_total, dtype=jnp.int32) // QLEN, jnp.repeat(segment, BLK)]
    )
    same_pair = pair_ids[:, None] == pair_ids[None, :]
    query_heads = projected[0].reshape(tokens, heads_here, HDIM)
    key_heads = projected[1].reshape(tokens, heads_here, HDIM)
    value_heads = projected[2].reshape(tokens, heads_here, HDIM)
    scores = jnp.einsum(
        "qhd,khd->hqk", query_heads, key_heads, preferred_element_type=jnp.float32
    ) * HDIM ** (-0.5)
    scores = jnp.where(same_pair[None, :, :], scores, -1e30)
    row_max = jnp.max(scores, axis=-1, keepdims=True)
    weights = jnp.exp(scores - row_max)
    probability = (weights / jnp.sum(weights, axis=-1, keepdims=True)).astype(jnp.bfloat16)
    context = (
        jnp.einsum("hqk,khd->qhd", probability, value_heads, preferred_element_type=jnp.float32)
        .astype(jnp.bfloat16)
        .reshape(tokens, heads_here * HDIM)
    )
    rows_here = tokens // devices
    first_mine = my_index * rows_here
    attended = lax.psum(jnp.dot(context, out_weight, preferred_element_type=jnp.float32), "tensor")
    stream_mid = (stream_in.astype(jnp.float32) + attended).astype(jnp.bfloat16)
    normal_mid = normed(stream_mid, gain_ffn)
    mid_mine = lax.dynamic_slice_in_dim(stream_mid, first_mine, rows_here, 0)
    gate_value = by_rows(normal_mid, gate_weight)
    up_value = by_rows(normal_mid, up_weight)
    hidden = (jax.nn.gelu(gate_value, approximate=True) * up_value).astype(jnp.bfloat16)
    ffn_result = lax.psum_scatter(
        jnp.dot(hidden, down_weight, preferred_element_type=jnp.float32),
        "tensor",
        scatter_dimension=0,
        tiled=True,
    )
    return (mid_mine.astype(jnp.float32) + ffn_result).astype(jnp.bfloat16)


Z, Y, C = 4, 2, 2
UNIT = 16
OWN = 14
HALF = 112
P1 = 4
P2 = 4
LAG1 = 3
LAG2 = 5
SLABS = 5
LAYER = Y * SLABS * 8
MESH = pl.DeviceIdType.MESH


def fits(mesh):
    return mesh.shape["tensor"] == Z * Y * C


def step_count(values, step, most):
    total = jnp.zeros_like(values)
    for k in range(1, most):
        total = total + jnp.where(values >= k * step, 1, 0)
    return total


def fused_kernel(
    queries, corpus, owner_h, slot_h, segment_h, wq, wk, wv, wo, wg, wu, wd, gain1_h, gain2_h,
    out_ref,
    owner, slot, segment, gain1, gain2, corpus_v, arrived, xsend, xin, qkv_v, wqkv_v, wo_v, wg_v, wu_v, wd_v,
    pair_col, ctx_out, ctx_in, resid, mid,
    part1, ry1, s1, rz1,
    keep2, part2, ry2, s2, rz2,
    lsem, xs, xr, ag1_s, ag1_r, rs1_s, rs1_r, ag2_s, ag2_r, rs2_s, rs2_r,
):
    bf, f32, i32 = jnp.bfloat16, jnp.float32, jnp.int32
    me = lax.axis_index("tensor")
    z, y, c = me // (Y * C), (me // C) % Y, me % C
    features = gain1.shape[1]
    half = features // 2
    blocks = slot.shape[0]

    def flat(zi, yi, ci):
        return zi * (Y * C) + yi * C + ci

    ypart = flat(z, 1 - y, c)
    cpart = flat(z, y, 1 - c)
    end = (z == 0) | (z == Z - 1)
    inner = (z > 0) & (z < Z - 1)
    zmate = z + 1 - 2 * (z % 2)
    zmid = jnp.where(z < 2, 2, 1)
    zend = jnp.where(z < 2, 3, 0)
    far = (zmid, zend)
    mate = flat(zmate, y, c)
    middle = flat(zmid, y, c)

    def local(src, dst, i):
        return pltpu.make_async_copy(src, dst, lsem.at[i])

    def remote(src, dst, ssem, rsem, peer):
        return pltpu.make_async_remote_copy(
            src_ref=src, dst_ref=dst, send_sem=ssem, recv_sem=rsem,
            device_id={"tensor": peer}, device_id_type=MESH,
        )

    def ag1_view(m, zi, yi, ci):
        if m == 0:
            return arrived.at[zi, yi * SLABS + ci]
        cols = pl.ds(pl.multiple_of(ci * half, half), half)
        return arrived.at[zi, pl.ds(yi * SLABS + 2, 3), :, cols]

    barrier = pltpu.get_barrier_semaphore()
    peers = (ypart, cpart, flat((z + 1) % Z, y, c), flat((z + 2) % Z, y, c), flat((z + 3) % Z, y, c))
    for peer in peers:
        pl.semaphore_signal(barrier, inc=1, device_id={"tensor": peer}, device_id_type=MESH)

    tables = [
        local(src, dst, 9 + k)
        for k, (src, dst) in enumerate(((owner_h, owner), (slot_h, slot), (segment_h, segment)))
    ]
    gains = [local(gain1_h, gain1, 12), local(gain2_h, gain2, 13)]
    for copy in tables:
        copy.start()
    get_query = local(queries, arrived.at[z, y * SLABS + c], 0)
    get_corpus = local(corpus, corpus_v, 1)
    get_query.start()
    get_corpus.start()
    for copy in gains:
        copy.start()
    qkv_loads = [
        local(w, wqkv_v.at[pl.ds(k * HDIM, HDIM)], 2 + k) for k, w in enumerate((wq, wk, wv))
    ]
    shared = [(wo, wo_v), (wg, wg_v), (wu, wu_v), (wd, wd_v)]
    own_loads = [local(w, v.at[0], 5 + k) for k, (w, v) in enumerate(shared)]
    give = [
        remote(w, v.at[1], xs.at[2 + k], xr.at[2 + k], cpart) for k, (w, v) in enumerate(shared)
    ]

    drains = []

    for copy in tables:
        copy.wait()
    found = jnp.int32(0)
    spots = [jnp.int32(0)] * CAP
    for b in range(blocks):
        hit = owner[0, b] == me
        row = slot[b]
        for k in range(CAP):
            spots[k] = jnp.where(hit & (found == k), row, spots[k])
        found = found + jnp.where(hit, 1, 0)
    pl.semaphore_wait(barrier, len(peers))

    order = (z, zmate, zmid, zend)

    def ag1_y(m, zi, yi):
        v, at = ag1_view(m, zi, yi, c), m * 20 + zi
        return remote(v, v, ag1_s.at[at], ag1_r.at[at], ypart)

    def ag1_c(m, zi, yi):
        v, at = ag1_view(m, zi, yi, c), m * 20 + 4 + zi * 2 + yi
        return remote(v, v, ag1_s.at[at], ag1_r.at[at], cpart)

    def ag1_c_in(m, zi, yi):
        v, at = ag1_view(m, zi, yi, 1 - c), m * 20 + 4 + zi * 2 + yi
        return remote(v, v, ag1_s.at[at], ag1_r.at[at], cpart)

    def ag1_z(m, zi, k, peer):
        v = ag1_view(m, zi, y, c)
        return remote(v, v, ag1_s.at[m * 20 + 12 + k], ag1_r.at[m * 20 + 12 + zi], peer)

    def ag1_first(m):
        ag1_z(m, z, 0, mate).start()
        pl.when(inner)(lambda: ag1_z(m, z, 1, middle).start())
        ag1_y(m, z, y).start()
        ag1_c(m, z, y).start()

    def ag1_drain():
        for m in range(2):
            ag1_z(m, z, 0, mate).wait_send()
            pl.when(inner)(lambda: ag1_z(m, z, 1, middle).wait_send())
            for zi in range(Z):
                ag1_y(m, zi, y).wait_send()
                for yi in range(Y):
                    ag1_c(m, zi, yi).wait_send()
            for i in (1, 2, 3):
                pl.when(inner)(lambda: ag1_z(m, order[i], 1 + i, mate).wait_send())

    get_query.wait()
    ag1_first(0)
    get_corpus.wait()
    mine = [corpus_v[spots[k]] for k in range(CAP)]
    for side in range(2):

        @pl.when(c == side)
        def _():
            here = slice(side * half, side * half + half)
            there = slice((1 - side) * half, (1 - side) * half + half)
            for k in range(CAP):
                xsend[k] = mine[k][:, there]
            swap = remote(xsend, xin, xs.at[0], xr.at[0], cpart)
            swap.start()
            for yi in range(Y):

                @pl.when(y == yi)
                def _():
                    for k in range(CAP):
                        arrived[z, yi * SLABS + 2 + k, side * BLK : side * BLK + BLK, here] = mine[k][:, here]

            swap.wait_recv()
            other = (1 - side) * BLK
            for yi in range(Y):

                @pl.when(y == yi)
                def _():
                    for k in range(CAP):
                        arrived[z, yi * SLABS + 2 + k, other : other + BLK, here] = xin[k]

    ag1_first(1)
    drains.append(lambda: remote(xsend, xin, xs.at[0], xr.at[0], cpart).wait_send())
    for load in qkv_loads + own_loads:
        load.start()
    for copy in give:
        copy.start()

    drains.append(lambda: [copy.wait_send() for copy in give])
    lane = lax.broadcasted_iota(i32, (8, 128), 1)
    owner_row = jnp.zeros((8, 128), i32)
    seg_row = jnp.zeros((8, 128), i32)
    for b in range(blocks):
        owner_row = jnp.where(lane == b, owner[0, b], owner_row)
        seg_row = jnp.where(lane == b, segment[b], seg_row)
    rank_row = jnp.zeros((8, 128), i32)
    for b in range(blocks):
        rank_row = rank_row + jnp.where((owner_row == owner[0, b]) & (lane > b), 1, 0)
    start_row = (
        (owner_row >> 2) * LAYER + ((owner_row >> 1) & 1) * (SLABS * 8) + 16
        + rank_row * 8 + (owner_row & 1) * BLK
    )
    start_row = jnp.where(lane < blocks, start_row, -1000).astype(f32)[:1]
    seg_row = seg_row.astype(f32)[:1]
    sub = lax.broadcasted_iota(i32, (128, 128), 0)
    lanes = lax.broadcasted_iota(i32, (128, 128), 1)
    start_col = jnp.sum(jnp.where(sub == lanes, start_row, 0.0), axis=1, keepdims=True)
    seg_col = jnp.sum(jnp.where(sub == lanes, seg_row, 0.0), axis=1, keepdims=True)

    def slot_parts(j):
        zj = step_count(j, LAYER, Z)
        rem = j - zj * LAYER
        within = rem - jnp.where(rem >= SLABS * 8, SLABS * 8, 0)
        return zj.astype(f32), within < 16, ((j >> 2) << 2).astype(f32)

    rows_all = Z * LAYER
    zj, is_query, begin = slot_parts(lax.broadcasted_iota(i32, (rows_all, 1), 0))
    held = jnp.max(jnp.where(begin == start_row, seg_row, -1.0), axis=1, keepdims=True)
    pair_col[...] = jnp.where(is_query, zj, held)
    zj, is_query, begin = slot_parts(lax.broadcasted_iota(i32, (1, rows_all), 1))
    held = jnp.max(jnp.where(begin == start_col, seg_col, -1.0), axis=0, keepdims=True)
    pair_row = jnp.where(is_query, zj, held)

    def chosen(first, count, side):
        i = lax.broadcasted_iota(i32, (count, 1), 0) + first
        turn = step_count(i, OWN, 8)
        row = OWN * (2 * turn + side) + i - OWN * turn
        from_query = (
            (row >> 5) * LAYER + ((row >> 4) & 1) * (SLABS * 8) + ((row >> 3) & 1) * 8 + (row & 7)
        )
        behind = row - Z * QLEN
        block = lax.broadcasted_iota(i32, (count, 128), 1) == (behind >> 2)
        start = jnp.sum(jnp.where(block, start_row, 0.0), axis=1, keepdims=True)
        src = jnp.where(behind < 0, from_query, start.astype(i32) + (behind & 3))
        at = lax.broadcasted_iota(i32, (count, rows_all), 1)
        return (at == src).astype(f32).astype(bf)

    for load in qkv_loads + gains:
        load.wait()

    def fold(i, carry):
        at = pl.ds(pl.multiple_of(i * 16, 16), 16)
        wqkv_v[at, :] = (wqkv_v[at, :].astype(f32) * gain1[...]).astype(bf)
        return carry

    lax.fori_loop(0, 3 * HDIM // 16, fold, 0)

    def project(layers):
        rows = jnp.concatenate([arrived[zi].reshape(LAYER, features) for zi in layers], axis=0)
        wide = rows.astype(f32)
        inverse = lax.rsqrt(jnp.mean(wide * wide, axis=1, keepdims=True) + 1e-06)
        found = (by_rows(rows, wqkv_v[...]) * inverse).astype(bf)
        for k, zi in enumerate(layers):
            qkv_v[zi] = found[k * LAYER : (k + 1) * LAYER]

    def from_z(i):
        zi = order[i]
        for m in range(2):
            ag1_z(m, zi, 0, mate).wait_recv()
            onward = middle if i == 1 else mate
            pl.when(inner)(lambda: ag1_z(m, zi, 1 + i, onward).start())
            ag1_y(m, zi, y).start()
            ag1_c(m, zi, y).start()

    def from_y(i):
        zi = order[i]
        for m in range(2):
            ag1_y(m, zi, 1 - y).wait_recv()
            ag1_c(m, zi, 1 - y).start()

    def finish(*layers):
        for i in layers:
            for m in range(2):
                for yi in range(Y):
                    ag1_c_in(m, order[i], yi).wait_recv()
        project([order[i] for i in layers])

    from_z(1)
    from_y(0)
    from_z(2)
    from_z(3)
    from_y(1)
    finish(0, 1)
    from_y(2)
    from_y(3)
    finish(2, 3)
    drains.append(ag1_drain)
    qkv = qkv_v[...].reshape(rows_all, 3 * HDIM)
    q, k, v = qkv[:, :HDIM], qkv[:, HDIM : 2 * HDIM], qkv[:, 2 * HDIM :]
    scores = by_rows(q, k) * HDIM ** (-0.5)
    scores = jnp.where(pair_col[...] == pair_row, scores, -1e30)
    weights = jnp.exp(scores - jnp.max(scores, axis=-1, keepdims=True))
    probability = (weights / jnp.sum(weights, axis=-1, keepdims=True)).astype(bf)
    context = jnp.dot(probability, v, preferred_element_type=f32).astype(bf)
    ctx_out[...] = jnp.dot(chosen(0, HALF, 1 - c), context, preferred_element_type=f32).astype(bf)
    ctx_swap = remote(ctx_out, ctx_in, xs.at[1], xr.at[1], cpart)
    ctx_swap.start()
    drains.append(ctx_swap.wait_send)
    ctx_mine = jnp.dot(chosen(0, HALF, c), context, preferred_element_type=f32).astype(bf)
    own_loads[0].wait()
    give[0].wait_recv()
    ctx_swap.wait_recv()
    ctx = jnp.concatenate([ctx_mine, ctx_in[...]], axis=1)

    def present(zi, yi):
        return (zi < Z - 1) | (yi == c)

    def compact(zi, yi):
        late = jnp.where((c == 1) & (zi == Z - 1) & (yi == 1), 1, 0)
        return jnp.minimum(zi * Y + yi - late, HALF // UNIT - 1)

    def when(cond, fn):
        if cond is None:
            fn()
        else:
            pl.when(cond)(fn)

    def both(a, b):
        return a if b is None else a & b

    class Scatter:
        def __init__(self, part, ry, s, rz, ss, rs, unit, has):
            self.part, self.ry, self.s, self.rz = part, ry, s, rz
            self.ss, self.rs, self.unit, self.has = ss, rs, unit, has

        def to_y(self, p, d):
            at = p * 12 + d
            return remote(
                self.part.at[p, self.unit(d, 1 - y)], self.ry.at[p, d],
                self.ss.at[at], self.rs.at[at], ypart,
            )

        def to_z(self, p, d, src):
            at = p * 12 + 4
            return remote(
                self.s.at[p, d], self.rz.at[p, src],
                self.ss.at[at + d], self.rs.at[at + src], flat(d, y, c),
            )

        def send_y(self, p, d):
            when(self.has(d, 1 - y), lambda: self.to_y(p, d).start())

        def mine_and_y(self, p, d):
            self.to_y(p, d).wait_recv()
            return self.part[p, self.unit(d, y)].astype(f32) + self.ry[p, d].astype(f32)

        def relay(self, p, d):
            def run():
                self.s[p, d] = self.mine_and_y(p, d).astype(bf)
                self.to_z(p, d, z).start()

            when(self.has(d, y), run)

        def own_sum(self, p):
            total = self.mine_and_y(p, z)
            for src in order[1:]:
                self.to_z(p, zmate, src).wait_recv()
                total = total + self.rz[p, src].astype(f32)
            return total

        def drain(self, pieces):
            for p in range(pieces):
                for d in range(Z):
                    when(self.has(d, 1 - y), lambda: self.to_y(p, d).wait_send())
                for d in order[1:]:
                    when(self.has(d, y), lambda: self.to_z(p, d, z).wait_send())

    turns = (zend, zmid, zmate, z)

    class Slabs(Scatter):
        def to_y(self, p, j):
            at, slabs = p * 12 + j, pl.ds(2 * j, 2 if j < Z - 1 else 1)
            return remote(
                self.part.at[p, slabs], self.ry.at[p, slabs], self.ss.at[at], self.rs.at[at], ypart
            )

        def mine_and_y(self, p, j):
            self.to_y(p, j).wait_recv()
            first, past = OWN * j // 8, -(-OWN * (j + 1) // 8)
            count = 8 * (past - first)
            i = lax.broadcasted_iota(i32, (UNIT, count), 0)
            k = lax.broadcasted_iota(i32, (UNIT, count), 1)
            pick = (i < OWN) & (k == i + OWN * j - 8 * first)
            rows = self.ry[p, first:past].reshape(count, self.ry.shape[-1])
            moved = jnp.dot(pick.astype(f32).astype(bf), rows, preferred_element_type=f32)
            return self.unit[p, j].astype(f32) + moved

        def relay(self, p, j):
            self.s[p, j] = self.mine_and_y(p, j).astype(bf)
            self.to_z(p, j, z).start()

        def to_z(self, p, j, src):
            at = p * 12 + 4
            return remote(
                self.s.at[p, j], self.rz.at[p, src],
                self.ss.at[at + j], self.rs.at[at + src], flat(turns[j], y, c),
            )

        def own_sum(self, p):
            total = self.mine_and_y(p, Z - 1)
            for src in order[1:]:
                self.to_z(p, 0, src).wait_recv()
                total = total + self.rz[p, src].astype(f32)
            return total

        def drain(self, pieces):
            for p in range(pieces):
                for j in range(Z):
                    self.to_y(p, j).wait_send()
                for j in range(Z - 1):
                    self.to_z(p, j, z).wait_send()

    one = Scatter(part1, ry1, s1, rz1, rs1_s, rs1_r, compact, present)
    width = features // P1
    wo_all = wo_v[...].reshape(2 * HDIM, features)
    for p in range(P1):
        cols = slice(p * width, (p + 1) * width)
        product = jnp.dot(ctx, wo_all[:, cols], preferred_element_type=f32)
        part1[p] = product.astype(bf).reshape(HALF // UNIT, UNIT, width)
        for d in (zend, zmid, zmate, z):
            one.send_y(p, d)

    drains.append(lambda: one.drain(P1))
    mine_at = compact(z, y)
    has_unit = present(z, y)
    rows_here = chosen(mine_at * UNIT, UNIT, c)
    for p in range(P1):
        for t in range(Z):
            for half_at in range(2):
                n = width // 2
                cols = slice(p * width + half_at * n, p * width + half_at * n + n)
                rows = arrived[t, :, :, cols].reshape(LAYER, n)
                took = jnp.dot(
                    rows_here[:, t * LAYER : (t + 1) * LAYER], rows, preferred_element_type=f32
                )
                spot = (p, slice(None), slice(half_at * n, half_at * n + n))
                resid[spot] = took if t == 0 else resid[spot] + took

    def ag2_y(p, zi, yi):
        v, at = mid.at[p, compact(zi, yi)], p * 12 + zi
        return remote(v, v, ag2_s.at[at], ag2_r.at[at], ypart)

    def ag2_z(p, zi, k, peer):
        v = mid.at[p, compact(zi, y)]
        return remote(v, v, ag2_s.at[p * 12 + 4 + k], ag2_r.at[p * 12 + 8 + zi], peer)

    def ag2_drain():
        for p in range(P1):

            @pl.when(has_unit)
            def _():
                ag2_z(p, z, 0, mate).wait_send()
                ag2_z(p, z, 1, middle).wait_send()

            for i in (2, 3):

                @pl.when(inner & present(order[i], y))
                def _():
                    ag2_z(p, order[i], i, mate).wait_send()

            for zi in range(Z):
                pl.when(present(zi, y))(lambda: ag2_y(p, zi, y).wait_send())

    def own_piece(p):
        @pl.when(has_unit)
        def _():
            mid[p, mine_at] = (resid[p] + one.own_sum(p)).astype(bf)
            ag2_z(p, z, 0, mate).start()
            ag2_z(p, z, 1, middle).start()
            ag2_y(p, z, y).start()

    def forward(p):
        for i in range(1, Z):
            zi = order[i]

            @pl.when(present(zi, y))
            def _():
                ag2_z(p, zi, 0, mate).wait_recv()
                if i > 1:
                    pl.when(inner)(lambda: ag2_z(p, zi, i, mate).start())
                ag2_y(p, zi, y).start()

    for step in range(P1 + LAG2):
        if 0 <= step - LAG1 < P1:
            own_piece(step - LAG1)
        if step < P1:
            for d in (zend, zmid, zmate):
                one.relay(step, d)
        if 0 <= step - LAG2 < P1:
            forward(step - LAG2)
    drains.append(ag2_drain)

    for k in (1, 2):
        own_loads[k].wait()
        give[k].wait_recv()
    hidden_units = wg_v.shape[1]
    squares = gate = up = None
    for p in range(P1):
        for zi in range(Z):
            when(present(zi, 1 - y), lambda: ag2_y(p, zi, 1 - y).wait_recv())
        cols = slice(p * width, (p + 1) * width)
        rows = mid[p].reshape(HALF, width).astype(f32)
        square = jnp.sum(rows * rows, axis=1, keepdims=True)
        scaled = (rows * gain2[:, cols]).astype(bf)
        g = by_rows(scaled, wg_v[:, :, cols].reshape(2 * hidden_units, width))
        u = by_rows(scaled, wu_v[:, :, cols].reshape(2 * hidden_units, width))
        squares, gate, up = (square, g, u) if p == 0 else (squares + square, gate + g, up + u)
    inverse = lax.rsqrt(squares * (1.0 / features) + 1e-06)
    hidden = (jax.nn.gelu(gate * inverse, approximate=True) * (up * inverse)).astype(bf)

    def spread(first, count):
        j = lax.broadcasted_iota(i32, (count, 1), 0) + first
        turn = j >> 4
        src = jnp.where((j & 15) < OWN, turn * OWN + (j & 15), -1)
        return (lax.broadcasted_iota(i32, (count, HALF), 1) == src).astype(f32).astype(bf)

    def turned(count, step, side):
        j = lax.broadcasted_iota(i32, (count, 1), 0)
        turn = step_count(j, step, Z)
        within = j - turn * step
        dest = jnp.where(
            turn == 0, zend, jnp.where(turn == 1, zmid, jnp.where(turn == 2, zmate, z))
        )
        src = jnp.where(within < OWN, (dest * Y + side) * OWN + within, -1)
        return (lax.broadcasted_iota(i32, (count, HALF), 1) == src).astype(f32).astype(bf)

    hidden = jnp.concatenate(
        [
            jnp.dot(turned(rows, step, side), hidden, preferred_element_type=f32).astype(bf)
            for rows, step, side in ((Z * UNIT, UNIT, y), (Z * OWN, OWN, 1 - y))
        ],
        axis=0,
    )
    own_loads[3].wait()
    give[3].wait_recv()

    two = Slabs(part2, ry2, s2, rz2, rs2_s, rs2_r, keep2, None)
    drains.append(lambda: two.drain(P2))
    width2 = features // P2
    wd_all = wd_v[...].reshape(2 * hidden_units, features)
    for p in range(P2):
        cols = slice(p * width2, (p + 1) * width2)
        product = jnp.dot(hidden, wd_all[:, cols], preferred_element_type=f32)
        product = product.astype(bf)
        keep2[p] = product[: Z * UNIT].reshape(Z, UNIT, width2)
        part2[p] = product[Z * UNIT :].reshape(Z * OWN // 8, 8, width2)
        two.to_y(p, 0).start()
    for j in range(1, Z):
        for p in range(P2):
            two.to_y(p, j).start()
    last_rows = spread((z * Y + y) * UNIT, UNIT)
    lasts = [
        jnp.dot(last_rows, mid[p].reshape(HALF, width), preferred_element_type=f32)
        for p in range(P1)
    ]
    last = jnp.concatenate(lasts, axis=1)
    for j in range(Z - 1):
        for p in range(P2):
            two.relay(p, j)
    for p in range(P2):
        cols = slice(p * width2, (p + 1) * width2)
        out_ref[:, cols] = (last[:, cols] + two.own_sum(p))[:OWN].astype(bf)

    for drain in drains:
        drain()


def fused_body(
    queries, corpus, block_owner, slot_row, segment, query_weight, key_weight, value_weight,
    out_weight, gain_attn, gain_ffn, gate_weight, up_weight, down_weight,
):
    features = queries.shape[1]
    hidden = gate_weight.shape[0]
    bf = jnp.bfloat16
    half = features // 2
    units = HALF // UNIT

    def scatter_bufs(pieces, count):
        width = features // pieces
        return [
            pltpu.VMEM((pieces, count, UNIT, width), bf),
            pltpu.VMEM((pieces, Z, UNIT, width), bf),
            pltpu.VMEM((pieces, Z, UNIT, width), bf),
            pltpu.VMEM((pieces, Z, UNIT, width), bf),
        ]

    dma = pltpu.SemaphoreType.DMA
    any_spec = pl.BlockSpec(memory_space=pl.ANY)
    vmem_spec = pl.BlockSpec(memory_space=pltpu.VMEM)
    return pl.pallas_call(
        fused_kernel,
        out_shape=jax.ShapeDtypeStruct((OWN, features), bf),
        in_specs=[any_spec] * 14,
        out_specs=vmem_spec,
        scratch_shapes=[
            pltpu.SMEM((1, block_owner.shape[0]), jnp.int32),
            pltpu.SMEM(slot_row.shape, jnp.int32),
            pltpu.SMEM(segment.shape, jnp.int32),
            pltpu.VMEM((1, features), jnp.float32),
            pltpu.VMEM((1, features), jnp.float32),
            pltpu.VMEM(corpus.shape, bf),
            pltpu.VMEM((Z, Y * SLABS, 8, features), bf),
            pltpu.VMEM((CAP, BLK, half), bf),
            pltpu.VMEM((CAP, BLK, half), bf),
            pltpu.VMEM((Z, LAYER, 3 * HDIM), bf),
            pltpu.VMEM((3 * HDIM, features), bf),
            pltpu.VMEM((2, HDIM, features), bf),
            pltpu.VMEM((2, hidden, features), bf),
            pltpu.VMEM((2, hidden, features), bf),
            pltpu.VMEM((2, hidden, features), bf),
            pltpu.VMEM((Z * LAYER, 1), jnp.float32),
            pltpu.VMEM((HALF, HDIM), bf),
            pltpu.VMEM((HALF, HDIM), bf),
            pltpu.VMEM((P1, UNIT, features // P1), jnp.float32),
            pltpu.VMEM((P1, units, UNIT, features // P1), bf),
        ]
        + scatter_bufs(P1, units)
        + [
            pltpu.VMEM((P2, Z, UNIT, features // P2), bf),
            pltpu.VMEM((P2, Z * OWN // 8, 8, features // P2), bf),
            pltpu.VMEM((P2, Z * OWN // 8, 8, features // P2), bf),
            pltpu.VMEM((P2, Z, UNIT, features // P2), bf),
            pltpu.VMEM((P2, Z, UNIT, features // P2), bf),
        ]
        + [dma((14,)), dma((6,)), dma((6,))]
        + [dma((40,))] * 2
        + [dma((12 * P1,))] * 4
        + [dma((12 * P2,))] * 2,
        compiler_params=pltpu.CompilerParams(
            collective_id=0, has_side_effects=True, vmem_limit_bytes=56 * 2**20
        ),
    )(
        queries, corpus, block_owner.reshape(1, -1), slot_row, segment, query_weight, key_weight,
        value_weight, out_weight, gate_weight, up_weight, down_weight, gain_attn[None, :], gain_ffn[None, :],
    )


def solution(mesh):
    placed = (
        P(("groups", "tensor"), None),
        P(("groups", "tensor"), None, None),
        P("groups", None),
        P("groups"),
        P("groups"),
        P("tensor", None),
        P("tensor", None),
        P("tensor", None),
        P("tensor", None),
        P(),
        P(),
        P("tensor", None),
        P("tensor", None),
        P("tensor", None),
    )
    body = fused_body if fits(mesh) else plain_body
    return jax.shard_map(
        body, mesh=mesh, in_specs=placed, out_specs=P(("groups", "tensor"), None), check_vma=False
    )
```

```python
import functools

import jax
import jax.numpy as jnp
from jax import lax
from jax.experimental import pallas as pl
from jax.experimental.pallas import tpu as pltpu
from jax.sharding import PartitionSpec as P

HDIM = 64
QLEN = 32
BLK = 4
CAP = 3


def normed(stream, gain):
    values = stream.astype(jnp.float32)
    mean_square = jnp.mean(values * values, axis=-1, keepdims=True)
    return (values * lax.rsqrt(mean_square + 1e-06) * gain).astype(jnp.bfloat16)


def by_rows(left, weight):
    return lax.dot_general(
        left, weight, (((1,), (1,)), ((), ())), preferred_element_type=jnp.float32
    )


def plain_body(
    queries,
    corpus,
    block_owner,
    slot_row,
    segment,
    query_weight,
    key_weight,
    value_weight,
    out_weight,
    gain_attn,
    gain_ffn,
    gate_weight,
    up_weight,
    down_weight,
):
    devices = lax.axis_size("tensor")
    my_index = lax.axis_index("tensor")
    owners = block_owner[:, 0]
    blocks_total = owners.shape[0]
    features = queries.shape[1]
    positions = jnp.arange(blocks_total, dtype=jnp.int32)
    earlier = (owners[:, None] == owners[None, :]) & (positions[:, None] < positions[None, :])
    slot_rank = jnp.sum(earlier.astype(jnp.int32), axis=0)
    slot_ids = jnp.arange(CAP, dtype=jnp.int32)
    choose_slot = (owners[None, :] == my_index) & (slot_rank[None, :] == slot_ids[:, None])
    local_rows = jnp.sum(jnp.where(choose_slot, slot_row[None, :], 0), axis=1)
    present = jnp.any(choose_slot, axis=1)
    outgoing = jnp.concatenate(
        [lax.dynamic_slice_in_dim(corpus, local_rows[k], 1, 0) for k in range(CAP)], axis=0
    )
    outgoing = jnp.where(present[:, None, None], outgoing, jnp.zeros_like(outgoing)).reshape(
        CAP, -1
    )
    location = owners * CAP + slot_rank
    query_all, arrived = (
        lax.all_gather(queries, "tensor", axis=0, tiled=True),
        lax.all_gather(outgoing, "tensor", axis=0, tiled=True),
    )
    slots = jnp.arange(arrived.shape[0], dtype=jnp.int32)
    chosen = (location[:, None] == slots[None, :]).astype(jnp.bfloat16)
    fetched = jnp.dot(chosen, arrived, preferred_element_type=jnp.float32).astype(jnp.bfloat16)
    stream_in = jnp.concatenate([query_all, fetched.reshape(-1, features)], axis=0)
    normal_rows = normed(stream_in, gain_attn)
    projected = tuple(
        (
            by_rows(normal_rows, weight).astype(jnp.bfloat16)
            for weight in (query_weight, key_weight, value_weight)
        )
    )
    tokens = stream_in.shape[0]
    heads_here = query_weight.shape[0] // HDIM
    query_rows_total = query_all.shape[0]
    pair_ids = jnp.concatenate(
        [jnp.arange(query_rows_total, dtype=jnp.int32) // QLEN, jnp.repeat(segment, BLK)]
    )
    same_pair = pair_ids[:, None] == pair_ids[None, :]
    query_heads = projected[0].reshape(tokens, heads_here, HDIM)
    key_heads = projected[1].reshape(tokens, heads_here, HDIM)
    value_heads = projected[2].reshape(tokens, heads_here, HDIM)
    scores = jnp.einsum(
        "qhd,khd->hqk", query_heads, key_heads, preferred_element_type=jnp.float32
    ) * HDIM ** (-0.5)
    scores = jnp.where(same_pair[None, :, :], scores, -1e30)
    row_max = jnp.max(scores, axis=-1, keepdims=True)
    weights = jnp.exp(scores - row_max)
    probability = (weights / jnp.sum(weights, axis=-1, keepdims=True)).astype(jnp.bfloat16)
    context = (
        jnp.einsum("hqk,khd->qhd", probability, value_heads, preferred_element_type=jnp.float32)
        .astype(jnp.bfloat16)
        .reshape(tokens, heads_here * HDIM)
    )
    rows_here = tokens // devices
    first_mine = my_index * rows_here
    attended = lax.psum(jnp.dot(context, out_weight, preferred_element_type=jnp.float32), "tensor")
    stream_mid = (stream_in.astype(jnp.float32) + attended).astype(jnp.bfloat16)
    normal_mid = normed(stream_mid, gain_ffn)
    mid_mine = lax.dynamic_slice_in_dim(stream_mid, first_mine, rows_here, 0)
    gate_value = by_rows(normal_mid, gate_weight)
    up_value = by_rows(normal_mid, up_weight)
    hidden = (jax.nn.gelu(gate_value, approximate=True) * up_value).astype(jnp.bfloat16)
    ffn_result = lax.psum_scatter(
        jnp.dot(hidden, down_weight, preferred_element_type=jnp.float32),
        "tensor",
        scatter_dimension=0,
        tiled=True,
    )
    return (mid_mine.astype(jnp.float32) + ffn_result).astype(jnp.bfloat16)


Z, Y, C = 4, 2, 2
UNIT = 16
OWN = 14
HALF = 112
P1 = 4
P2 = 4
LAG1 = 3
LAG2 = 5
SLABS = 5
LAYER = Y * SLABS * 8
MESH = pl.DeviceIdType.MESH


def fits(mesh):
    return mesh.shape["tensor"] == Z * Y * C


def step_count(values, step, most):
    total = jnp.zeros_like(values)
    for k in range(1, most):
        total = total + jnp.where(values >= k * step, 1, 0)
    return total


def fused_kernel(
    queries, corpus, owner_h, slot_h, segment_h, wq, wk, wv, wo, wg, wu, wd, gain1_h, gain2_h,
    out_ref,
    owner, slot, segment, gain1, gain2, corpus_v, arrived, xsend, xin, qkv_v, wqkv_v, wo_v, wg_v, wu_v, wd_v,
    pair_col, ctx_out, ctx_in, resid, mid,
    part1, ry1, s1, rz1,
    keep2, part2, ry2, s2, rz2,
    lsem, xs, xr, ag1_s, ag1_r, rs1_s, rs1_r, ag2_s, ag2_r, rs2_s, rs2_r,
):
    bf, f32, i32 = jnp.bfloat16, jnp.float32, jnp.int32
    me = lax.axis_index("tensor")
    z, y, c = me // (Y * C), (me // C) % Y, me % C
    features = gain1.shape[1]
    half = features // 2
    blocks = slot.shape[0]

    def flat(zi, yi, ci):
        return zi * (Y * C) + yi * C + ci

    ypart = flat(z, 1 - y, c)
    cpart = flat(z, y, 1 - c)
    end = (z == 0) | (z == Z - 1)
    inner = (z > 0) & (z < Z - 1)
    zmate = z + 1 - 2 * (z % 2)
    zmid = jnp.where(z < 2, 2, 1)
    zend = jnp.where(z < 2, 3, 0)
    far = (zmid, zend)
    mate = flat(zmate, y, c)
    middle = flat(zmid, y, c)

    def local(src, dst, i):
        return pltpu.make_async_copy(src, dst, lsem.at[i])

    def remote(src, dst, ssem, rsem, peer):
        return pltpu.make_async_remote_copy(
            src_ref=src, dst_ref=dst, send_sem=ssem, recv_sem=rsem,
            device_id={"tensor": peer}, device_id_type=MESH,
        )

    def ag1_view(m, zi, yi, ci):
        if m == 0:
            return arrived.at[zi, yi * SLABS + ci]
        cols = pl.ds(pl.multiple_of(ci * half, half), half)
        return arrived.at[zi, pl.ds(yi * SLABS + 2, 3), :, cols]

    barrier = pltpu.get_barrier_semaphore()
    peers = (ypart, cpart, flat((z + 1) % Z, y, c), flat((z + 2) % Z, y, c), flat((z + 3) % Z, y, c))
    for peer in peers:
        pl.semaphore_signal(barrier, inc=1, device_id={"tensor": peer}, device_id_type=MESH)

    tables = [
        local(src, dst, 9 + k)
        for k, (src, dst) in enumerate(((owner_h, owner), (slot_h, slot), (segment_h, segment)))
    ]
    gains = [local(gain1_h, gain1, 12), local(gain2_h, gain2, 13)]
    for copy in tables:
        copy.start()
    get_query = local(queries, arrived.at[z, y * SLABS + c], 0)
    get_corpus = local(corpus, corpus_v, 1)
    get_query.start()
    get_corpus.start()
    for copy in gains:
        copy.start()
    qkv_loads = [
        local(w, wqkv_v.at[pl.ds(k * HDIM, HDIM)], 2 + k) for k, w in enumerate((wq, wk, wv))
    ]
    shared = [(wo, wo_v), (wg, wg_v), (wu, wu_v), (wd, wd_v)]
    own_loads = [local(w, v.at[0], 5 + k) for k, (w, v) in enumerate(shared)]
    give = [
        remote(w, v.at[1], xs.at[2 + k], xr.at[2 + k], cpart) for k, (w, v) in enumerate(shared)
    ]

    drains = []

    for copy in tables:
        copy.wait()
    found = jnp.int32(0)
    spots = [jnp.int32(0)] * CAP
    for b in range(blocks):
        hit = owner[0, b] == me
        row = slot[b]
        for k in range(CAP):
            spots[k] = jnp.where(hit & (found == k), row, spots[k])
        found = found + jnp.where(hit, 1, 0)
    pl.semaphore_wait(barrier, len(peers))

    order = (z, zmate, zmid, zend)

    def ag1_y(m, zi, yi):
        v, at = ag1_view(m, zi, yi, c), m * 20 + zi
        return remote(v, v, ag1_s.at[at], ag1_r.at[at], ypart)

    def ag1_c(m, zi, yi):
        v, at = ag1_view(m, zi, yi, c), m * 20 + 4 + zi * 2 + yi
        return remote(v, v, ag1_s.at[at], ag1_r.at[at], cpart)

    def ag1_c_in(m, zi, yi):
        v, at = ag1_view(m, zi, yi, 1 - c), m * 20 + 4 + zi * 2 + yi
        return remote(v, v, ag1_s.at[at], ag1_r.at[at], cpart)

    def ag1_z(m, zi, k, peer):
        v = ag1_view(m, zi, y, c)
        return remote(v, v, ag1_s.at[m * 20 + 12 + k], ag1_r.at[m * 20 + 12 + zi], peer)

    def ag1_first(m):
        ag1_z(m, z, 0, mate).start()
        pl.when(inner)(lambda: ag1_z(m, z, 1, middle).start())
        ag1_y(m, z, y).start()
        ag1_c(m, z, y).start()

    def ag1_drain():
        for m in range(2):
            ag1_z(m, z, 0, mate).wait_send()
            pl.when(inner)(lambda: ag1_z(m, z, 1, middle).wait_send())
            for zi in range(Z):
                ag1_y(m, zi, y).wait_send()
                for yi in range(Y):
                    ag1_c(m, zi, yi).wait_send()
            for i in (1, 2, 3):
                pl.when(inner)(lambda: ag1_z(m, order[i], 1 + i, mate).wait_send())

    get_query.wait()
    ag1_first(0)
    get_corpus.wait()
    mine = [corpus_v[spots[k]] for k in range(CAP)]
    for side in range(2):

        @pl.when(c == side)
        def _():
            here = slice(side * half, side * half + half)
            there = slice((1 - side) * half, (1 - side) * half + half)
            for k in range(CAP):
                xsend[k] = mine[k][:, there]
            swap = remote(xsend, xin, xs.at[0], xr.at[0], cpart)
            swap.start()
            for yi in range(Y):

                @pl.when(y == yi)
                def _():
                    for k in range(CAP):
                        arrived[z, yi * SLABS + 2 + k, side * BLK : side * BLK + BLK, here] = mine[k][:, here]

            swap.wait_recv()
            other = (1 - side) * BLK
            for yi in range(Y):

                @pl.when(y == yi)
                def _():
                    for k in range(CAP):
                        arrived[z, yi * SLABS + 2 + k, other : other + BLK, here] = xin[k]

    ag1_first(1)
    drains.append(lambda: remote(xsend, xin, xs.at[0], xr.at[0], cpart).wait_send())
    for load in qkv_loads + own_loads:
        load.start()
    for copy in give:
        copy.start()

    drains.append(lambda: [copy.wait_send() for copy in give])
    lane = lax.broadcasted_iota(i32, (8, 128), 1)
    owner_row = jnp.zeros((8, 128), i32)
    seg_row = jnp.zeros((8, 128), i32)
    for b in range(blocks):
        owner_row = jnp.where(lane == b, owner[0, b], owner_row)
        seg_row = jnp.where(lane == b, segment[b], seg_row)
    rank_row = jnp.zeros((8, 128), i32)
    for b in range(blocks):
        rank_row = rank_row + jnp.where((owner_row == owner[0, b]) & (lane > b), 1, 0)
    start_row = (
        (owner_row >> 2) * LAYER + ((owner_row >> 1) & 1) * (SLABS * 8) + 16
        + rank_row * 8 + (owner_row & 1) * BLK
    )
    start_row = jnp.where(lane < blocks, start_row, -1000).astype(f32)[:1]
    seg_row = seg_row.astype(f32)[:1]
    sub = lax.broadcasted_iota(i32, (128, 128), 0)
    lanes = lax.broadcasted_iota(i32, (128, 128), 1)
    start_col = jnp.sum(jnp.where(sub == lanes, start_row, 0.0), axis=1, keepdims=True)
    seg_col = jnp.sum(jnp.where(sub == lanes, seg_row, 0.0), axis=1, keepdims=True)

    def slot_parts(j):
        zj = step_count(j, LAYER, Z)
        rem = j - zj * LAYER
        within = rem - jnp.where(rem >= SLABS * 8, SLABS * 8, 0)
        return zj.astype(f32), within < 16, ((j >> 2) << 2).astype(f32)

    rows_all = Z * LAYER
    zj, is_query, begin = slot_parts(lax.broadcasted_iota(i32, (rows_all, 1), 0))
    held = jnp.max(jnp.where(begin == start_row, seg_row, -1.0), axis=1, keepdims=True)
    pair_col[...] = jnp.where(is_query, zj, held)
    zj, is_query, begin = slot_parts(lax.broadcasted_iota(i32, (1, rows_all), 1))
    held = jnp.max(jnp.where(begin == start_col, seg_col, -1.0), axis=0, keepdims=True)
    pair_row = jnp.where(is_query, zj, held)

    def chosen(first, count, side):
        i = lax.broadcasted_iota(i32, (count, 1), 0) + first
        turn = step_count(i, OWN, 8)
        row = OWN * (2 * turn + side) + i - OWN * turn
        from_query = (
            (row >> 5) * LAYER + ((row >> 4) & 1) * (SLABS * 8) + ((row >> 3) & 1) * 8 + (row & 7)
        )
        behind = row - Z * QLEN
        block = lax.broadcasted_iota(i32, (count, 128), 1) == (behind >> 2)
        start = jnp.sum(jnp.where(block, start_row, 0.0), axis=1, keepdims=True)
        src = jnp.where(behind < 0, from_query, start.astype(i32) + (behind & 3))
        at = lax.broadcasted_iota(i32, (count, rows_all), 1)
        return (at == src).astype(f32).astype(bf)

    for load in qkv_loads + gains:
        load.wait()

    def fold(i, carry):
        at = pl.ds(pl.multiple_of(i * 16, 16), 16)
        wqkv_v[at, :] = (wqkv_v[at, :].astype(f32) * gain1[...]).astype(bf)
        return carry

    lax.fori_loop(0, 3 * HDIM // 16, fold, 0)

    def project(layers):
        rows = jnp.concatenate([arrived[zi].reshape(LAYER, features) for zi in layers], axis=0)
        wide = rows.astype(f32)
        inverse = lax.rsqrt(jnp.mean(wide * wide, axis=1, keepdims=True) + 1e-06)
        found = (by_rows(rows, wqkv_v[...]) * inverse).astype(bf)
        for k, zi in enumerate(layers):
            qkv_v[zi] = found[k * LAYER : (k + 1) * LAYER]

    def from_z(i):
        zi = order[i]
        for m in range(2):
            ag1_z(m, zi, 0, mate).wait_recv()
            onward = middle if i == 1 else mate
            pl.when(inner)(lambda: ag1_z(m, zi, 1 + i, onward).start())
            ag1_y(m, zi, y).start()
            ag1_c(m, zi, y).start()

    def from_y(i):
        zi = order[i]
        for m in range(2):
            ag1_y(m, zi, 1 - y).wait_recv()
            ag1_c(m, zi, 1 - y).start()

    def finish(*layers):
        for i in layers:
            for m in range(2):
                for yi in range(Y):
                    ag1_c_in(m, order[i], yi).wait_recv()
        project([order[i] for i in layers])

    from_z(1)
    from_y(0)
    from_z(2)
    from_z(3)
    from_y(1)
    finish(0, 1)
    from_y(2)
    from_y(3)
    finish(2, 3)
    drains.append(ag1_drain)
    qkv = qkv_v[...].reshape(rows_all, 3 * HDIM)
    q, k, v = qkv[:, :HDIM], qkv[:, HDIM : 2 * HDIM], qkv[:, 2 * HDIM :]
    scores = by_rows(q, k) * HDIM ** (-0.5)
    scores = jnp.where(pair_col[...] == pair_row, scores, -1e30)
    weights = jnp.exp(scores - jnp.max(scores, axis=-1, keepdims=True))
    probability = (weights / jnp.sum(weights, axis=-1, keepdims=True)).astype(bf)
    context = jnp.dot(probability, v, preferred_element_type=f32).astype(bf)
    ctx_out[...] = jnp.dot(chosen(0, HALF, 1 - c), context, preferred_element_type=f32).astype(bf)
    ctx_swap = remote(ctx_out, ctx_in, xs.at[1], xr.at[1], cpart)
    ctx_swap.start()
    drains.append(ctx_swap.wait_send)
    ctx_mine = jnp.dot(chosen(0, HALF, c), context, preferred_element_type=f32).astype(bf)
    own_loads[0].wait()
    give[0].wait_recv()
    ctx_swap.wait_recv()
    ctx = jnp.concatenate([ctx_mine, ctx_in[...]], axis=1)

    def present(zi, yi):
        return (zi < Z - 1) | (yi == c)

    def compact(zi, yi):
        late = jnp.where((c == 1) & (zi == Z - 1) & (yi == 1), 1, 0)
        return jnp.minimum(zi * Y + yi - late, HALF // UNIT - 1)

    def when(cond, fn):
        if cond is None:
            fn()
        else:
            pl.when(cond)(fn)

    def both(a, b):
        return a if b is None else a & b

    class Scatter:
        def __init__(self, part, ry, s, rz, ss, rs, unit, has):
            self.part, self.ry, self.s, self.rz = part, ry, s, rz
            self.ss, self.rs, self.unit, self.has = ss, rs, unit, has

        def to_y(self, p, d):
            at = p * 12 + d
            return remote(
                self.part.at[p, self.unit(d, 1 - y)], self.ry.at[p, d],
                self.ss.at[at], self.rs.at[at], ypart,
            )

        def to_z(self, p, d, src):
            at = p * 12 + 4
            return remote(
                self.s.at[p, d], self.rz.at[p, src],
                self.ss.at[at + d], self.rs.at[at + src], flat(d, y, c),
            )

        def send_y(self, p, d):
            when(self.has(d, 1 - y), lambda: self.to_y(p, d).start())

        def mine_and_y(self, p, d):
            self.to_y(p, d).wait_recv()
            return self.part[p, self.unit(d, y)].astype(f32) + self.ry[p, d].astype(f32)

        def relay(self, p, d):
            def run():
                self.s[p, d] = self.mine_and_y(p, d).astype(bf)
                self.to_z(p, d, z).start()

            when(self.has(d, y), run)

        def own_sum(self, p):
            total = self.mine_and_y(p, z)
            for src in order[1:]:
                self.to_z(p, zmate, src).wait_recv()
                total = total + self.rz[p, src].astype(f32)
            return total

        def drain(self, pieces):
            for p in range(pieces):
                for d in range(Z):
                    when(self.has(d, 1 - y), lambda: self.to_y(p, d).wait_send())
                for d in order[1:]:
                    when(self.has(d, y), lambda: self.to_z(p, d, z).wait_send())

    turns = (zend, zmid, zmate, z)

    class Slabs(Scatter):
        def to_y(self, p, j):
            at, slabs = p * 12 + j, pl.ds(2 * j, 2 if j < Z - 1 else 1)
            return remote(
                self.part.at[p, slabs], self.ry.at[p, slabs], self.ss.at[at], self.rs.at[at], ypart
            )

        def mine_and_y(self, p, j):
            self.to_y(p, j).wait_recv()
            first, past = OWN * j // 8, -(-OWN * (j + 1) // 8)
            count = 8 * (past - first)
            i = lax.broadcasted_iota(i32, (UNIT, count), 0)
            k = lax.broadcasted_iota(i32, (UNIT, count), 1)
            pick = (i < OWN) & (k == i + OWN * j - 8 * first)
            rows = self.ry[p, first:past].reshape(count, self.ry.shape[-1])
            moved = jnp.dot(pick.astype(f32).astype(bf), rows, preferred_element_type=f32)
            return self.unit[p, j].astype(f32) + moved

        def relay(self, p, j):
            self.s[p, j] = self.mine_and_y(p, j).astype(bf)
            self.to_z(p, j, z).start()

        def to_z(self, p, j, src):
            at = p * 12 + 4
            return remote(
                self.s.at[p, j], self.rz.at[p, src],
                self.ss.at[at + j], self.rs.at[at + src], flat(turns[j], y, c),
            )

        def own_sum(self, p):
            total = self.mine_and_y(p, Z - 1)
            for src in order[1:]:
                self.to_z(p, 0, src).wait_recv()
                total = total + self.rz[p, src].astype(f32)
            return total

        def drain(self, pieces):
            for p in range(pieces):
                for j in range(Z):
                    self.to_y(p, j).wait_send()
                for j in range(Z - 1):
                    self.to_z(p, j, z).wait_send()

    one = Scatter(part1, ry1, s1, rz1, rs1_s, rs1_r, compact, present)
    width = features // P1
    wo_all = wo_v[...].reshape(2 * HDIM, features)
    for p in range(P1):
        cols = slice(p * width, (p + 1) * width)
        product = jnp.dot(ctx, wo_all[:, cols], preferred_element_type=f32)
        part1[p] = product.astype(bf).reshape(HALF // UNIT, UNIT, width)
        for d in (zend, zmid, zmate, z):
            one.send_y(p, d)

    drains.append(lambda: one.drain(P1))
    mine_at = compact(z, y)
    has_unit = present(z, y)
    rows_here = chosen(mine_at * UNIT, UNIT, c)
    for p in range(P1):
        for t in range(Z):
            for half_at in range(2):
                n = width // 2
                cols = slice(p * width + half_at * n, p * width + half_at * n + n)
                rows = arrived[t, :, :, cols].reshape(LAYER, n)
                took = jnp.dot(
                    rows_here[:, t * LAYER : (t + 1) * LAYER], rows, preferred_element_type=f32
                )
                spot = (p, slice(None), slice(half_at * n, half_at * n + n))
                resid[spot] = took if t == 0 else resid[spot] + took

    def ag2_y(p, zi, yi):
        v, at = mid.at[p, compact(zi, yi)], p * 12 + zi
        return remote(v, v, ag2_s.at[at], ag2_r.at[at], ypart)

    def ag2_z(p, zi, k, peer):
        v = mid.at[p, compact(zi, y)]
        return remote(v, v, ag2_s.at[p * 12 + 4 + k], ag2_r.at[p * 12 + 8 + zi], peer)

    def ag2_drain():
        for p in range(P1):

            @pl.when(has_unit)
            def _():
                ag2_z(p, z, 0, mate).wait_send()
                ag2_z(p, z, 1, middle).wait_send()

            for i in (2, 3):

                @pl.when(inner & present(order[i], y))
                def _():
                    ag2_z(p, order[i], i, mate).wait_send()

            for zi in range(Z):
                pl.when(present(zi, y))(lambda: ag2_y(p, zi, y).wait_send())

    def own_piece(p):
        @pl.when(has_unit)
        def _():
            mid[p, mine_at] = (resid[p] + one.own_sum(p)).astype(bf)
            ag2_y(p, z, y).start()
            ag2_z(p, z, 1, middle).start()
            ag2_z(p, z, 0, mate).start()

    def forward(p):
        for i in range(1, Z):
            zi = order[i]

            @pl.when(present(zi, y))
            def _():
                ag2_z(p, zi, 0, mate).wait_recv()
                if i > 1:
                    pl.when(inner)(lambda: ag2_z(p, zi, i, mate).start())
                ag2_y(p, zi, y).start()

    for step in range(P1 + LAG2):
        if 0 <= step - LAG1 < P1:
            own_piece(step - LAG1)
        if step < P1:
            for d in (zend, zmid, zmate):
                one.relay(step, d)
        if 0 <= step - LAG2 < P1:
            forward(step - LAG2)
    drains.append(ag2_drain)

    for k in (1, 2):
        own_loads[k].wait()
        give[k].wait_recv()
    hidden_units = wg_v.shape[1]
    squares = gate = up = None
    for p in range(P1):
        for zi in range(Z):
            when(present(zi, 1 - y), lambda: ag2_y(p, zi, 1 - y).wait_recv())
        cols = slice(p * width, (p + 1) * width)
        rows = mid[p].reshape(HALF, width).astype(f32)
        square = jnp.sum(rows * rows, axis=1, keepdims=True)
        scaled = (rows * gain2[:, cols]).astype(bf)
        g = by_rows(scaled, wg_v[:, :, cols].reshape(2 * hidden_units, width))
        u = by_rows(scaled, wu_v[:, :, cols].reshape(2 * hidden_units, width))
        squares, gate, up = (square, g, u) if p == 0 else (squares + square, gate + g, up + u)
    inverse = lax.rsqrt(squares * (1.0 / features) + 1e-06)
    hidden = (jax.nn.gelu(gate * inverse, approximate=True) * (up * inverse)).astype(bf)

    def spread(first, count):
        j = lax.broadcasted_iota(i32, (count, 1), 0) + first
        turn = j >> 4
        src = jnp.where((j & 15) < OWN, turn * OWN + (j & 15), -1)
        return (lax.broadcasted_iota(i32, (count, HALF), 1) == src).astype(f32).astype(bf)

    def turned(count, step, side):
        j = lax.broadcasted_iota(i32, (count, 1), 0)
        turn = step_count(j, step, Z)
        within = j - turn * step
        dest = jnp.where(
            turn == 0, zend, jnp.where(turn == 1, zmid, jnp.where(turn == 2, zmate, z))
        )
        src = jnp.where(within < OWN, (dest * Y + side) * OWN + within, -1)
        return (lax.broadcasted_iota(i32, (count, HALF), 1) == src).astype(f32).astype(bf)

    hidden = jnp.concatenate(
        [
            jnp.dot(turned(rows, step, side), hidden, preferred_element_type=f32).astype(bf)
            for rows, step, side in ((Z * UNIT, UNIT, y), (Z * OWN, OWN, 1 - y))
        ],
        axis=0,
    )
    own_loads[3].wait()
    give[3].wait_recv()

    two = Slabs(part2, ry2, s2, rz2, rs2_s, rs2_r, keep2, None)
    drains.append(lambda: two.drain(P2))
    width2 = features // P2
    wd_all = wd_v[...].reshape(2 * hidden_units, features)
    for p in range(P2):
        cols = slice(p * width2, (p + 1) * width2)
        product = jnp.dot(hidden, wd_all[:, cols], preferred_element_type=f32)
        product = product.astype(bf)
        keep2[p] = product[: Z * UNIT].reshape(Z, UNIT, width2)
        part2[p] = product[Z * UNIT :].reshape(Z * OWN // 8, 8, width2)
        two.to_y(p, 0).start()
    for j in range(1, Z):
        for p in range(P2):
            two.to_y(p, j).start()
    last_rows = spread((z * Y + y) * UNIT, UNIT)
    lasts = [
        jnp.dot(last_rows, mid[p].reshape(HALF, width), preferred_element_type=f32)
        for p in range(P1)
    ]
    last = jnp.concatenate(lasts, axis=1)
    for j in range(Z - 1):
        for p in range(P2):
            two.relay(p, j)
    for p in range(P2):
        cols = slice(p * width2, (p + 1) * width2)
        out_ref[:, cols] = (last[:, cols] + two.own_sum(p))[:OWN].astype(bf)

    for drain in drains:
        drain()


def fused_body(
    queries, corpus, block_owner, slot_row, segment, query_weight, key_weight, value_weight,
    out_weight, gain_attn, gain_ffn, gate_weight, up_weight, down_weight,
):
    features = queries.shape[1]
    hidden = gate_weight.shape[0]
    bf = jnp.bfloat16
    half = features // 2
    units = HALF // UNIT

    def scatter_bufs(pieces, count):
        width = features // pieces
        return [
            pltpu.VMEM((pieces, count, UNIT, width), bf),
            pltpu.VMEM((pieces, Z, UNIT, width), bf),
            pltpu.VMEM((pieces, Z, UNIT, width), bf),
            pltpu.VMEM((pieces, Z, UNIT, width), bf),
        ]

    dma = pltpu.SemaphoreType.DMA
    any_spec = pl.BlockSpec(memory_space=pl.ANY)
    vmem_spec = pl.BlockSpec(memory_space=pltpu.VMEM)
    return pl.pallas_call(
        fused_kernel,
        out_shape=jax.ShapeDtypeStruct((OWN, features), bf),
        in_specs=[any_spec] * 14,
        out_specs=vmem_spec,
        scratch_shapes=[
            pltpu.SMEM((1, block_owner.shape[0]), jnp.int32),
            pltpu.SMEM(slot_row.shape, jnp.int32),
            pltpu.SMEM(segment.shape, jnp.int32),
            pltpu.VMEM((1, features), jnp.float32),
            pltpu.VMEM((1, features), jnp.float32),
            pltpu.VMEM(corpus.shape, bf),
            pltpu.VMEM((Z, Y * SLABS, 8, features), bf),
            pltpu.VMEM((CAP, BLK, half), bf),
            pltpu.VMEM((CAP, BLK, half), bf),
            pltpu.VMEM((Z, LAYER, 3 * HDIM), bf),
            pltpu.VMEM((3 * HDIM, features), bf),
            pltpu.VMEM((2, HDIM, features), bf),
            pltpu.VMEM((2, hidden, features), bf),
            pltpu.VMEM((2, hidden, features), bf),
            pltpu.VMEM((2, hidden, features), bf),
            pltpu.VMEM((Z * LAYER, 1), jnp.float32),
            pltpu.VMEM((HALF, HDIM), bf),
            pltpu.VMEM((HALF, HDIM), bf),
            pltpu.VMEM((P1, UNIT, features // P1), jnp.float32),
            pltpu.VMEM((P1, units, UNIT, features // P1), bf),
        ]
        + scatter_bufs(P1, units)
        + [
            pltpu.VMEM((P2, Z, UNIT, features // P2), bf),
            pltpu.VMEM((P2, Z * OWN // 8, 8, features // P2), bf),
            pltpu.VMEM((P2, Z * OWN // 8, 8, features // P2), bf),
            pltpu.VMEM((P2, Z, UNIT, features // P2), bf),
            pltpu.VMEM((P2, Z, UNIT, features // P2), bf),
        ]
        + [dma((14,)), dma((6,)), dma((6,))]
        + [dma((40,))] * 2
        + [dma((12 * P1,))] * 4
        + [dma((12 * P2,))] * 2,
        compiler_params=pltpu.CompilerParams(
            collective_id=0, has_side_effects=True, vmem_limit_bytes=56 * 2**20
        ),
    )(
        queries, corpus, block_owner.reshape(1, -1), slot_row, segment, query_weight, key_weight,
        value_weight, out_weight, gate_weight, up_weight, down_weight, gain_attn[None, :], gain_ffn[None, :],
    )


def solution(mesh):
    placed = (
        P(("groups", "tensor"), None),
        P(("groups", "tensor"), None, None),
        P("groups", None),
        P("groups"),
        P("groups"),
        P("tensor", None),
        P("tensor", None),
        P("tensor", None),
        P("tensor", None),
        P(),
        P(),
        P("tensor", None),
        P("tensor", None),
        P("tensor", None),
    )
    body = fused_body if fits(mesh) else plain_body
    return jax.shard_map(
        body, mesh=mesh, in_specs=placed, out_specs=P(("groups", "tensor"), None), check_vma=False
    )
```
